32 devices in a mesh: mem: 4 (over x, core), tile: 8 (over z, y).
Axes of the slice: x: 2, y: 2, z: 4, core: 2. Of those that a mesh axis runs over, the one named last changes fastest.
Arguments:
- gradient: float32 [4, 256, 1024], P(None, 'tile', 'mem'), may hold values from -6 to 6
- static_scale: float32 [4, 256, 1024], P(None, 'tile', 'mem'), may hold values from 0.5 to 2
- static_rate: float32 [4], replicated, may hold values from 0.05 to 0.24
- interp_index: int32 [4, 128, 512], P(None, 'tile', 'mem'), may hold values from 0 to 15
- interp_weight: float32 [4, 128, 512], P(None, 'tile', 'mem'), may hold values from 0.1 to 0.4
- members: bfloat16 [80, 4, 128, 512], P('mem', None, 'tile'), may hold values from -6 to 6
- spread_rate: float32 [128, 512], P('tile'), may hold values from 0.02 to 0.24
Outputs:
- hybrid: float32 [4, 256, 1024], P(None, 'tile', 'mem')
The draws below stay inside these ranges and needn't reach their ends.
Inputs may be any that keep to these rules, and one draw needn't show every extreme that they name: `interp_index`: the fine cell (a, b) of a coarse cell's 4 x 4 block, numbered 4 * a + b; slots may name the same cell.
All inputs are finite; a program needn't handle non-finite values.
Results may differ from the reference program's by a relative error of at most 0.0003.
Values sent between devices are 32-bit elements; how exact they have to be, the bound alone decides.
No kernel may reach another device: no remote copies, remote signals or barrier semaphores. Data moves between devices by JAX's collectives and lax.ppermute only.
A program may use at most 128 MiB of HBM per device.

```python
import math
import jax
import jax.numpy as jnp
from jax import lax

BLOCK_SLOTS = 4
STATIC_PASSES = 4
SPREAD_PASSES = 8
FIELDS = 4
GRID_ROWS = 256
GRID_COLS = 1024
COARSE_ROWS = 128
COARSE_COLS = 512
MEMBERS = 80


def with_ends(result, stream_key, least, top_value):
    longest = result.shape.index(max(result.shape))
    spots = []
    for shift in (0, 1):
        where = [jax.random.randint(jax.random.fold_in(stream_key, axis), (), 0, length) for axis, length in enumerate(result.shape)]
        where[longest] = (where[longest] + shift) % result.shape[longest]
        spots.append(tuple(where))
    return result.at[spots[0]].set(least).at[spots[1]].set(top_value)


def steps_of(rng, extent, cuts, low, top_value):
    def one(dim, parts):
        heights = jax.random.uniform(jax.random.fold_in(jax.random.fold_in(rng, 6), dim), (parts,), jnp.float32, low / len(cuts), top_value / len(cuts))
        return jnp.repeat(jnp.exp(heights), extent[dim] // parts).reshape((-1,) + (1,) * (len(extent) - dim - 1))

    factor_of = one(*cuts[0])
    for cut in cuts[1:]:
        factor_of = factor_of * one(*cut)
    return factor_of


def normal_values(rng, dims, scale, most, shards=(), held_as=jnp.bfloat16):
    result = scale * jax.random.normal(rng, dims, jnp.float32)
    if shards:
        result = result * steps_of(rng, dims, shards, -0.22, 0.18)
    return jnp.clip(result, -most, most).astype(held_as)


def setup_inputs(seed: int = 0) -> dict:
    key_list = jax.random.split(jax.random.key(seed), 8)
    gradient = normal_values(key_list[0], (FIELDS, GRID_ROWS, GRID_COLS), 1.0, 6.0, ((1, 8), (2, 4)), jnp.float32)
    static_scale = jnp.clip(jnp.exp(math.log(2.0) - 1.3862944 * jax.random.uniform(key_list[1], (FIELDS, GRID_ROWS, GRID_COLS), jnp.float32) ** steps_of(key_list[1], (FIELDS, GRID_ROWS, GRID_COLS), ((1, 8), (2, 4)), -0.2, 0.2)), 0.5, 2.0)
    static_rate = jnp.clip(jnp.exp(jax.random.uniform(key_list[2], (FIELDS,), jnp.float32, math.log(0.05), math.log(0.24))), 0.05, 0.24)
    interp_index = with_ends(jax.random.randint(key_list[3], (BLOCK_SLOTS, COARSE_ROWS, COARSE_COLS), 0, 16), jax.random.fold_in(key_list[3], 1), 0, 15).astype(jnp.int32)
    interp_weight = jnp.clip(0.1 + 0.3 * jax.random.uniform(key_list[4], (BLOCK_SLOTS, COARSE_ROWS, COARSE_COLS), jnp.float32) ** steps_of(key_list[4], (BLOCK_SLOTS, COARSE_ROWS, COARSE_COLS), ((1, 8), (2, 4)), -0.2, 0.2), 0.1, 0.4)
    members = normal_values(key_list[5], (MEMBERS, FIELDS, COARSE_ROWS, COARSE_COLS), 1.0, 6.0, ((0, 4), (2, 8)))
    spread_rate = jnp.clip(jnp.exp(math.log(0.24) - 2.4849066 * jax.random.uniform(key_list[6], (COARSE_ROWS, COARSE_COLS), jnp.float32) ** steps_of(key_list[6], (COARSE_ROWS, COARSE_COLS), ((0, 8),), -0.2, 0.2)), 0.02, 0.24)
    return {"gradient": gradient, "static_scale": static_scale, "static_rate": static_rate, "interp_index": interp_index, "interp_weight": interp_weight, "members": members, "spread_rate": spread_rate}


def pad_edges(values, margin):
    return jnp.pad(values, [(0, 0)] * (values.ndim - 2) + [(margin, margin), (margin, margin)])


def diffuse(padded, rate_field):
    centre = padded[..., 1:-1, 1:-1]
    beside = padded[..., 2:, 1:-1] + padded[..., :-2, 1:-1] + padded[..., 1:-1, 2:] + padded[..., 1:-1, :-2]
    return centre + rate_field * (beside - 4.0 * centre)


def weights_table(slot_index, slot_weight):
    offsets = jnp.arange(16, dtype=jnp.int32)[:, None, None]
    offset_table = jnp.zeros((16,) + slot_index.shape[1:], jnp.float32)
    for slot_number in range(slot_index.shape[0]):
        offset_table = offset_table + jnp.where(slot_index[slot_number][None] == offsets, slot_weight[slot_number][None], 0.0)
    return offset_table


def restrict(padded, offset_table):
    height = (padded.shape[1] - 4) // 2
    breadth = (padded.shape[2] - 4) // 2
    accumulated = jnp.zeros((padded.shape[0], height, breadth), jnp.float32)
    for row_shift in range(4):
        for col_shift in range(4):
            picked = padded[:, row_shift + 1:row_shift + 1 + 2 * height:2, col_shift + 1:col_shift + 1 + 2 * breadth:2]
            accumulated = accumulated + offset_table[4 * row_shift + col_shift] * picked
    return accumulated


def prolong(offset_table, ensemble):
    height = ensemble.shape[1]
    breadth = ensemble.shape[2]
    placed = jnp.zeros((ensemble.shape[0], 2 * height + 4, 2 * breadth + 4), jnp.float32)
    for row_shift in range(4):
        for col_shift in range(4):
            contrib = offset_table[4 * row_shift + col_shift][None] * ensemble
            placed = placed.at[:, row_shift:row_shift + 2 * height:2, col_shift:col_shift + 2 * breadth:2].add(contrib)
    return placed


def reference(gradient, static_scale, static_rate, interp_index, interp_weight, members, spread_rate):
    smooth = static_scale * gradient
    for repeat in range(STATIC_PASSES):
        smooth = diffuse(pad_edges(smooth, 1), static_rate[:, None, None])
    static = static_scale * smooth
    offset_table = weights_table(interp_index, interp_weight)
    coarse = restrict(pad_edges(gradient, 2), offset_table)

    def spread_member(running, member_field):
        perturbed = member_field.astype(jnp.float32)
        values = perturbed * coarse
        for repeat in range(SPREAD_PASSES):
            values = diffuse(pad_edges(values, 1), spread_rate)
        return running + perturbed * values, None

    summed, unused = lax.scan(spread_member, jnp.zeros_like(coarse), members)
    ensemble = summed / (MEMBERS - 1)
    spread = prolong(offset_table, ensemble)
    fine_grid = spread[:, 1:1 + GRID_ROWS, 1:1 + GRID_COLS]
    return 0.3 * static + 2.8 * fine_grid
```

```python
import functools

import jax
import jax.numpy as jnp
from jax import lax
from jax.experimental import pallas as pl
from jax.experimental.pallas import tpu as pltpu
from jax.sharding import PartitionSpec as P

STATIC_PASSES = 4
SPREAD_PASSES = 8
LANES = 128
SUB = 8


F32 = jnp.float32
EXACT = lax.Precision.HIGHEST


def call(kernel, out_shapes, scratch=(), **kw):
    return pl.pallas_call(
        kernel,
        out_shape=tuple(jax.ShapeDtypeStruct(s, F32) for s in out_shapes),
        scratch_shapes=[pltpu.VMEM(s, F32) for s in scratch],
        **kw,
    )


def pack_tile(grad, scale, index, weight, rate, up, down):
    fields, rows, cols = grad.shape
    slots, height, breadth = index.shape
    parts = rate.shape[1] // cols
    reach = SPREAD_PASSES
    up[...] = jnp.zeros(up.shape, F32)
    down[...] = jnp.zeros(down.shape, F32)
    for f in range(fields):
        top = 2 * reach + 1
        up[f * 24 : f * 24 + top, :] = grad[f, 0:top, :]
        up[f * 24 + top : f * 24 + top + STATIC_PASSES, :] = (
            scale[f, 0:STATIC_PASSES, :] * grad[f, 0:STATIC_PASSES, :]
        )
        down[f * 8 : f * 8 + 1, :] = grad[f, rows - 1 : rows, :]
        down[f * 8 + 1 : f * 8 + 1 + STATIC_PASSES, :] = (
            scale[f, rows - STATIC_PASSES : rows, :] * grad[f, rows - STATIC_PASSES : rows, :]
        )
    base = fields * 24
    low = fields * 8
    for s in range(slots):
        up[base + s * 8 : base + s * 8 + 8, 0:breadth] = index[s, 0:8, :].astype(F32)
        up[base + s * 8 : base + s * 8 + 8, breadth:] = weight[s, 0:8, :]
        down[low + s : low + s + 1, 0:breadth] = index[s, height - 1 : height, :].astype(F32)
        down[low + s : low + s + 1, breadth:] = weight[s, height - 1 : height, :]
    base += slots * 8
    low += slots
    for p in range(parts):
        part = slice(p * cols, (p + 1) * cols)
        up[base + p * 8 : base + p * 8 + 8, :] = rate[0:8, part]
        down[low + p * 4 : low + p * 4 + 4, :] = rate[height - 4 : height, part]


def pack_mem(grad, scale, index, weight, rate, up, down, west, east, rate_out):
    fields, rows, cols = grad.shape
    slots, height, breadth = index.shape
    parts = rate.shape[1] // cols
    n = STATIC_PASSES
    top = 2 * SPREAD_PASSES + 1
    for out, at in ((west, 0), (east, 1)):
        out[...] = jnp.zeros(out.shape, F32)
        wide = slice(0, n) if at == 0 else slice(cols - n, cols)
        one = slice(0, 1) if at == 0 else slice(cols - 1, cols)
        lone = slice(0, 1) if at == 0 else slice(breadth - 1, breadth)
        wone = slice(breadth, breadth + 1) if at == 0 else slice(2 * breadth - 1, 2 * breadth)
        for f in range(fields):
            lane = slice(4 * f, 4 * f + n)
            out[8 : 8 + rows, lane] = scale[f, :, wide] * grad[f, :, wide]
            out[8 - n : 8, lane] = down[f * 8 + 1 : f * 8 + 1 + n, wide]
            out[8 + rows : 8 + rows + n, lane] = up[f * 24 + top : f * 24 + top + n, wide]
            lane = slice(16 + f, 17 + f)
            out[8 : 8 + rows, lane] = grad[f, :, one]
            out[7:8, lane] = down[f * 8 : f * 8 + 1, one]
            out[8 + rows : 8 + rows + top, lane] = up[f * 24 : f * 24 + top, one]
        base = fields * 24
        low = fields * 8
        for s in range(slots):
            lane = slice(32 + s, 33 + s)
            out[8 : 8 + height, lane] = index[s, :, lone].astype(F32)
            out[7:8, lane] = down[low + s : low + s + 1, lone]
            out[8 + height : 9 + height, lane] = up[base + s * 8 : base + s * 8 + 1, lone]
            lane = slice(36 + s, 37 + s)
            out[8 : 8 + height, lane] = weight[s, :, lone]
            out[7:8, lane] = down[low + s : low + s + 1, wone]
            out[8 + height : 9 + height, lane] = up[base + s * 8 : base + s * 8 + 1, wone]
    base = fields * 24 + slots * 8
    low = fields * 8 + slots
    rate_out[0:4, :] = jnp.zeros((4, rate.shape[1]), F32)
    for p in range(parts):
        part = slice(p * cols, (p + 1) * cols)
        rate_out[4:8, part] = down[low + p * 4 : low + p * 4 + 4, :]
        rate_out[8 + height : 16 + height, part] = up[base + p * 8 : base + p * 8 + 8, :]
    rate_out[8 : 8 + height, :] = rate[...]


def lane_iota(shape):
    return lax.broadcasted_iota(jnp.int32, shape, len(shape) - 1)


def pick_columns(cols):
    source = lax.broadcasted_iota(jnp.int32, (cols, cols), 0)
    target = lax.broadcasted_iota(jnp.int32, (cols, cols), 1)
    half = cols // 2
    wanted = jnp.where(target < half, 2 * target, 2 * (target - half) + 1)
    return jnp.where(source == wanted, 1.0, 0.0).astype(F32)


def spread_columns(cols):
    source = lax.broadcasted_iota(jnp.int32, (cols, cols), 0)
    target = lax.broadcasted_iota(jnp.int32, (cols, cols), 1)
    half = cols // 2
    wanted = jnp.where(source < half, 2 * source, 2 * (source - half) + 1)
    return jnp.where(target == wanted, 1.0, 0.0).astype(F32)


def table_rows(index, weight):
    rows = []
    for o in range(16):
        total = jnp.zeros(index[0].shape, F32)
        for i, w in zip(index, weight):
            total = total + jnp.where(i == float(o), w, 0.0)
        rows.append(total)
    return rows


def restrict(grad, index, weight, up, down, from_west, from_east, out, ext, cols4):
    fields, rows, cols = grad.shape
    slots, height, breadth = index.shape
    top = 2 * SPREAD_PASSES + 1
    tall = height + SPREAD_PASSES
    base = fields * 24
    table = table_rows(
        [
            jnp.concatenate(
                [index[s].astype(F32), up[base + s * 8 : base + s * 8 + 8, 0:breadth]], axis=0
            )
            for s in range(slots)
        ],
        [
            jnp.concatenate([weight[s], up[base + s * 8 : base + s * 8 + 8, breadth:]], axis=0)
            for s in range(slots)
        ],
    )
    pick = pick_columns(cols)
    ext[...] = jnp.zeros(ext.shape, F32)
    lane = lane_iota((ext.shape[0], breadth))
    for f in range(fields):
        ext[8 : 8 + rows, :] = grad[f]
        ext[7:8, :] = down[f * 8 : f * 8 + 1, :]
        ext[8 + rows : 8 + rows + top, :] = up[f * 24 : f * 24 + top, :]
        both = jnp.dot(ext[...], pick, precision=EXACT, preferred_element_type=F32)
        even = both[:, :breadth]
        odd = both[:, breadth:]
        left = pltpu.roll(from_west[...], LANES - 16 - f, 1)
        right = pltpu.roll(from_east[...], LANES - 17 - f, 1)
        cols4[0] = jnp.where(lane == 0, left, pltpu.roll(odd, 1, 1))
        cols4[1] = even
        cols4[2] = odd
        cols4[3] = jnp.where(lane == breadth - 1, right, pltpu.roll(even, breadth - 1, 1))
        total = jnp.zeros((tall, breadth), F32)
        for a in range(4):
            for b in range(4):
                total = total + table[4 * a + b] * cols4[b, pl.ds(a + 7, tall, stride=2), :]
        out[f * tall : (f + 1) * tall, :] = total


def side(grad, scale, stat_rate, index, weight, up, down, from_west, from_east,
         static, table_out, box, idx, wgt, tab, *, members_all):
    fields, rows, cols = grad.shape
    slots, height, breadth = index.shape
    n = STATIC_PASSES
    top = 2 * SPREAD_PASSES + 1
    wide = cols + 2 * LANES
    shape = (rows + 16, wide)
    row = lax.broadcasted_iota(jnp.int32, shape, 0)
    col = lane_iota(shape)
    first_row = jnp.where(lax.axis_index("tile") == 0, 8, 0)
    last_row = jnp.where(lax.axis_index("tile") == lax.axis_size("tile") - 1, 8 + rows, rows + 16)
    first_col = jnp.where(lax.axis_index("mem") == 0, LANES, 0)
    last_col = jnp.where(lax.axis_index("mem") == lax.axis_size("mem") - 1, LANES + cols, wide)
    inside = (row >= first_row) & (row < last_row) & (col >= first_col) & (col < last_col)
    for f in range(fields):
        box[...] = jnp.zeros(box.shape, F32)
        box[8 : 8 + rows, LANES : LANES + cols] = scale[f] * grad[f]
        box[8 - n : 8, LANES : LANES + cols] = down[f * 8 + 1 : f * 8 + 1 + n, :]
        box[8 + rows : 8 + rows + n, LANES : LANES + cols] = up[f * 24 + top : f * 24 + top + n, :]
        box[:, LANES - n : LANES] = from_west[0 : rows + 16, 4 * f : 4 * f + n]
        box[:, LANES + cols : LANES + cols + n] = from_east[0 : rows + 16, 4 * f : 4 * f + n]
        field = box[...]
        rate = jnp.where(inside, stat_rate[f], 0.0)
        for _ in range(n):
            beside = (
                pltpu.roll(field, 1, 0)
                + pltpu.roll(field, rows + 15, 0)
                + pltpu.roll(field, 1, 1)
                + pltpu.roll(field, wide - 1, 1)
            )
            field = field + rate * (beside - 4.0 * field)
        static[f] = 0.3 * scale[f] * field[8 : 8 + rows, LANES : LANES + cols]
    factor = 2.8 / (members_all - 1)
    base = fields * 24
    low = fields * 8
    tall = height + 16
    lane = lane_iota((tall, breadth))
    for s in range(slots):
        idx[s] = jnp.zeros((tall, breadth), F32)
        wgt[s] = jnp.zeros((tall, breadth), F32)
        idx[s, 8 : 8 + height, :] = index[s].astype(F32)
        wgt[s, 8 : 8 + height, :] = weight[s]
        idx[s, 7:8, :] = down[low + s : low + s + 1, 0:breadth]
        wgt[s, 7:8, :] = down[low + s : low + s + 1, breadth:]
        idx[s, 8 + height : 9 + height, :] = up[base + s * 8 : base + s * 8 + 1, 0:breadth]
        wgt[s, 8 + height : 9 + height, :] = up[base + s * 8 : base + s * 8 + 1, breadth:]
    west = from_west[0:tall, :]
    east = from_east[0:tall, :]

    def shifted(x, shift, at):
        if shift == 1:
            return jnp.where(lane == 0, pltpu.roll(west, LANES - at, 1), pltpu.roll(x, 1, 1))
        if shift == 2:
            return jnp.where(
                lane == breadth - 1,
                pltpu.roll(east, LANES - 1 - at, 1),
                pltpu.roll(x, breadth - 1, 1),
            )
        return x

    for shift, columns in ((0, (1, 2)), (1, (3,)), (2, (0,))):
        table = table_rows(
            [shifted(idx[s], shift, 32 + s) for s in range(slots)],
            [shifted(wgt[s], shift, 36 + s) for s in range(slots)],
        )
        for b in columns:
            for a in range(4):
                off = (1, 0, 0, -1)[a]
                tab[...] = factor * table[4 * a + b]
                table_out[4 * a + b] = tab[8 + off : 8 + off + height, :]


def parts_of(width):
    return [slice(t, t + LANES) for t in range(0, width, LANES)]


def sweep(v, keep, rate, lo, hi, v_at, rate_at):
    parts = parts_of(v.shape[2])
    tiles = len(parts)
    lane = lane_iota((SUB, LANES))
    first = lane == 0
    last = lane == LANES - 1
    zero = jnp.zeros((SUB, LANES), F32)
    above = [v[lo - 1 + v_at, :, p] for p in parts]
    here = [v[lo + v_at, :, p] for p in parts]
    for r in range(lo, hi):
        below = [v[r + 1 + v_at, :, p] for p in parts]
        to_right = [pltpu.roll(x, 1, 1) for x in here]
        to_left = [pltpu.roll(x, LANES - 1, 1) for x in here]
        for t, p in enumerate(parts):
            left = jnp.where(first, to_right[t - 1] if t else zero, to_right[t])
            right = jnp.where(last, to_left[t + 1] if t + 1 < tiles else zero, to_left[t])
            total = (above[t] + below[t]) + (left + right)
            v[r + v_at, :, p] = keep[r + rate_at, :, p] * here[t] + rate[r + rate_at, :, p] * total
        above, here = here, below


def fill_rates(rate_ref, keep, rate, rows, at):
    for r in range(rows):
        line = jnp.broadcast_to(rate_ref[r + at : r + at + 1, :], rate.shape[1:])
        rate[r] = line
        keep[r] = 1.0 - 4.0 * line


def fold(total, fields):
    folded = total[0:fields]
    for j in range(fields, SUB, fields):
        folded = folded + total[j : j + fields]
    return folded


def own(*refs, count, fields):
    member_block, rate_ref = refs[0:2]
    pieces = refs[2 : 2 + count]
    own_out, beyond, far_coarse, v, m, keep, rate, c, mw, acc = refs[2 + count :]
    height = m.shape[0]
    reach = SPREAD_PASSES
    tall = height + reach
    step = pl.program_id(0)
    parts = parts_of(v.shape[2])

    @pl.when(step == 0)
    def _():
        fill_rates(rate_ref, keep, rate, height + 12, 4)
        me = lax.axis_index("mem")
        for d, piece in enumerate(pieces):
            breadth = piece.shape[1]
            where = lax.rem(me - d + count, count)
            at = pl.ds(pl.multiple_of(where * breadth, LANES), breadth)
            for r in range(tall):
                row = piece[pl.ds(r, fields, stride=tall), :]
                for j in range(0, SUB, fields):
                    if r < height:
                        c[r, j : j + fields, at] = row
                    else:
                        far_coarse[r - height, j : j + fields, at] = row
        acc[...] = jnp.zeros(acc.shape, F32)

    off = 5
    v[0:off] = jnp.zeros((off,) + v.shape[1:], F32)
    v[height + off :] = jnp.zeros((v.shape[0] - height - off,) + v.shape[1:], F32)
    for t, p in enumerate(parts):
        mw[t] = member_block[:, :, :, p].astype(F32).reshape(mw.shape[1:])
        for r in range(height):
            line = mw[t, pl.ds(r, SUB, stride=height), :]
            m[r, :, p] = line
            v[r + off, :, p] = line * c[r, :, p]
    half = SPREAD_PASSES // 2

    def early(_, x):
        sweep(v, keep, rate, -half, height + half, off, 4)
        return x

    def late(_, x):
        sweep(v, keep, rate, 1 - half, height + reach, off, 4)
        return x

    lax.fori_loop(0, half, early, 0)
    lax.fori_loop(0, SPREAD_PASSES - half, late, 0)
    for r in range(height):
        acc[r] = acc[r] + m[r] * v[r + off]
    for r in range(reach):
        beyond[0, r] = v[r + height + off]

    @pl.when(step == pl.num_programs(0) - 1)
    def _():
        for r in range(height):
            own_out[r * fields : (r + 1) * fields, :] = fold(acc[r], fields)


def cross(far_block, member_block, beyond, far_coarse, rate_ref, near_out, far_out,
          w, keep, rate, mw, fw, near, far, *, fields):
    reach = SPREAD_PASSES
    height = member_block.shape[2]
    step = pl.program_id(0)
    parts = parts_of(w.shape[2])

    @pl.when(step == 0)
    def _():
        fill_rates(rate_ref, keep, rate, 2 * reach, height)
        near[...] = jnp.zeros(near.shape, F32)
        far[...] = jnp.zeros(far.shape, F32)

    w[0 : reach + 1] = jnp.zeros((reach + 1,) + w.shape[1:], F32)
    for t, p in enumerate(parts):
        mw[t] = member_block[:, :, :, p].astype(F32).reshape(mw.shape[1:])
        fw[t] = far_block[:, :, :, p].reshape(fw.shape[1:])
        for r in range(reach):
            line = fw[t, pl.ds(r, SUB, stride=reach), :]
            w[r + reach + 1, :, p] = line * far_coarse[r, :, p]
            far[r, :, p] = far[r, :, p] + line * beyond[0, r, :, p]
    for s in range(1, SPREAD_PASSES + 1):
        sweep(w, keep, rate, height - s, height - s + reach, reach + 1 - height, reach - height)
    for t, p in enumerate(parts):
        for r in range(reach):
            line = mw[t, pl.ds(r + height - reach, SUB, stride=height), :]
            near[r, :, p] = near[r, :, p] + line * w[r + 1, :, p]

    @pl.when(step == pl.num_programs(0) - 1)
    def _():
        for r in range(reach):
            near_out[r * fields : (r + 1) * fields, :] = fold(near[r], fields)
            far_out[r * fields : (r + 1) * fields, :] = fold(far[r], fields)


def gather_parts(*refs, groups, fields):
    own_ref = refs[0]
    nears = refs[1 : 1 + groups]
    fars = refs[1 + groups : 1 + 2 * groups]
    total_out, below_out = refs[1 + 2 * groups :]
    rows = own_ref.shape[0]
    reach = SPREAD_PASSES * fields
    near = nears[0][...]
    far = fars[0][...]
    for x, y in zip(nears[1:], fars[1:]):
        near = near + x[...]
        far = far + y[...]
    near = near + own_ref[rows - reach : rows, :]
    total_out[0 : rows - reach, :] = own_ref[0 : rows - reach, :]
    total_out[rows - reach : rows, :] = near
    below_out[0:fields, :] = jnp.zeros((fields, near.shape[1]), F32)
    below_out[fields : 2 * fields, :] = near[reach - fields : reach, :]
    below_out[2 * fields :, :] = far


def pack_sums(total, below, from_above, from_below, *refs, count, fields):
    outs, held = refs[:-1], refs[-1]
    rows = total.shape[0]
    tall = held.shape[1]
    two = 2 * fields
    tiles = held.shape[0] - 2
    held[0] = jnp.zeros(held.shape[1:], F32)
    held[tiles + 1] = jnp.zeros(held.shape[1:], F32)
    parts = parts_of(total.shape[1])
    reach = from_above.shape[0]
    for t, p in enumerate(parts):
        held[t + 1, 0:two, :] = from_above[0:two, p]
        held[t + 1, two:reach, :] = from_above[two:reach, p] + total[0 : reach - two, p]
        held[t + 1, reach : rows + two, :] = total[reach - two : rows, p]
        held[t + 1, rows + two : tall, :] = below[two : 2 * two, p] + from_below[0:two, p]
    me = lax.axis_index("mem")
    lane = lane_iota((SUB, LANES))
    width = tiles // count
    for d in range(count):
        at = lax.rem(me + d, count) * width
        packed = jnp.zeros((SUB, LANES), F32)
        for w in range(width):
            outs[d][0:tall, w * LANES : (w + 1) * LANES] = held[at + 1 + w]
        for k in range(tall // SUB):
            rows8 = slice(k * SUB, (k + 1) * SUB)
            edge = jnp.where(lane == 0, held[at + 1 + width, rows8, :], held[at, rows8, :])
            edge = pltpu.roll(edge, 2 * k + 1, 1)
            packed = jnp.where((lane == 2 * k) | (lane == 2 * k + 1), edge, packed)
        outs[d][tall : tall + SUB, 0:LANES] = packed


def finish(*refs, count, fields):
    pieces = refs[:count]
    static, table, out, held, wide = refs[count:]
    height = table.shape[1]
    rows, cols = out.shape[1:]
    breadth = table.shape[2]
    tall = held.shape[1]
    total = pieces[0][...]
    for piece in pieces[1:]:
        total = total + piece[...]
    packed = total[tall:, :]
    lane = lane_iota((SUB, LANES))
    for k in range(tall // SUB):
        x = total[k * SUB : (k + 1) * SUB, :]
        rows8 = slice(k * SUB, (k + 1) * SUB)
        held[0, rows8, :] = x
        left = pltpu.roll(packed, LANES - 2 * k, 1) if k else packed
        right = pltpu.roll(packed, LANES - 2 - 2 * k, 1)
        held[1, rows8, :] = jnp.where(lane == 0, left, pltpu.roll(x, 1, 1))
        held[2, rows8, :] = jnp.where(lane == LANES - 1, right, pltpu.roll(x, LANES - 1, 1))
    for f in range(fields):
        for p in range(2):
            even = jnp.zeros((height, breadth), F32)
            odd = jnp.zeros((height, breadth), F32)
            for a, off in ((1 + p, 0), (3 - 3 * p, 2 * p - 1)):
                at = pl.ds(f + fields * (2 + off), height, stride=fields)
                here = held[0, at, :]
                even = even + table[4 * a + 1] * here + table[4 * a + 3] * held[1, at, :]
                odd = odd + table[4 * a + 2] * here + table[4 * a] * held[2, at, :]
            at = pl.ds(f * rows + p, height, stride=2)
            wide[0, at, :] = even
            wide[1, at, :] = odd
    both = jnp.concatenate([wide[0], wide[1]], axis=1)
    fine = jnp.dot(both, spread_columns(cols), precision=EXACT, preferred_element_type=F32)
    for f in range(fields):
        out[f] = static[f] + fine[f * rows : (f + 1) * rows, :]


def groups_of(pairs, count):
    count = min(count, pairs)
    sizes = [pairs // count + (1 if g < pairs % count else 0) for g in range(count)]
    return [(sum(sizes[:g]), size) for g, size in enumerate(sizes)]


def local(gradient, static_scale, static_rate, interp_index, interp_weight, members, spread_rate):
    fields, rows, cols = gradient.shape
    slots, height, breadth = interp_index.shape
    member_count, _, _, width = members.shape
    reach = SPREAD_PASSES
    tiles = lax.axis_size("tile")
    count = lax.axis_size("mem")
    upward = [(i + 1, i) for i in range(tiles - 1)]
    downward = [(i, i + 1) for i in range(tiles - 1)]
    per = SUB // fields
    pairs = member_count // per
    vmem = pl.BlockSpec(memory_space=pltpu.VMEM)
    smem = pl.BlockSpec(memory_space=pltpu.SMEM)
    smalls = (gradient, static_scale, interp_index, interp_weight, spread_rate)
    column_parts = width // cols

    up, down = call(
        pack_tile,
        [
            (fields * 24 + slots * 8 + column_parts * 8, cols),
            (fields * 8 + (slots + column_parts * 4 + 7) // 8 * 8, cols),
        ],
        name="pack_tile",
    )(*smalls)
    up = lax.ppermute(up, "tile", upward)
    down = lax.ppermute(down, "tile", downward)

    groups = groups_of(pairs, 4)
    far_members = [
        lax.ppermute(
            members[per * g : per * (g + n), :, 0:reach, :].astype(F32), "tile", upward
        )
        for g, n in groups
    ]

    west, east, rates = call(
        pack_mem,
        [(64, LANES), (64, LANES), (height + 16, width)],
        name="pack_mem",
    )(*smalls, up, down)
    from_east = lax.ppermute(west, "mem", [(i + 1, i) for i in range(count - 1)])
    from_west = lax.ppermute(east, "mem", [(i, i + 1) for i in range(count - 1)])

    tall = height + reach
    (quarter,) = call(
        restrict,
        [(fields * tall, breadth)],
        [(64, cols), (4, 64, breadth)],
        name="restrict",
    )(gradient, interp_index, interp_weight, up, down, from_west, from_east)
    pieces = [quarter] + [
        lax.ppermute(quarter, "mem", [(i, (i + d) % count) for i in range(count)])
        for d in range(1, count)
    ]

    static, table = call(
        functools.partial(side, members_all=member_count * count),
        [(fields, rows, cols), (16, height, breadth)],
        [
            (rows + 16, cols + 2 * LANES),
            (slots, height + 16, breadth),
            (slots, height + 16, breadth),
            (height + 16, breadth),
        ],
        in_specs=[vmem, vmem, smem] + [vmem] * 6,
        name="side",
    )(
        gradient, static_scale, static_rate, interp_index, interp_weight,
        up, down, from_west, from_east,
    )

    line = (SUB, width)
    lane_tiles = width // LANES
    whole = lambda i: (0, 0)
    own_sum, beyond, far_coarse = call(
        functools.partial(own, count=count, fields=fields),
        [(height * fields, width), (pairs, reach) + line, (reach,) + line],
        [
            (height + reach + 6,) + line,
            (height,) + line,
            (height + 12,) + line,
            (height + 12,) + line,
            (height,) + line,
            (lane_tiles, SUB * height, LANES),
            (height,) + line,
        ],
        grid=(pairs,),
        in_specs=[
            pl.BlockSpec((per, fields, height, width), lambda i: (i, 0, 0, 0)),
            pl.BlockSpec(rates.shape, whole),
        ]
        + [pl.BlockSpec(quarter.shape, whole)] * count,
        out_specs=(
            pl.BlockSpec((height * fields, width), whole),
            pl.BlockSpec((1, reach) + line, lambda i: (i, 0, 0, 0)),
            pl.BlockSpec((reach,) + line, lambda i: (0, 0, 0)),
        ),
        name="own",
    )(members, rates, *pieces)
    edge = lax.ppermute(own_sum[0 : 2 * fields], "tile", upward)

    nears, fars = [], []
    for (g, n), far_block in zip(groups, far_members):
        near, far = call(
            functools.partial(cross, fields=fields),
            [(reach * fields, width)] * 2,
            [
                (2 * reach + 1,) + line,
                (2 * reach,) + line,
                (2 * reach,) + line,
                (lane_tiles, SUB * height, LANES),
                (lane_tiles, SUB * reach, LANES),
                (reach,) + line,
                (reach,) + line,
            ],
            grid=(n,),
            in_specs=[
                pl.BlockSpec((per, fields, reach, width), lambda i: (i, 0, 0, 0)),
                pl.BlockSpec((per, fields, height, width), lambda i, g=g: (i + g, 0, 0, 0)),
                pl.BlockSpec((1, reach) + line, lambda i, g=g: (i + g, 0, 0, 0)),
                pl.BlockSpec((reach,) + line, lambda i: (0, 0, 0)),
                pl.BlockSpec(rates.shape, whole),
            ],
            out_specs=(pl.BlockSpec((reach * fields, width), whole),) * 2,
            name="cross",
        )(far_block, members, beyond, far_coarse, rates)
        nears.append(near)
        fars.append(far)

    total, below = call(
        functools.partial(gather_parts, groups=len(groups), fields=fields),
        [(height * fields, width), ((reach + 2) * fields, width)],
        name="gather_parts",
    )(own_sum, *nears, *fars)
    from_above = lax.ppermute(below, "tile", downward)
    high = (height + 4) * fields
    sums = call(
        functools.partial(pack_sums, count=count, fields=fields),
        [(high + SUB, breadth)] * count,
        [(lane_tiles + 2, high, LANES)],
        name="pack_sums",
    )(total, below, from_above, edge)
    arrived = [sums[0]] + [
        lax.ppermute(sums[d], "mem", [(i, (i + d) % count) for i in range(count)])
        for d in range(1, count)
    ]
    (hybrid,) = call(
        functools.partial(finish, count=count, fields=fields),
        [(fields, rows, cols)],
        [(3, high, LANES), (2, fields * rows, breadth)],
        name="finish",
    )(*arrived, static, table)
    return hybrid


def solution(mesh):
    return jax.shard_map(
        local,
        mesh=mesh,
        in_specs=(
            P(None, "tile", "mem"),
            P(None, "tile", "mem"),
            P(),
            P(None, "tile", "mem"),
            P(None, "tile", "mem"),
            P("mem", None, "tile", None),
            P("tile", None),
        ),
        out_specs=P(None, "tile", "mem"),
        check_vma=False,
    )
```

```python
import functools

import jax
import jax.numpy as jnp
from jax import lax
from jax.experimental import pallas as pl
from jax.experimental.pallas import tpu as pltpu
from jax.sharding import PartitionSpec as P


STATIC_PASSES = 4
SPREAD_PASSES = 8
LANES = 128
SUB = 8


F32 = jnp.float32
EXACT = lax.Precision.HIGHEST


def call(kernel, out_shapes, scratch=(), limit=4, **kw):
    return pl.pallas_call(
        kernel,
        out_shape=tuple(jax.ShapeDtypeStruct(s, F32) for s in out_shapes),
        scratch_shapes=[pltpu.VMEM(s, F32) for s in scratch],
        compiler_params=pltpu.CompilerParams(vmem_limit_bytes=limit << 20),
        **kw,
    )


def pack_tile(grad, scale, index, weight, rate, up, down):
    fields, rows, cols = grad.shape
    slots, height, breadth = index.shape
    parts = rate.shape[1] // cols
    reach = SPREAD_PASSES
    up[...] = jnp.zeros(up.shape, F32)
    down[...] = jnp.zeros(down.shape, F32)
    for f in range(fields):
        top = 2 * reach + 1
        up[f * 24 : f * 24 + top, :] = grad[f, 0:top, :]
        up[f * 24 + top : f * 24 + top + STATIC_PASSES, :] = (
            scale[f, 0:STATIC_PASSES, :] * grad[f, 0:STATIC_PASSES, :]
        )
        down[f * 8 : f * 8 + 1, :] = grad[f, rows - 1 : rows, :]
        down[f * 8 + 1 : f * 8 + 1 + STATIC_PASSES, :] = (
            scale[f, rows - STATIC_PASSES : rows, :] * grad[f, rows - STATIC_PASSES : rows, :]
        )
    base = fields * 24
    low = fields * 8
    for s in range(slots):
        up[base + s * 8 : base + s * 8 + 8, 0:breadth] = index[s, 0:8, :].astype(F32)
        up[base + s * 8 : base + s * 8 + 8, breadth:] = weight[s, 0:8, :]
        down[low + s : low + s + 1, 0:breadth] = index[s, height - 1 : height, :].astype(F32)
        down[low + s : low + s + 1, breadth:] = weight[s, height - 1 : height, :]
    base += slots * 8
    low += slots
    for p in range(parts):
        part = slice(p * cols, (p + 1) * cols)
        up[base + p * 8 : base + p * 8 + 8, :] = rate[0:8, part]
        down[low + p * 4 : low + p * 4 + 4, :] = rate[height - 4 : height, part]


def pack_mem(grad, scale, index, weight, rate, up, down, west, east, rate_out):
    fields, rows, cols = grad.shape
    slots, height, breadth = index.shape
    parts = rate.shape[1] // cols
    n = STATIC_PASSES
    top = 2 * SPREAD_PASSES + 1
    for out, at in ((west, 0), (east, 1)):
        out[...] = jnp.zeros(out.shape, F32)
        wide = slice(0, n) if at == 0 else slice(cols - n, cols)
        one = slice(0, 1) if at == 0 else slice(cols - 1, cols)
        lone = slice(0, 1) if at == 0 else slice(breadth - 1, breadth)
        wone = slice(breadth, breadth + 1) if at == 0 else slice(2 * breadth - 1, 2 * breadth)
        for f in range(fields):
            lane = slice(4 * f, 4 * f + n)
            out[8 : 8 + rows, lane] = scale[f, :, wide] * grad[f, :, wide]
            out[8 - n : 8, lane] = down[f * 8 + 1 : f * 8 + 1 + n, wide]
            out[8 + rows : 8 + rows + n, lane] = up[f * 24 + top : f * 24 + top + n, wide]
            lane = slice(16 + f, 17 + f)
            out[8 : 8 + rows, lane] = grad[f, :, one]
            out[7:8, lane] = down[f * 8 : f * 8 + 1, one]
            out[8 + rows : 8 + rows + top, lane] = up[f * 24 : f * 24 + top, one]
        base = fields * 24
        low = fields * 8
        for s in range(slots):
            lane = slice(32 + s, 33 + s)
            out[8 : 8 + height, lane] = index[s, :, lone].astype(F32)
            out[7:8, lane] = down[low + s : low + s + 1, lone]
            out[8 + height : 9 + height, lane] = up[base + s * 8 : base + s * 8 + 1, lone]
            lane = slice(36 + s, 37 + s)
            out[8 : 8 + height, lane] = weight[s, :, lone]
            out[7:8, lane] = down[low + s : low + s + 1, wone]
            out[8 + height : 9 + height, lane] = up[base + s * 8 : base + s * 8 + 1, wone]
    base = fields * 24 + slots * 8
    low = fields * 8 + slots
    rate_out[0:4, :] = jnp.zeros((4, rate.shape[1]), F32)
    for p in range(parts):
        part = slice(p * cols, (p + 1) * cols)
        rate_out[4:8, part] = down[low + p * 4 : low + p * 4 + 4, :]
        rate_out[8 + height : 16 + height, part] = up[base + p * 8 : base + p * 8 + 8, :]
    rate_out[8 : 8 + height, :] = rate[...]


def lane_iota(shape):
    return lax.broadcasted_iota(jnp.int32, shape, len(shape) - 1)


def pick_columns(cols):
    source = lax.broadcasted_iota(jnp.int32, (cols, cols), 0)
    target = lax.broadcasted_iota(jnp.int32, (cols, cols), 1)
    half = cols // 2
    wanted = jnp.where(target < half, 2 * target, 2 * (target - half) + 1)
    return jnp.where(source == wanted, 1.0, 0.0).astype(F32)


def spread_columns(cols):
    source = lax.broadcasted_iota(jnp.int32, (cols, cols), 0)
    target = lax.broadcasted_iota(jnp.int32, (cols, cols), 1)
    half = cols // 2
    wanted = jnp.where(source < half, 2 * source, 2 * (source - half) + 1)
    return jnp.where(target == wanted, 1.0, 0.0).astype(F32)


def table_rows(index, weight):
    rows = []
    for o in range(16):
        total = jnp.zeros(index[0].shape, F32)
        for i, w in zip(index, weight):
            total = total + jnp.where(i == float(o), w, 0.0)
        rows.append(total)
    return rows


def restrict(grad, index, weight, up, down, from_west, from_east, out, ext, cols4):
    fields, rows, cols = grad.shape
    slots, height, breadth = index.shape
    top = 2 * SPREAD_PASSES + 1
    tall = height + SPREAD_PASSES
    base = fields * 24
    table = table_rows(
        [
            jnp.concatenate(
                [index[s].astype(F32), up[base + s * 8 : base + s * 8 + 8, 0:breadth]], axis=0
            )
            for s in range(slots)
        ],
        [
            jnp.concatenate([weight[s], up[base + s * 8 : base + s * 8 + 8, breadth:]], axis=0)
            for s in range(slots)
        ],
    )
    pick = pick_columns(cols)
    ext[...] = jnp.zeros(ext.shape, F32)
    lane = lane_iota((ext.shape[0], breadth))
    for f in range(fields):
        ext[8 : 8 + rows, :] = grad[f]
        ext[7:8, :] = down[f * 8 : f * 8 + 1, :]
        ext[8 + rows : 8 + rows + top, :] = up[f * 24 : f * 24 + top, :]
        both = jnp.dot(ext[...], pick, precision=EXACT, preferred_element_type=F32)
        even = both[:, :breadth]
        odd = both[:, breadth:]
        left = pltpu.roll(from_west[...], LANES - 16 - f, 1)
        right = pltpu.roll(from_east[...], LANES - 17 - f, 1)
        cols4[0] = jnp.where(lane == 0, left, pltpu.roll(odd, 1, 1))
        cols4[1] = even
        cols4[2] = odd
        cols4[3] = jnp.where(lane == breadth - 1, right, pltpu.roll(even, breadth - 1, 1))
        total = jnp.zeros((tall, breadth), F32)
        for a in range(4):
            for b in range(4):
                total = total + table[4 * a + b] * cols4[b, pl.ds(a + 7, tall, stride=2), :]
        out[f * tall : (f + 1) * tall, :] = total


def side(grad, scale, stat_rate, index, weight, up, down, from_west, from_east,
         static, table_out, box, idx, wgt, tab, *, members_all):
    fields, rows, cols = grad.shape
    slots, height, breadth = index.shape
    n = STATIC_PASSES
    top = 2 * SPREAD_PASSES + 1
    wide = cols + 2 * LANES
    shape = (rows + 16, wide)
    row = lax.broadcasted_iota(jnp.int32, shape, 0)
    col = lane_iota(shape)
    first_row = jnp.where(lax.axis_index("tile") == 0, 8, 0)
    last_row = jnp.where(lax.axis_index("tile") == lax.axis_size("tile") - 1, 8 + rows, rows + 16)
    first_col = jnp.where(lax.axis_index("mem") == 0, LANES, 0)
    last_col = jnp.where(lax.axis_index("mem") == lax.axis_size("mem") - 1, LANES + cols, wide)
    inside = (row >= first_row) & (row < last_row) & (col >= first_col) & (col < last_col)
    for f in range(fields):
        box[...] = jnp.zeros(box.shape, F32)
        box[8 : 8 + rows, LANES : LANES + cols] = scale[f] * grad[f]
        box[8 - n : 8, LANES : LANES + cols] = down[f * 8 + 1 : f * 8 + 1 + n, :]
        box[8 + rows : 8 + rows + n, LANES : LANES + cols] = up[f * 24 + top : f * 24 + top + n, :]
        box[:, LANES - n : LANES] = from_west[0 : rows + 16, 4 * f : 4 * f + n]
        box[:, LANES + cols : LANES + cols + n] = from_east[0 : rows + 16, 4 * f : 4 * f + n]
        field = box[...]
        rate = jnp.where(inside, stat_rate[f], 0.0)
        for _ in range(n):
            beside = (
                pltpu.roll(field, 1, 0)
                + pltpu.roll(field, rows + 15, 0)
                + pltpu.roll(field, 1, 1)
                + pltpu.roll(field, wide - 1, 1)
            )
            field = field + rate * (beside - 4.0 * field)
        static[f] = 0.3 * scale[f] * field[8 : 8 + rows, LANES : LANES + cols]
    factor = 2.8 / (members_all - 1)
    base = fields * 24
    low = fields * 8
    tall = height + 16
    lane = lane_iota((tall, breadth))
    for s in range(slots):
        idx[s] = jnp.zeros((tall, breadth), F32)
        wgt[s] = jnp.zeros((tall, breadth), F32)
        idx[s, 8 : 8 + height, :] = index[s].astype(F32)
        wgt[s, 8 : 8 + height, :] = weight[s]
        idx[s, 7:8, :] = down[low + s : low + s + 1, 0:breadth]
        wgt[s, 7:8, :] = down[low + s : low + s + 1, breadth:]
        idx[s, 8 + height : 9 + height, :] = up[base + s * 8 : base + s * 8 + 1, 0:breadth]
        wgt[s, 8 + height : 9 + height, :] = up[base + s * 8 : base + s * 8 + 1, breadth:]
    west = from_west[0:tall, :]
    east = from_east[0:tall, :]

    def shifted(x, shift, at):
        if shift == 1:
            return jnp.where(lane == 0, pltpu.roll(west, LANES - at, 1), pltpu.roll(x, 1, 1))
        if shift == 2:
            return jnp.where(
                lane == breadth - 1,
                pltpu.roll(east, LANES - 1 - at, 1),
                pltpu.roll(x, breadth - 1, 1),
            )
        return x

    for shift, columns in ((0, (1, 2)), (1, (3,)), (2, (0,))):
        table = table_rows(
            [shifted(idx[s], shift, 32 + s) for s in range(slots)],
            [shifted(wgt[s], shift, 36 + s) for s in range(slots)],
        )
        for b in columns:
            for a in range(4):
                off = (1, 0, 0, -1)[a]
                tab[...] = factor * table[4 * a + b]
                table_out[4 * a + b] = tab[8 + off : 8 + off + height, :]


def parts_of(width):
    return [slice(t, t + LANES) for t in range(0, width, LANES)]


def sweep(v, keep, rate, lo, hi, v_at, rate_at):
    parts = parts_of(v.shape[2])
    lane = lane_iota((SUB, LANES))
    zero = jnp.zeros((SUB, LANES), F32)
    above = [v[lo - 1 + v_at, :, p] for p in parts]
    here = [v[lo + v_at, :, p] for p in parts]
    for r in range(lo, hi):
        below = [v[r + 1 + v_at, :, p] for p in parts]
        left = [jnp.where(lane == 0, zero, pltpu.roll(here[-1], 1, 1))] + here[:-1]
        right = here[1:] + [jnp.where(lane == LANES - 1, zero, pltpu.roll(here[0], LANES - 1, 1))]
        for t, p in enumerate(parts):
            total = (above[t] + below[t]) + (left[t] + right[t])
            v[r + v_at, :, p] = keep[r + rate_at, :, p] * here[t] + rate[r + rate_at, :, p] * total
        above, here = here, below


def permutation(width):
    source = lax.broadcasted_iota(jnp.int32, (width, width), 0)
    target = lax.broadcasted_iota(jnp.int32, (width, width), 1)
    tiles = width // LANES
    return jnp.where(source == tiles * (target % LANES) + target // LANES, 1.0, 0.0).astype(
        jnp.bfloat16
    )


def reorder(x, order, contract=0):
    dims = (((1,), (contract,)), ((), ()))
    high = x.astype(jnp.bfloat16)
    rest = x - high.astype(F32)
    middle = rest.astype(jnp.bfloat16)
    low = (rest - middle.astype(F32)).astype(jnp.bfloat16)
    moved = [
        lax.dot_general(y, order, dims, preferred_element_type=F32) for y in (high, middle, low)
    ]
    return moved[0] + (moved[1] + moved[2])


def fill_rates(rate_ref, keep, rate, rows, at):
    for r in range(rows):
        line = jnp.broadcast_to(rate_ref[r + at : r + at + 1, :], rate.shape[1:])
        rate[r] = line
        keep[r] = 1.0 - 4.0 * line


def fold(total, fields):
    folded = total[0:fields]
    for j in range(fields, SUB, fields):
        folded = folded + total[j : j + fields]
    return folded


def own(*refs, count, fields):
    member_block, rate_ref, order = refs[0:3]
    pieces = refs[3 : 3 + count]
    own_out, beyond, near_members, far_coarse, rates_out = refs[3 + count : 8 + count]
    v, m, keep, rate, c, cw, cp, mw, acc = refs[8 + count :]
    height = m.shape[0]
    reach = SPREAD_PASSES
    tall = height + reach
    step = pl.program_id(0)
    parts = parts_of(v.shape[2])

    @pl.when(step == 0)
    def _():
        rates_out[...] = reorder(rate_ref[...], order[...])
        fill_rates(rates_out, keep, rate, height + 12, 4)
        me = lax.axis_index("mem")
        for d, piece in enumerate(pieces):
            breadth = piece.shape[1]
            where = lax.rem(me - d + count, count)
            cw[:, pl.ds(pl.multiple_of(where * breadth, LANES), breadth)] = piece[...]
        moved = reorder(cw[...], order[...])
        for t, p in enumerate(parts):
            cp[t] = moved[:, p]
            for r in range(tall):
                row = cp[t, pl.ds(r, fields, stride=tall), :]
                for j in range(0, SUB, fields):
                    if r < height:
                        c[r, j : j + fields, p] = row
                    else:
                        far_coarse[r - height, j : j + fields, p] = row
        acc[...] = jnp.zeros(acc.shape, F32)

    off = 5
    v[0:off] = jnp.zeros((off,) + v.shape[1:], F32)
    v[height + off :] = jnp.zeros((v.shape[0] - height - off,) + v.shape[1:], F32)
    block = member_block[...].reshape(mw.shape[1], v.shape[2])
    moved = jnp.dot(block, order[...], preferred_element_type=F32)
    for t, p in enumerate(parts):
        mw[t] = moved[:, p]
        for r in range(height):
            line = mw[t, pl.ds(r, SUB, stride=height), :]
            m[r, :, p] = line
            v[r + off, :, p] = line * c[r, :, p]
    for s in range(1, SPREAD_PASSES + 1):
        sweep(v, keep, rate, -min(s, SPREAD_PASSES - s), height + s, off, 4)
    for r in range(height):
        acc[r] = acc[r] + m[r] * v[r + off]
    for r in range(reach):
        beyond[0, r] = v[r + height + off]
        near_members[0, r] = m[height - reach + r]

    @pl.when(step == pl.num_programs(0) - 1)
    def _():
        for r in range(height):
            own_out[r * fields : (r + 1) * fields, :] = fold(acc[r], fields)


def cross(far_block, near_members, beyond, far_coarse, rates, order, near_out, far_out,
          w, keep, rate, fw, near, far, *, fields, height):
    reach = SPREAD_PASSES
    step = pl.program_id(0)
    parts = parts_of(w.shape[2])

    @pl.when(step == 0)
    def _():
        fill_rates(rates, keep, rate, 2 * reach, height)
        near[...] = jnp.zeros(near.shape, F32)
        far[...] = jnp.zeros(far.shape, F32)

    w[0 : reach + 1] = jnp.zeros((reach + 1,) + w.shape[1:], F32)
    block = far_block[...].reshape(fw.shape[1], w.shape[2]).astype(jnp.bfloat16)
    moved = jnp.dot(block, order[...], preferred_element_type=F32)
    for t, p in enumerate(parts):
        fw[t] = moved[:, p]
        for r in range(reach):
            line = fw[t, pl.ds(r, SUB, stride=reach), :]
            w[r + reach + 1, :, p] = line * far_coarse[r, :, p]
            far[r, :, p] = far[r, :, p] + line * beyond[0, r, :, p]
    for s in range(1, SPREAD_PASSES + 1):
        sweep(w, keep, rate, height - s, height - s + reach, reach + 1 - height, reach - height)
    for r in range(reach):
        near[r] = near[r] + near_members[0, r] * w[r + 1]

    @pl.when(step == pl.num_programs(0) - 1)
    def _():
        for r in range(reach):
            near_out[r * fields : (r + 1) * fields, :] = fold(near[r], fields)
            far_out[r * fields : (r + 1) * fields, :] = fold(far[r], fields)


def gather_parts(*refs, groups, fields):
    own_ref = refs[0]
    nears = refs[1 : 1 + groups]
    fars = refs[1 + groups : 1 + 2 * groups]
    total_out, below_out = refs[1 + 2 * groups :]
    rows = own_ref.shape[0]
    reach = SPREAD_PASSES * fields
    near = nears[0][...]
    far = fars[0][...]
    for x, y in zip(nears[1:], fars[1:]):
        near = near + x[...]
        far = far + y[...]
    near = near + own_ref[rows - reach : rows, :]
    total_out[0 : rows - reach, :] = own_ref[0 : rows - reach, :]
    total_out[rows - reach : rows, :] = near
    below_out[0:fields, :] = jnp.zeros((fields, near.shape[1]), F32)
    below_out[fields : 2 * fields, :] = near[reach - fields : reach, :]
    below_out[2 * fields :, :] = far


def pack_sums(total, below, from_above, from_below, order, *refs, count, fields):
    outs, moved_in, held = refs[:-2], refs[-2], refs[-1]
    rows = total.shape[0]
    tall = held.shape[1]
    two = 2 * fields
    tiles = held.shape[0] - 2
    held[0] = jnp.zeros(held.shape[1:], F32)
    held[tiles + 1] = jnp.zeros(held.shape[1:], F32)
    reach = from_above.shape[0]
    moved_in[0:two, :] = from_above[0:two, :]
    moved_in[two:reach, :] = from_above[two:reach, :] + total[0 : reach - two, :]
    moved_in[reach : rows + two, :] = total[reach - two : rows, :]
    moved_in[rows + two : tall, :] = below[two : 2 * two, :] + from_below[0:two, :]
    natural = reorder(moved_in[...], order[...], 1)
    for t, p in enumerate(parts_of(total.shape[1])):
        held[t + 1] = natural[:, p]
    me = lax.axis_index("mem")
    lane = lane_iota((SUB, LANES))
    width = tiles // count
    for d in range(count):
        at = lax.rem(me + d, count) * width
        packed = jnp.zeros((SUB, LANES), F32)
        for w in range(width):
            outs[d][0:tall, w * LANES : (w + 1) * LANES] = held[at + 1 + w]
        for k in range(tall // SUB):
            rows8 = slice(k * SUB, (k + 1) * SUB)
            edge = jnp.where(lane == 0, held[at + 1 + width, rows8, :], held[at, rows8, :])
            edge = pltpu.roll(edge, 2 * k + 1, 1)
            packed = jnp.where((lane == 2 * k) | (lane == 2 * k + 1), edge, packed)
        outs[d][tall : tall + SUB, 0:LANES] = packed


def finish(*refs, count, fields):
    pieces = refs[:count]
    static, table, out, held, wide = refs[count:]
    height = table.shape[1]
    rows, cols = out.shape[1:]
    breadth = table.shape[2]
    tall = held.shape[1]
    total = pieces[0][...]
    for piece in pieces[1:]:
        total = total + piece[...]
    packed = total[tall:, :]
    lane = lane_iota((SUB, LANES))
    for k in range(tall // SUB):
        x = total[k * SUB : (k + 1) * SUB, :]
        rows8 = slice(k * SUB, (k + 1) * SUB)
        held[0, rows8, :] = x
        left = pltpu.roll(packed, LANES - 2 * k, 1) if k else packed
        right = pltpu.roll(packed, LANES - 2 - 2 * k, 1)
        held[1, rows8, :] = jnp.where(lane == 0, left, pltpu.roll(x, 1, 1))
        held[2, rows8, :] = jnp.where(lane == LANES - 1, right, pltpu.roll(x, LANES - 1, 1))
    for f in range(fields):
        for p in range(2):
            even = jnp.zeros((height, breadth), F32)
            odd = jnp.zeros((height, breadth), F32)
            for a, off in ((1 + p, 0), (3 - 3 * p, 2 * p - 1)):
                at = pl.ds(f + fields * (2 + off), height, stride=fields)
                here = held[0, at, :]
                even = even + table[4 * a + 1] * here + table[4 * a + 3] * held[1, at, :]
                odd = odd + table[4 * a + 2] * here + table[4 * a] * held[2, at, :]
            at = pl.ds(f * rows + p, height, stride=2)
            wide[0, at, :] = even
            wide[1, at, :] = odd
    both = jnp.concatenate([wide[0], wide[1]], axis=1)
    fine = jnp.dot(both, spread_columns(cols), precision=EXACT, preferred_element_type=F32)
    for f in range(fields):
        out[f] = static[f] + fine[f * rows : (f + 1) * rows, :]


def groups_of(pairs, count):
    count = min(count, pairs)
    sizes = [pairs // count + (1 if g < pairs % count else 0) for g in range(count)]
    return [(sum(sizes[:g]), size) for g, size in enumerate(sizes)]


def local(gradient, static_scale, static_rate, interp_index, interp_weight, members, spread_rate):
    fields, rows, cols = gradient.shape
    slots, height, breadth = interp_index.shape
    member_count, _, _, width = members.shape
    reach = SPREAD_PASSES
    tiles = lax.axis_size("tile")
    count = lax.axis_size("mem")
    upward = [(i + 1, i) for i in range(tiles - 1)]
    downward = [(i, i + 1) for i in range(tiles - 1)]
    rings = [[(i, (i + d) % count) for i in range(count)] for d in range(count)]
    per = SUB // fields
    pairs = member_count // per
    vmem = pl.BlockSpec(memory_space=pltpu.VMEM)
    smem = pl.BlockSpec(memory_space=pltpu.SMEM)
    smalls = (gradient, static_scale, interp_index, interp_weight, spread_rate)
    column_parts = width // cols
    order = permutation(width)

    up, down = call(
        pack_tile,
        [
            (fields * 24 + slots * 8 + column_parts * 8, cols),
            (fields * 8 + (slots + column_parts * 4 + 7) // 8 * 8, cols),
        ],
        name="pack_tile",
    )(*smalls)
    up = lax.ppermute(up, "tile", upward)
    down = lax.ppermute(down, "tile", downward)

    groups = groups_of(pairs, 4)
    far_members = [
        lax.ppermute(members[per * g : per * (g + n), :, 0:reach, :].astype(F32), "tile", upward)
        for g, n in groups
    ]

    west, east, rates = call(
        pack_mem,
        [(64, LANES), (64, LANES), (height + 16, width)],
        name="pack_mem",
    )(*smalls, up, down)
    from_east = lax.ppermute(west, "mem", [(i + 1, i) for i in range(count - 1)])
    from_west = lax.ppermute(east, "mem", [(i, i + 1) for i in range(count - 1)])

    tall = height + reach
    (quarter,) = call(
        restrict,
        [(fields * tall, breadth)],
        [(64, cols), (4, 64, breadth)],
        name="restrict",
    )(gradient, interp_index, interp_weight, up, down, from_west, from_east)
    pieces = [quarter] + [lax.ppermute(quarter, "mem", rings[d]) for d in range(1, count)]

    static, table = call(
        functools.partial(side, members_all=member_count * count),
        [(fields, rows, cols), (16, height, breadth)],
        [
            (rows + 16, cols + 2 * LANES),
            (slots, height + 16, breadth),
            (slots, height + 16, breadth),
            (height + 16, breadth),
        ],
        in_specs=[vmem, vmem, smem] + [vmem] * 6,
        name="side",
    )(
        gradient, static_scale, static_rate, interp_index, interp_weight,
        up, down, from_west, from_east,
    )

    line = (SUB, width)
    lane_tiles = width // LANES
    whole = lambda i: (0, 0)
    per_pair = pl.BlockSpec((1, reach) + line, lambda i: (i, 0, 0, 0))
    own_sum, beyond, near_members, far_coarse, rates = call(
        functools.partial(own, count=count, fields=fields),
        [
            (height * fields, width),
            (pairs, reach) + line,
            (pairs, reach) + line,
            (reach,) + line,
            rates.shape,
        ],
        [
            (height + reach + 6,) + line,
            (height,) + line,
            (height + 12,) + line,
            (height + 12,) + line,
            (height,) + line,
            (fields * tall, width),
            (lane_tiles, fields * tall, LANES),
            (lane_tiles, SUB * height, LANES),
            (height,) + line,
        ],
        grid=(pairs,),
        in_specs=[
            pl.BlockSpec((per, fields, height, width), lambda i: (i, 0, 0, 0)),
            pl.BlockSpec(rates.shape, whole),
            pl.BlockSpec(order.shape, whole),
        ]
        + [pl.BlockSpec(quarter.shape, whole)] * count,
        out_specs=(
            pl.BlockSpec((height * fields, width), whole),
            per_pair,
            per_pair,
            pl.BlockSpec((reach,) + line, lambda i: (0, 0, 0)),
            pl.BlockSpec(rates.shape, whole),
        ),
        limit=12,
        name="own",
    )(members, rates, order, *pieces)
    edge = lax.ppermute(own_sum[0 : 2 * fields], "tile", upward)

    nears, fars = [], []
    for k, (g, n) in enumerate(groups):
        shifted = pl.BlockSpec((1, reach) + line, lambda i, g=g: (i + g, 0, 0, 0))
        near, far = call(
            functools.partial(cross, fields=fields, height=height),
            [(reach * fields, width)] * 2,
            [
                (2 * reach + 1,) + line,
                (2 * reach,) + line,
                (2 * reach,) + line,
                (lane_tiles, SUB * reach, LANES),
                (reach,) + line,
                (reach,) + line,
            ],
            grid=(n,),
            in_specs=[
                pl.BlockSpec((per, fields, reach, width), lambda i: (i, 0, 0, 0)),
                shifted,
                shifted,
                pl.BlockSpec((reach,) + line, lambda i: (0, 0, 0)),
                pl.BlockSpec(rates.shape, whole),
                pl.BlockSpec(order.shape, whole),
            ],
            out_specs=(pl.BlockSpec((reach * fields, width), whole),) * 2,
            limit=8,
            name="cross",
        )(far_members[k], near_members, beyond, far_coarse, rates, order)
        nears.append(near)
        fars.append(far)

    total, below = call(
        functools.partial(gather_parts, groups=len(groups), fields=fields),
        [(height * fields, width), ((reach + 2) * fields, width)],
        name="gather_parts",
    )(own_sum, *nears, *fars)
    from_above = lax.ppermute(below, "tile", downward)
    high = (height + 4) * fields
    sums = call(
        functools.partial(pack_sums, count=count, fields=fields),
        [(high + SUB, breadth)] * count,
        [(high, width), (lane_tiles + 2, high, LANES)],
        name="pack_sums",
    )(total, below, from_above, edge, order)
    arrived = [sums[0]] + [lax.ppermute(sums[d], "mem", rings[d]) for d in range(1, count)]
    (hybrid,) = call(
        functools.partial(finish, count=count, fields=fields),
        [(fields, rows, cols)],
        [(3, high, LANES), (2, fields * rows, breadth)],
        name="finish",
    )(*arrived, static, table)
    return hybrid


def solution(mesh):
    return jax.shard_map(
        local,
        mesh=mesh,
        in_specs=(
            P(None, "tile", "mem"),
            P(None, "tile", "mem"),
            P(),
            P(None, "tile", "mem"),
            P(None, "tile", "mem"),
            P("mem", None, "tile", None),
            P("tile", None),
        ),
        out_specs=P(None, "tile", "mem"),
        check_vma=False,
    )
```

```python
import functools

import jax
import jax.numpy as jnp
from jax import lax
from jax.experimental import pallas as pl
from jax.experimental.pallas import tpu as pltpu
from jax.sharding import PartitionSpec as P


STATIC_PASSES = 4
SPREAD_PASSES = 8
LANES = 128
SUB = 8
VMEM_BYTES = 67043328


F32 = jnp.float32
EXACT = lax.Precision.HIGHEST


def call(kernel, out_shapes, scratch=(), limit=4, **kw):
    return pl.pallas_call(
        kernel,
        out_shape=tuple(jax.ShapeDtypeStruct(s, F32) for s in out_shapes),
        scratch_shapes=[pltpu.VMEM(s, F32) if isinstance(s, tuple) else s for s in scratch],
        compiler_params=pltpu.CompilerParams(vmem_limit_bytes=int(limit * (1 << 20))),
        **kw,
    )


def pack_tile(*refs):
    sources, (up, down), held, done = refs[:5], refs[5:7], refs[7:12], refs[12]
    copies = [
        pltpu.make_async_copy(source, target, done.at[k])
        for k, (source, target) in enumerate(zip(sources, held))
    ]
    for copy in copies:
        copy.start()
    for copy in copies:
        copy.wait()
    grad, scale, index, weight, rate = held
    fields, rows, cols = grad.shape
    slots, height, breadth = index.shape
    parts = rate.shape[1] // cols
    reach = SPREAD_PASSES
    up[...] = jnp.zeros(up.shape, F32)
    down[...] = jnp.zeros(down.shape, F32)
    for f in range(fields):
        top = 2 * reach + 1
        up[f * 24 : f * 24 + top, :] = grad[f, 0:top, :]
        up[f * 24 + top : f * 24 + top + STATIC_PASSES, :] = (
            scale[f, 0:STATIC_PASSES, :] * grad[f, 0:STATIC_PASSES, :]
        )
        down[f * 8 : f * 8 + 1, :] = grad[f, rows - 1 : rows, :]
        down[f * 8 + 1 : f * 8 + 1 + STATIC_PASSES, :] = (
            scale[f, rows - STATIC_PASSES : rows, :] * grad[f, rows - STATIC_PASSES : rows, :]
        )
    base = fields * 24
    low = fields * 8
    for s in range(slots):
        up[base + s * 8 : base + s * 8 + 8, 0:breadth] = index[s, 0:8, :].astype(F32)
        up[base + s * 8 : base + s * 8 + 8, breadth:] = weight[s, 0:8, :]
        down[low + s : low + s + 1, 0:breadth] = index[s, height - 1 : height, :].astype(F32)
        down[low + s : low + s + 1, breadth:] = weight[s, height - 1 : height, :]
    base += slots * 8
    low += slots
    for p in range(parts):
        part = slice(p * cols, (p + 1) * cols)
        up[base + p * 8 : base + p * 8 + 8, :] = rate[0:8, part]
        down[low + p * 4 : low + p * 4 + 4, :] = rate[height - 4 : height, part]


def pack_mem(grad, scale, index, weight, rate, up, down, west, east, rate_out):
    fields, rows, cols = grad.shape
    slots, height, breadth = index.shape
    parts = rate.shape[1] // cols
    n = STATIC_PASSES
    top = 2 * SPREAD_PASSES + 1
    for out, at in ((west, 0), (east, 1)):
        out[...] = jnp.zeros(out.shape, F32)
        wide = slice(0, n) if at == 0 else slice(cols - n, cols)
        one = slice(0, 1) if at == 0 else slice(cols - 1, cols)
        lone = slice(0, 1) if at == 0 else slice(breadth - 1, breadth)
        wone = slice(breadth, breadth + 1) if at == 0 else slice(2 * breadth - 1, 2 * breadth)
        for f in range(fields):
            lane = slice(4 * f, 4 * f + n)
            out[8 : 8 + rows, lane] = scale[f, :, wide] * grad[f, :, wide]
            out[8 - n : 8, lane] = down[f * 8 + 1 : f * 8 + 1 + n, wide]
            out[8 + rows : 8 + rows + n, lane] = up[f * 24 + top : f * 24 + top + n, wide]
            lane = slice(16 + f, 17 + f)
            out[8 : 8 + rows, lane] = grad[f, :, one]
            out[7:8, lane] = down[f * 8 : f * 8 + 1, one]
            out[8 + rows : 8 + rows + top, lane] = up[f * 24 : f * 24 + top, one]
        base = fields * 24
        low = fields * 8
        for s in range(slots):
            lane = slice(32 + s, 33 + s)
            out[8 : 8 + height, lane] = index[s, :, lone].astype(F32)
            out[7:8, lane] = down[low + s : low + s + 1, lone]
            out[8 + height : 9 + height, lane] = up[base + s * 8 : base + s * 8 + 1, lone]
            lane = slice(36 + s, 37 + s)
            out[8 : 8 + height, lane] = weight[s, :, lone]
            out[7:8, lane] = down[low + s : low + s + 1, wone]
            out[8 + height : 9 + height, lane] = up[base + s * 8 : base + s * 8 + 1, wone]
    base = fields * 24 + slots * 8
    low = fields * 8 + slots
    rate_out[0:4, :] = jnp.zeros((4, rate.shape[1]), F32)
    for p in range(parts):
        part = slice(p * cols, (p + 1) * cols)
        rate_out[4:8, part] = down[low + p * 4 : low + p * 4 + 4, :]
        rate_out[8 + height : 16 + height, part] = up[base + p * 8 : base + p * 8 + 8, :]
    rate_out[8 : 8 + height, :] = rate[...]


def lane_iota(shape):
    return lax.broadcasted_iota(jnp.int32, shape, len(shape) - 1)


def pick_columns(cols):
    source = lax.broadcasted_iota(jnp.int32, (cols, cols), 0)
    target = lax.broadcasted_iota(jnp.int32, (cols, cols), 1)
    half = cols // 2
    wanted = jnp.where(target < half, 2 * target, 2 * (target - half) + 1)
    return jnp.where(source == wanted, 1.0, 0.0).astype(F32)


def spread_columns(cols):
    source = lax.broadcasted_iota(jnp.int32, (cols, cols), 0)
    target = lax.broadcasted_iota(jnp.int32, (cols, cols), 1)
    half = cols // 2
    wanted = jnp.where(source < half, 2 * source, 2 * (source - half) + 1)
    return jnp.where(target == wanted, 1.0, 0.0).astype(F32)


def table_rows(index, weight):
    rows = []
    for o in range(16):
        total = jnp.zeros(index[0].shape, F32)
        for i, w in zip(index, weight):
            total = total + jnp.where(i == float(o), w, 0.0)
        rows.append(total)
    return rows


def restrict(grad, index, weight, up, down, from_west, from_east, out, ext, cols4):
    fields, rows, cols = grad.shape
    slots, height, breadth = index.shape
    top = 2 * SPREAD_PASSES + 1
    tall = height + SPREAD_PASSES
    base = fields * 24
    table = table_rows(
        [
            jnp.concatenate(
                [index[s].astype(F32), up[base + s * 8 : base + s * 8 + 8, 0:breadth]], axis=0
            )
            for s in range(slots)
        ],
        [
            jnp.concatenate([weight[s], up[base + s * 8 : base + s * 8 + 8, breadth:]], axis=0)
            for s in range(slots)
        ],
    )
    pick = pick_columns(cols)
    ext[...] = jnp.zeros(ext.shape, F32)
    lane = lane_iota((ext.shape[0], breadth))
    for f in range(fields):
        ext[8 : 8 + rows, :] = grad[f]
        ext[7:8, :] = down[f * 8 : f * 8 + 1, :]
        ext[8 + rows : 8 + rows + top, :] = up[f * 24 : f * 24 + top, :]
        both = jnp.dot(ext[...], pick, precision=EXACT, preferred_element_type=F32)
        even = both[:, :breadth]
        odd = both[:, breadth:]
        left = pltpu.roll(from_west[...], LANES - 16 - f, 1)
        right = pltpu.roll(from_east[...], LANES - 17 - f, 1)
        cols4[0] = jnp.where(lane == 0, left, pltpu.roll(odd, 1, 1))
        cols4[1] = even
        cols4[2] = odd
        cols4[3] = jnp.where(lane == breadth - 1, right, pltpu.roll(even, breadth - 1, 1))
        total = jnp.zeros((tall, breadth), F32)
        for a in range(4):
            for b in range(4):
                total = total + table[4 * a + b] * cols4[b, pl.ds(a + 7, tall, stride=2), :]
        out[f * tall : (f + 1) * tall, :] = total


def side(grad, scale, stat_rate, index, weight, up, down, from_west, from_east,
         static, table_out, box, idx, wgt, tab, *, members_all):
    fields, rows, cols = grad.shape
    slots, height, breadth = index.shape
    n = STATIC_PASSES
    top = 2 * SPREAD_PASSES + 1
    wide = cols + 2 * LANES
    shape = (rows + 16, wide)
    row = lax.broadcasted_iota(jnp.int32, shape, 0)
    col = lane_iota(shape)
    first_row = jnp.where(lax.axis_index("tile") == 0, 8, 0)
    last_row = jnp.where(lax.axis_index("tile") == lax.axis_size("tile") - 1, 8 + rows, rows + 16)
    first_col = jnp.where(lax.axis_index("mem") == 0, LANES, 0)
    last_col = jnp.where(lax.axis_index("mem") == lax.axis_size("mem") - 1, LANES + cols, wide)
    inside = (row >= first_row) & (row < last_row) & (col >= first_col) & (col < last_col)
    for f in range(fields):
        box[...] = jnp.zeros(box.shape, F32)
        box[8 : 8 + rows, LANES : LANES + cols] = scale[f] * grad[f]
        box[8 - n : 8, LANES : LANES + cols] = down[f * 8 + 1 : f * 8 + 1 + n, :]
        box[8 + rows : 8 + rows + n, LANES : LANES + cols] = up[f * 24 + top : f * 24 + top + n, :]
        box[:, LANES - n : LANES] = from_west[0 : rows + 16, 4 * f : 4 * f + n]
        box[:, LANES + cols : LANES + cols + n] = from_east[0 : rows + 16, 4 * f : 4 * f + n]
        field = box[...]
        rate = jnp.where(inside, stat_rate[f], 0.0)
        for _ in range(n):
            beside = (
                pltpu.roll(field, 1, 0)
                + pltpu.roll(field, rows + 15, 0)
                + pltpu.roll(field, 1, 1)
                + pltpu.roll(field, wide - 1, 1)
            )
            field = field + rate * (beside - 4.0 * field)
        static[f] = 0.3 * scale[f] * field[8 : 8 + rows, LANES : LANES + cols]
    factor = 2.8 / (members_all - 1)
    base = fields * 24
    low = fields * 8
    tall = height + 16
    lane = lane_iota((tall, breadth))
    for s in range(slots):
        idx[s] = jnp.zeros((tall, breadth), F32)
        wgt[s] = jnp.zeros((tall, breadth), F32)
        idx[s, 8 : 8 + height, :] = index[s].astype(F32)
        wgt[s, 8 : 8 + height, :] = weight[s]
        idx[s, 7:8, :] = down[low + s : low + s + 1, 0:breadth]
        wgt[s, 7:8, :] = down[low + s : low + s + 1, breadth:]
        idx[s, 8 + height : 9 + height, :] = up[base + s * 8 : base + s * 8 + 1, 0:breadth]
        wgt[s, 8 + height : 9 + height, :] = up[base + s * 8 : base + s * 8 + 1, breadth:]
    west = from_west[0:tall, :]
    east = from_east[0:tall, :]

    def shifted(x, shift, at):
        if shift == 1:
            return jnp.where(lane == 0, pltpu.roll(west, LANES - at, 1), pltpu.roll(x, 1, 1))
        if shift == 2:
            return jnp.where(
                lane == breadth - 1,
                pltpu.roll(east, LANES - 1 - at, 1),
                pltpu.roll(x, breadth - 1, 1),
            )
        return x

    for shift, columns in ((0, (1, 2)), (1, (3,)), (2, (0,))):
        table = table_rows(
            [shifted(idx[s], shift, 32 + s) for s in range(slots)],
            [shifted(wgt[s], shift, 36 + s) for s in range(slots)],
        )
        for b in columns:
            for a in range(4):
                off = (1, 0, 0, -1)[a]
                tab[...] = factor * table[4 * a + b]
                table_out[4 * a + b] = tab[8 + off : 8 + off + height, :]


def parts_of(width):
    return [slice(t, t + LANES) for t in range(0, width, LANES)]


def sweep(v, keep, rate, lo, hi, v_at, rate_at):
    parts = parts_of(v.shape[2])
    lane = lane_iota((SUB, LANES))
    zero = jnp.zeros((SUB, LANES), F32)
    above = [v[lo - 1 + v_at, :, p] for p in parts]
    here = [v[lo + v_at, :, p] for p in parts]
    for r in range(lo, hi):
        below = [v[r + 1 + v_at, :, p] for p in parts]
        left = [jnp.where(lane == 0, zero, pltpu.roll(here[-1], 1, 1))] + here[:-1]
        right = here[1:] + [jnp.where(lane == LANES - 1, zero, pltpu.roll(here[0], LANES - 1, 1))]
        for t, p in enumerate(parts):
            total = (above[t] + below[t]) + (left[t] + right[t])
            v[r + v_at, :, p] = keep[r + rate_at, :, p] * here[t] + rate[r + rate_at, :, p] * total
        above, here = here, below


def permutation(width):
    source = lax.broadcasted_iota(jnp.int32, (width, width), 0)
    target = lax.broadcasted_iota(jnp.int32, (width, width), 1)
    tiles = width // LANES
    return jnp.where(source == tiles * (target % LANES) + target // LANES, 1.0, 0.0).astype(
        jnp.bfloat16
    )


def reorder(x, order, contract=0):
    dims = (((1,), (contract,)), ((), ()))
    high = x.astype(jnp.bfloat16)
    rest = x - high.astype(F32)
    middle = rest.astype(jnp.bfloat16)
    low = (rest - middle.astype(F32)).astype(jnp.bfloat16)
    moved = [
        lax.dot_general(y, order, dims, preferred_element_type=F32) for y in (high, middle, low)
    ]
    return moved[0] + (moved[1] + moved[2])


def fill_rates(rate_ref, keep, rate, rows, at):
    for r in range(rows):
        line = jnp.broadcast_to(rate_ref[r + at : r + at + 1, :], rate.shape[1:])
        rate[r] = line
        keep[r] = 1.0 - 4.0 * line


def fold(total, fields):
    folded = total[0:fields]
    for j in range(fields, SUB, fields):
        folded = folded + total[j : j + fields]
    return folded


def own(*refs, count, fields):
    member_block, rate_ref, order = refs[0:3]
    pieces = refs[3 : 3 + count]
    own_out, beyond, near_members, far_coarse, rates_out = refs[3 + count : 8 + count]
    v, m, keep, rate, c, cw, cp, mw, acc = refs[8 + count :]
    height = m.shape[0]
    reach = SPREAD_PASSES
    tall = height + reach
    step = pl.program_id(0)
    parts = parts_of(v.shape[2])

    @pl.when(step == 0)
    def _():
        rates_out[...] = reorder(rate_ref[...], order[...])
        fill_rates(rates_out, keep, rate, height + 12, 4)
        me = lax.axis_index("mem")
        for d, piece in enumerate(pieces):
            breadth = piece.shape[1]
            where = lax.rem(me - d + count, count)
            cw[:, pl.ds(pl.multiple_of(where * breadth, LANES), breadth)] = piece[...]
        moved = reorder(cw[...], order[...])
        for t, p in enumerate(parts):
            cp[t] = moved[:, p]
            for r in range(tall):
                row = cp[t, pl.ds(r, fields, stride=tall), :]
                for j in range(0, SUB, fields):
                    if r < height:
                        c[r, j : j + fields, p] = row
                    else:
                        far_coarse[r - height, j : j + fields, p] = row
        acc[...] = jnp.zeros(acc.shape, F32)

    off = 5
    v[0:off] = jnp.zeros((off,) + v.shape[1:], F32)
    v[height + off :] = jnp.zeros((v.shape[0] - height - off,) + v.shape[1:], F32)
    block = member_block[...].reshape(mw.shape[1], v.shape[2])
    moved = jnp.dot(block, order[...], preferred_element_type=F32)
    for t, p in enumerate(parts):
        mw[t] = moved[:, p]
        for r in range(height):
            line = mw[t, pl.ds(r, SUB, stride=height), :]
            m[r, :, p] = line
            v[r + off, :, p] = line * c[r, :, p]
    for s in range(1, SPREAD_PASSES + 1):
        sweep(v, keep, rate, -min(s, SPREAD_PASSES - s), height + s, off, 4)
    for r in range(height):
        acc[r] = acc[r] + m[r] * v[r + off]
    for r in range(reach):
        beyond[0, r] = v[r + height + off]
        near_members[0, r] = m[height - reach + r]

    @pl.when(step == pl.num_programs(0) - 1)
    def _():
        for r in range(height):
            own_out[r * fields : (r + 1) * fields, :] = fold(acc[r], fields)


def cross(far_block, near_members, beyond, far_coarse, rates, order, near_out, far_out,
          w, keep, rate, fw, near, far, *, fields, height):
    reach = SPREAD_PASSES
    step = pl.program_id(0)
    parts = parts_of(w.shape[2])

    @pl.when(step == 0)
    def _():
        fill_rates(rates, keep, rate, 2 * reach, height)
        near[...] = jnp.zeros(near.shape, F32)
        far[...] = jnp.zeros(far.shape, F32)

    w[0 : reach + 1] = jnp.zeros((reach + 1,) + w.shape[1:], F32)
    block = far_block[...].reshape(fw.shape[1], w.shape[2]).astype(jnp.bfloat16)
    moved = jnp.dot(block, order[...], preferred_element_type=F32)
    for t, p in enumerate(parts):
        fw[t] = moved[:, p]
        for r in range(reach):
            line = fw[t, pl.ds(r, SUB, stride=reach), :]
            w[r + reach + 1, :, p] = line * far_coarse[r, :, p]
            far[r, :, p] = far[r, :, p] + line * beyond[0, r, :, p]
    for s in range(1, SPREAD_PASSES + 1):
        sweep(w, keep, rate, height - s, height - s + reach, reach + 1 - height, reach - height)
    for r in range(reach):
        near[r] = near[r] + near_members[0, r] * w[r + 1]

    @pl.when(step == pl.num_programs(0) - 1)
    def _():
        for r in range(reach):
            near_out[r * fields : (r + 1) * fields, :] = fold(near[r], fields)
            far_out[r * fields : (r + 1) * fields, :] = fold(far[r], fields)


def gather_parts(*refs, groups, fields):
    own_ref = refs[0]
    nears = refs[1 : 1 + groups]
    fars = refs[1 + groups : 1 + 2 * groups]
    total_out, below_out = refs[1 + 2 * groups :]
    rows = own_ref.shape[0]
    reach = SPREAD_PASSES * fields
    near = nears[0][...]
    far = fars[0][...]
    for x, y in zip(nears[1:], fars[1:]):
        near = near + x[...]
        far = far + y[...]
    near = near + own_ref[rows - reach : rows, :]
    total_out[0 : rows - reach, :] = own_ref[0 : rows - reach, :]
    total_out[rows - reach : rows, :] = near
    below_out[0:fields, :] = jnp.zeros((fields, near.shape[1]), F32)
    below_out[fields : 2 * fields, :] = near[reach - fields : reach, :]
    below_out[2 * fields :, :] = far


def pack_sums(total, below, from_above, from_below, order, *refs, count, fields):
    outs, moved_in, held = refs[:-2], refs[-2], refs[-1]
    rows = total.shape[0]
    tall = held.shape[1]
    two = 2 * fields
    tiles = held.shape[0] - 2
    held[0] = jnp.zeros(held.shape[1:], F32)
    held[tiles + 1] = jnp.zeros(held.shape[1:], F32)
    reach = from_above.shape[0]
    moved_in[0:two, :] = from_above[0:two, :]
    moved_in[two:reach, :] = from_above[two:reach, :] + total[0 : reach - two, :]
    moved_in[reach : rows + two, :] = total[reach - two : rows, :]
    moved_in[rows + two : tall, :] = below[two : 2 * two, :] + from_below[0:two, :]
    natural = reorder(moved_in[...], order[...], 1)
    for t, p in enumerate(parts_of(total.shape[1])):
        held[t + 1] = natural[:, p]
    me = lax.axis_index("mem")
    lane = lane_iota((SUB, LANES))
    width = tiles // count
    for d in range(count):
        at = lax.rem(me + d, count) * width
        packed = jnp.zeros((SUB, LANES), F32)
        for w in range(width):
            outs[d][0:tall, w * LANES : (w + 1) * LANES] = held[at + 1 + w]
        for k in range(tall // SUB):
            rows8 = slice(k * SUB, (k + 1) * SUB)
            edge = jnp.where(lane == 0, held[at + 1 + width, rows8, :], held[at, rows8, :])
            edge = pltpu.roll(edge, 2 * k + 1, 1)
            packed = jnp.where((lane == 2 * k) | (lane == 2 * k + 1), edge, packed)
        outs[d][tall : tall + SUB, 0:LANES] = packed


def finish(*refs, count, fields):
    pieces = refs[:count]
    static, table, out, held, wide = refs[count:]
    height = table.shape[1]
    rows, cols = out.shape[1:]
    breadth = table.shape[2]
    tall = held.shape[1]
    total = pieces[0][...]
    for piece in pieces[1:]:
        total = total + piece[...]
    packed = total[tall:, :]
    lane = lane_iota((SUB, LANES))
    for k in range(tall // SUB):
        x = total[k * SUB : (k + 1) * SUB, :]
        rows8 = slice(k * SUB, (k + 1) * SUB)
        held[0, rows8, :] = x
        left = pltpu.roll(packed, LANES - 2 * k, 1) if k else packed
        right = pltpu.roll(packed, LANES - 2 - 2 * k, 1)
        held[1, rows8, :] = jnp.where(lane == 0, left, pltpu.roll(x, 1, 1))
        held[2, rows8, :] = jnp.where(lane == LANES - 1, right, pltpu.roll(x, LANES - 1, 1))
    for f in range(fields):
        for p in range(2):
            even = jnp.zeros((height, breadth), F32)
            odd = jnp.zeros((height, breadth), F32)
            for a, off in ((1 + p, 0), (3 - 3 * p, 2 * p - 1)):
                at = pl.ds(f + fields * (2 + off), height, stride=fields)
                here = held[0, at, :]
                even = even + table[4 * a + 1] * here + table[4 * a + 3] * held[1, at, :]
                odd = odd + table[4 * a + 2] * here + table[4 * a] * held[2, at, :]
            at = pl.ds(f * rows + p, height, stride=2)
            wide[0, at, :] = even
            wide[1, at, :] = odd
    both = jnp.concatenate([wide[0], wide[1]], axis=1)
    fine = jnp.dot(both, spread_columns(cols), precision=EXACT, preferred_element_type=F32)
    for f in range(fields):
        out[f] = static[f] + fine[f * rows : (f + 1) * rows, :]


def groups_of(pairs):
    first = (pairs + 1) // 2
    last = 1 if pairs > first else 0
    sizes = [n for n in (first, pairs - first - last, last) if n]
    return [(sum(sizes[:g]), size) for g, size in enumerate(sizes)]


def local(gradient, static_scale, static_rate, interp_index, interp_weight, members, spread_rate):
    fields, rows, cols = gradient.shape
    slots, height, breadth = interp_index.shape
    member_count, _, _, width = members.shape
    reach = SPREAD_PASSES
    tiles = lax.axis_size("tile")
    count = lax.axis_size("mem")
    upward = [(i + 1, i) for i in range(tiles - 1)]
    downward = [(i, i + 1) for i in range(tiles - 1)]
    rings = [[(i, (i + d) % count) for i in range(count)] for d in range(count)]
    per = SUB // fields
    pairs = member_count // per
    vmem = pl.BlockSpec(memory_space=pltpu.VMEM)
    smem = pl.BlockSpec(memory_space=pltpu.SMEM)
    smalls = (gradient, static_scale, interp_index, interp_weight, spread_rate)
    column_parts = width // cols
    order = permutation(width)

    up, down = call(
        pack_tile,
        [
            (fields * 24 + slots * 8 + column_parts * 8, cols),
            (fields * 8 + (slots + column_parts * 4 + 7) // 8 * 8, cols),
        ],
        [pltpu.VMEM(x.shape, x.dtype) for x in smalls] + [pltpu.SemaphoreType.DMA((5,))],
        in_specs=[pl.BlockSpec(memory_space=pltpu.HBM)] * 5,
        limit=VMEM_BYTES / (1 << 20),
        name="pack_tile",
    )(*smalls)
    up = lax.ppermute(up, "tile", upward)
    down = lax.ppermute(down, "tile", downward)

    groups = groups_of(pairs)
    far_members = [
        lax.ppermute(members[per * g : per * (g + n), :, 0:reach, :].astype(F32), "tile", upward)
        for g, n in groups
    ]

    west, east, rates = call(
        pack_mem,
        [(64, LANES), (64, LANES), (height + 16, width)],
        name="pack_mem",
    )(*smalls, up, down)
    from_east = lax.ppermute(west, "mem", [(i + 1, i) for i in range(count - 1)])
    from_west = lax.ppermute(east, "mem", [(i, i + 1) for i in range(count - 1)])

    tall = height + reach
    (quarter,) = call(
        restrict,
        [(fields * tall, breadth)],
        [(64, cols), (4, 64, breadth)],
        name="restrict",
    )(gradient, interp_index, interp_weight, up, down, from_west, from_east)
    pieces = [quarter] + [lax.ppermute(quarter, "mem", rings[d]) for d in range(1, count)]

    static, table = call(
        functools.partial(side, members_all=member_count * count),
        [(fields, rows, cols), (16, height, breadth)],
        [
            (rows + 16, cols + 2 * LANES),
            (slots, height + 16, breadth),
            (slots, height + 16, breadth),
            (height + 16, breadth),
        ],
        in_specs=[vmem, vmem, smem] + [vmem] * 6,
        name="side",
    )(
        gradient, static_scale, static_rate, interp_index, interp_weight,
        up, down, from_west, from_east,
    )

    line = (SUB, width)
    lane_tiles = width // LANES
    whole = lambda i: (0, 0)
    per_pair = pl.BlockSpec((1, reach) + line, lambda i: (i, 0, 0, 0))
    own_sum, beyond, near_members, far_coarse, rates = call(
        functools.partial(own, count=count, fields=fields),
        [
            (height * fields, width),
            (pairs, reach) + line,
            (pairs, reach) + line,
            (reach,) + line,
            rates.shape,
        ],
        [
            (height + reach + 6,) + line,
            (height,) + line,
            (height + 12,) + line,
            (height + 12,) + line,
            (height,) + line,
            (fields * tall, width),
            (lane_tiles, fields * tall, LANES),
            (lane_tiles, SUB * height, LANES),
            (height,) + line,
        ],
        grid=(pairs,),
        in_specs=[
            pl.BlockSpec((per, fields, height, width), lambda i: (i, 0, 0, 0)),
            pl.BlockSpec(rates.shape, whole),
            pl.BlockSpec(order.shape, whole),
        ]
        + [pl.BlockSpec(quarter.shape, whole)] * count,
        out_specs=(
            pl.BlockSpec((height * fields, width), whole),
            per_pair,
            per_pair,
            pl.BlockSpec((reach,) + line, lambda i: (0, 0, 0)),
            pl.BlockSpec(rates.shape, whole),
        ),
        limit=12,
        name="own",
    )(members, rates, order, *pieces)
    edge = lax.ppermute(own_sum[0 : 2 * fields], "tile", upward)

    nears, fars = [], []
    for k, (g, n) in enumerate(groups):
        shifted = pl.BlockSpec((1, reach) + line, lambda i, g=g: (i + g, 0, 0, 0))
        near, far = call(
            functools.partial(cross, fields=fields, height=height),
            [(reach * fields, width)] * 2,
            [
                (2 * reach + 1,) + line,
                (2 * reach,) + line,
                (2 * reach,) + line,
                (lane_tiles, SUB * reach, LANES),
                (reach,) + line,
                (reach,) + line,
            ],
            grid=(n,),
            in_specs=[
                pl.BlockSpec((per, fields, reach, width), lambda i: (i, 0, 0, 0)),
                shifted,
                shifted,
                pl.BlockSpec((reach,) + line, lambda i: (0, 0, 0)),
                pl.BlockSpec(rates.shape, whole),
                pl.BlockSpec(order.shape, whole),
            ],
            out_specs=(pl.BlockSpec((reach * fields, width), whole),) * 2,
            limit=8,
            name="cross",
        )(far_members[k], near_members, beyond, far_coarse, rates, order)
        nears.append(near)
        fars.append(far)

    total, below = call(
        functools.partial(gather_parts, groups=len(groups), fields=fields),
        [(height * fields, width), ((reach + 2) * fields, width)],
        name="gather_parts",
    )(own_sum, *nears, *fars)
    from_above = lax.ppermute(below, "tile", downward)
    high = (height + 4) * fields
    sums = call(
        functools.partial(pack_sums, count=count, fields=fields),
        [(high + SUB, breadth)] * count,
        [(high, width), (lane_tiles + 2, high, LANES)],
        name="pack_sums",
    )(total, below, from_above, edge, order)
    arrived = [sums[0]] + [lax.ppermute(sums[d], "mem", rings[d]) for d in range(1, count)]
    (hybrid,) = call(
        functools.partial(finish, count=count, fields=fields),
        [(fields, rows, cols)],
        [(3, high, LANES), (2, fields * rows, breadth)],
        name="finish",
    )(*arrived, static, table)
    return hybrid


def solution(mesh):
    return jax.shard_map(
        local,
        mesh=mesh,
        in_specs=(
            P(None, "tile", "mem"),
            P(None, "tile", "mem"),
            P(),
            P(None, "tile", "mem"),
            P(None, "tile", "mem"),
            P("mem", None, "tile", None),
            P("tile", None),
        ),
        out_specs=P(None, "tile", "mem"),
        check_vma=False,
    )
```

```python
import functools

import jax
import jax.numpy as jnp
from jax import lax
from jax.experimental import pallas as pl
from jax.experimental.pallas import tpu as pltpu
from jax.sharding import PartitionSpec as P


STATIC_PASSES = 4
SPREAD_PASSES = 8
LANES = 128
SUB = 8
VMEM_BYTES = 67043328


F32 = jnp.float32
EXACT = lax.Precision.HIGHEST


def call(kernel, out_shapes, scratch=(), limit=4, **kw):
    return pl.pallas_call(
        kernel,
        out_shape=tuple(jax.ShapeDtypeStruct(s, F32) for s in out_shapes),
        scratch_shapes=[pltpu.VMEM(s, F32) if isinstance(s, tuple) else s for s in scratch],
        compiler_params=pltpu.CompilerParams(vmem_limit_bytes=int(limit * (1 << 20))),
        **kw,
    )


def pack_tile(*refs):
    sources, (up, down), held, done = refs[:5], refs[5:7], refs[7:12], refs[12]
    copies = [
        pltpu.make_async_copy(source, target, done.at[k])
        for k, (source, target) in enumerate(zip(sources, held))
    ]
    for copy in copies:
        copy.start()
    for copy in copies:
        copy.wait()
    grad, scale, index, weight, rate = held
    fields, rows, cols = grad.shape
    slots, height, breadth = index.shape
    parts = rate.shape[1] // cols
    reach = SPREAD_PASSES
    up[...] = jnp.zeros(up.shape, F32)
    down[...] = jnp.zeros(down.shape, F32)
    for f in range(fields):
        top = 2 * reach + 1
        up[f * 24 : f * 24 + top, :] = grad[f, 0:top, :]
        up[f * 24 + top : f * 24 + top + STATIC_PASSES, :] = (
            scale[f, 0:STATIC_PASSES, :] * grad[f, 0:STATIC_PASSES, :]
        )
        down[f * 8 : f * 8 + 1, :] = grad[f, rows - 1 : rows, :]
        down[f * 8 + 1 : f * 8 + 1 + STATIC_PASSES, :] = (
            scale[f, rows - STATIC_PASSES : rows, :] * grad[f, rows - STATIC_PASSES : rows, :]
        )
    base = fields * 24
    low = fields * 8
    for s in range(slots):
        up[base + s * 8 : base + s * 8 + 8, 0:breadth] = index[s, 0:8, :].astype(F32)
        up[base + s * 8 : base + s * 8 + 8, breadth:] = weight[s, 0:8, :]
        down[low + s : low + s + 1, 0:breadth] = index[s, height - 1 : height, :].astype(F32)
        down[low + s : low + s + 1, breadth:] = weight[s, height - 1 : height, :]
    base += slots * 8
    low += slots
    for p in range(parts):
        part = slice(p * cols, (p + 1) * cols)
        up[base + p * 8 : base + p * 8 + 8, :] = rate[0:8, part]
        down[low + p * 4 : low + p * 4 + 4, :] = rate[height - 4 : height, part]


def lane_iota(shape):
    return lax.broadcasted_iota(jnp.int32, shape, len(shape) - 1)


def pick_columns(cols):
    source = lax.broadcasted_iota(jnp.int32, (cols, cols), 0)
    target = lax.broadcasted_iota(jnp.int32, (cols, cols), 1)
    half = cols // 2
    wanted = jnp.where(target < half, 2 * target, 2 * (target - half) + 1)
    return jnp.where(source == wanted, 1.0, 0.0).astype(F32)


def spread_columns(cols):
    source = lax.broadcasted_iota(jnp.int32, (cols, cols), 0)
    target = lax.broadcasted_iota(jnp.int32, (cols, cols), 1)
    half = cols // 2
    wanted = jnp.where(source < half, 2 * source, 2 * (source - half) + 1)
    return jnp.where(target == wanted, 1.0, 0.0).astype(F32)


def table_rows(index, weight):
    rows = []
    for o in range(16):
        total = jnp.zeros(index[0].shape, F32)
        for i, w in zip(index, weight):
            total = total + jnp.where(i == float(o), w, 0.0)
        rows.append(total)
    return rows


def restrict(grad, scale, index, weight, rate, up, down, out, rate_out, ext, cols4, edge):
    fields, rows, cols = grad.shape
    slots, height, breadth = index.shape
    parts = rate.shape[1] // cols
    n = STATIC_PASSES
    top = 2 * SPREAD_PASSES + 1
    tall = height + SPREAD_PASSES
    base = fields * 24
    low = fields * 8
    table = table_rows(
        [
            jnp.concatenate(
                [index[s].astype(F32), up[base + s * 8 : base + s * 8 + 8, 0:breadth]], axis=0
            )
            for s in range(slots)
        ],
        [
            jnp.concatenate([weight[s], up[base + s * 8 : base + s * 8 + 8, breadth:]], axis=0)
            for s in range(slots)
        ],
    )
    pick = pick_columns(cols)
    ext[...] = jnp.zeros(ext.shape, F32)
    edge[...] = jnp.zeros(edge.shape, F32)
    lane = lane_iota((ext.shape[0], breadth))
    for f in range(fields):
        ext[8 : 8 + rows, :] = grad[f]
        ext[7:8, :] = down[f * 8 : f * 8 + 1, :]
        ext[8 + rows : 8 + rows + top, :] = up[f * 24 : f * 24 + top, :]
        edge[:, 16 + f : 17 + f] = ext[:, 0:1]
        edge[:, 80 + f : 81 + f] = ext[:, cols - 1 : cols]
        both = jnp.dot(ext[...], pick, precision=EXACT, preferred_element_type=F32)
        even = both[:, :breadth]
        odd = both[:, breadth:]
        cols4[0] = jnp.where(lane == 0, 0.0, pltpu.roll(odd, 1, 1))
        cols4[1] = even
        cols4[2] = odd
        cols4[3] = jnp.where(lane == breadth - 1, 0.0, pltpu.roll(even, breadth - 1, 1))
        total = jnp.zeros((tall, breadth), F32)
        for a in range(4):
            for b in range(4):
                total = total + table[4 * a + b] * cols4[b, pl.ds(a + 7, tall, stride=2), :]
        out[f * tall : (f + 1) * tall, :] = total
    for at, wide, lone in ((0, 0, 0), (64, cols - n, breadth - 1)):
        for f in range(fields):
            lanes = slice(at + 4 * f, at + 4 * f + n)
            columns = slice(wide, wide + n)
            edge[8 : 8 + rows, lanes] = scale[f, :, columns] * grad[f, :, columns]
            edge[8 - n : 8, lanes] = down[f * 8 + 1 : f * 8 + 1 + n, columns]
            edge[8 + rows : 8 + rows + n, lanes] = up[f * 24 + top : f * 24 + top + n, columns]
        one = slice(lone, lone + 1)
        second = slice(breadth + lone, breadth + lone + 1)
        for s in range(slots):
            lanes = slice(at + 32 + s, at + 33 + s)
            edge[8 : 8 + height, lanes] = index[s, :, one].astype(F32)
            edge[7:8, lanes] = down[low + s : low + s + 1, one]
            edge[8 + height : 9 + height, lanes] = up[base + s * 8 : base + s * 8 + 1, one]
            lanes = slice(at + 36 + s, at + 37 + s)
            edge[8 : 8 + height, lanes] = weight[s, :, one]
            edge[7:8, lanes] = down[low + s : low + s + 1, second]
            edge[8 + height : 9 + height, lanes] = up[base + s * 8 : base + s * 8 + 1, second]
        for a in range(4):
            entry = table[4 * a] if at == 0 else table[4 * a + 3]
            edge[8 : 8 + tall, at + 40 + a : at + 41 + a] = entry[:, one]
    out[fields * tall :, :] = edge[...]
    base = fields * 24 + slots * 8
    low = fields * 8 + slots
    rate_out[0:4, :] = jnp.zeros((4, rate.shape[1]), F32)
    for p in range(parts):
        part = slice(p * cols, (p + 1) * cols)
        rate_out[4:8, part] = down[low + p * 4 : low + p * 4 + 4, :]
        rate_out[8 + height : 16 + height, part] = up[base + p * 8 : base + p * 8 + 8, :]
    rate_out[8 : 8 + height, :] = rate[...]


def side(grad, scale, stat_rate, index, weight, up, down, west_message, east_message,
         static, table_out, box, idx, wgt, tab, *, members_all):
    fields, rows, cols = grad.shape
    slots, height, breadth = index.shape
    n = STATIC_PASSES
    top = 2 * SPREAD_PASSES + 1
    me = lax.axis_index("mem")
    skip = fields * (height + SPREAD_PASSES)
    from_west = jnp.where(me > 0, pltpu.roll(west_message[skip:, :], 64, 1), 0.0)
    from_east = jnp.where(me < lax.axis_size("mem") - 1, east_message[skip:, :], 0.0)
    wide = cols + 2 * LANES
    shape = (rows + 16, wide)
    row = lax.broadcasted_iota(jnp.int32, shape, 0)
    col = lane_iota(shape)
    first_row = jnp.where(lax.axis_index("tile") == 0, 8, 0)
    last_row = jnp.where(lax.axis_index("tile") == lax.axis_size("tile") - 1, 8 + rows, rows + 16)
    first_col = jnp.where(lax.axis_index("mem") == 0, LANES, 0)
    last_col = jnp.where(lax.axis_index("mem") == lax.axis_size("mem") - 1, LANES + cols, wide)
    inside = (row >= first_row) & (row < last_row) & (col >= first_col) & (col < last_col)
    for f in range(fields):
        box[...] = jnp.zeros(box.shape, F32)
        box[8 : 8 + rows, LANES : LANES + cols] = scale[f] * grad[f]
        box[8 - n : 8, LANES : LANES + cols] = down[f * 8 + 1 : f * 8 + 1 + n, :]
        box[8 + rows : 8 + rows + n, LANES : LANES + cols] = up[f * 24 + top : f * 24 + top + n, :]
        box[:, LANES - n : LANES] = from_west[0 : rows + 16, 4 * f : 4 * f + n]
        box[:, LANES + cols : LANES + cols + n] = from_east[0 : rows + 16, 4 * f : 4 * f + n]
        field = box[...]
        rate = jnp.where(inside, stat_rate[f], 0.0)
        for _ in range(n):
            beside = (
                pltpu.roll(field, 1, 0)
                + pltpu.roll(field, rows + 15, 0)
                + pltpu.roll(field, 1, 1)
                + pltpu.roll(field, wide - 1, 1)
            )
            field = field + rate * (beside - 4.0 * field)
        static[f] = 0.3 * scale[f] * field[8 : 8 + rows, LANES : LANES + cols]
    factor = 2.8 / (members_all - 1)
    base = fields * 24
    low = fields * 8
    tall = height + 16
    lane = lane_iota((tall, breadth))
    for s in range(slots):
        idx[s] = jnp.zeros((tall, breadth), F32)
        wgt[s] = jnp.zeros((tall, breadth), F32)
        idx[s, 8 : 8 + height, :] = index[s].astype(F32)
        wgt[s, 8 : 8 + height, :] = weight[s]
        idx[s, 7:8, :] = down[low + s : low + s + 1, 0:breadth]
        wgt[s, 7:8, :] = down[low + s : low + s + 1, breadth:]
        idx[s, 8 + height : 9 + height, :] = up[base + s * 8 : base + s * 8 + 1, 0:breadth]
        wgt[s, 8 + height : 9 + height, :] = up[base + s * 8 : base + s * 8 + 1, breadth:]
    west = from_west[0:tall, :]
    east = from_east[0:tall, :]

    def shifted(x, shift, at):
        if shift == 1:
            return jnp.where(lane == 0, pltpu.roll(west, LANES - at, 1), pltpu.roll(x, 1, 1))
        if shift == 2:
            return jnp.where(
                lane == breadth - 1,
                pltpu.roll(east, LANES - 1 - at, 1),
                pltpu.roll(x, breadth - 1, 1),
            )
        return x

    for shift, columns in ((0, (1, 2)), (1, (3,)), (2, (0,))):
        table = table_rows(
            [shifted(idx[s], shift, 32 + s) for s in range(slots)],
            [shifted(wgt[s], shift, 36 + s) for s in range(slots)],
        )
        for b in columns:
            for a in range(4):
                off = (1, 0, 0, -1)[a]
                tab[...] = factor * table[4 * a + b]
                table_out[4 * a + b] = tab[8 + off : 8 + off + height, :]


def parts_of(width):
    return [slice(t, t + LANES) for t in range(0, width, LANES)]


def sweep(v, keep, rate, lo, hi, v_at, rate_at):
    parts = parts_of(v.shape[2])
    lane = lane_iota((SUB, LANES))
    zero = jnp.zeros((SUB, LANES), F32)
    above = [v[lo - 1 + v_at, :, p] for p in parts]
    here = [v[lo + v_at, :, p] for p in parts]
    for r in range(lo, hi):
        below = [v[r + 1 + v_at, :, p] for p in parts]
        left = [jnp.where(lane == 0, zero, pltpu.roll(here[-1], 1, 1))] + here[:-1]
        right = here[1:] + [jnp.where(lane == LANES - 1, zero, pltpu.roll(here[0], LANES - 1, 1))]
        for t, p in enumerate(parts):
            total = (above[t] + below[t]) + (left[t] + right[t])
            v[r + v_at, :, p] = keep[r + rate_at, :, p] * here[t] + rate[r + rate_at, :, p] * total
        above, here = here, below


def permutation(width):
    source = lax.broadcasted_iota(jnp.int32, (width, width), 0)
    target = lax.broadcasted_iota(jnp.int32, (width, width), 1)
    tiles = width // LANES
    return jnp.where(source == tiles * (target % LANES) + target // LANES, 1.0, 0.0).astype(
        jnp.bfloat16
    )


def reorder(x, order, contract=0):
    dims = (((1,), (contract,)), ((), ()))
    high = x.astype(jnp.bfloat16)
    rest = x - high.astype(F32)
    middle = rest.astype(jnp.bfloat16)
    low = (rest - middle.astype(F32)).astype(jnp.bfloat16)
    moved = [
        lax.dot_general(y, order, dims, preferred_element_type=F32) for y in (high, middle, low)
    ]
    return moved[0] + (moved[1] + moved[2])


def fill_rates(rate_ref, keep, rate, rows, at):
    for r in range(rows):
        line = jnp.broadcast_to(rate_ref[r + at : r + at + 1, :], rate.shape[1:])
        rate[r] = line
        keep[r] = 1.0 - 4.0 * line


def fold(total, fields):
    folded = total[0:fields]
    for j in range(fields, SUB, fields):
        folded = folded + total[j : j + fields]
    return folded


def own(*refs, count, fields):
    member_block, rate_ref, order = refs[0:3]
    pieces = refs[3 : 3 + count]
    own_out, beyond, near_members, far_coarse, rates_out = refs[3 + count : 8 + count]
    v, m, keep, rate, c, cw, cp, mw, acc, eb = refs[8 + count :]
    height = m.shape[0]
    reach = SPREAD_PASSES
    tall = height + reach
    step = pl.program_id(0)
    parts = parts_of(v.shape[2])

    @pl.when(step == 0)
    def _():
        rates_out[...] = reorder(rate_ref[...], order[...])
        fill_rates(rates_out, keep, rate, height + 12, 4)
        me = lax.axis_index("mem")
        for d, piece in enumerate(pieces):
            breadth = piece.shape[1]
            where = lax.rem(me - d + count, count)
            at = pl.ds(pl.multiple_of(where * breadth, LANES), breadth)
            cw[:, at] = piece[0 : fields * tall, :]
            eb[where] = piece[fields * tall :, :]
        lane = lane_iota((tall, LANES))
        for q in range(count - 1):
            last = (q + 1) * breadth
            for mine, other, table_at, grad_at, goal in (
                (q, q + 1, 104, 16, last - 1),
                (q + 1, q, 40, 80, last),
            ):
                added = jnp.zeros((tall, LANES), F32)
                for a in range(4):
                    entry = eb[mine, 8 : 8 + tall, table_at + a : table_at + a + 1]
                    added = added + entry * eb[other, pl.ds(a + 7, tall, stride=2), :]
                begin = goal // LANES * LANES
                for f in range(fields):
                    turn = (goal - begin - grad_at - f) % LANES
                    here = jnp.where(lane == goal - begin, pltpu.roll(added, turn, 1), 0.0)
                    rows = slice(f * tall, (f + 1) * tall)
                    cw[rows, begin : begin + LANES] = cw[rows, begin : begin + LANES] + here
        moved = reorder(cw[...], order[...])
        for t, p in enumerate(parts):
            cp[t] = moved[:, p]
            for r in range(tall):
                row = cp[t, pl.ds(r, fields, stride=tall), :]
                for j in range(0, SUB, fields):
                    if r < height:
                        c[r, j : j + fields, p] = row
                    else:
                        far_coarse[r - height, j : j + fields, p] = row
        acc[...] = jnp.zeros(acc.shape, F32)

    off = 5
    v[0:off] = jnp.zeros((off,) + v.shape[1:], F32)
    v[height + off :] = jnp.zeros((v.shape[0] - height - off,) + v.shape[1:], F32)
    block = member_block[...].reshape(mw.shape[1], v.shape[2])
    moved = jnp.dot(block, order[...], preferred_element_type=F32)
    for t, p in enumerate(parts):
        mw[t] = moved[:, p]
        for r in range(height):
            line = mw[t, pl.ds(r, SUB, stride=height), :]
            m[r, :, p] = line
            v[r + off, :, p] = line * c[r, :, p]
    for s in range(1, SPREAD_PASSES + 1):
        sweep(v, keep, rate, -min(s, SPREAD_PASSES - s), height + s, off, 4)
    for r in range(height):
        acc[r] = acc[r] + m[r] * v[r + off]
    for r in range(reach):
        beyond[0, r] = v[r + height + off]
        near_members[0, r] = m[height - reach + r]

    @pl.when(step == pl.num_programs(0) - 1)
    def _():
        for r in range(height):
            own_out[r * fields : (r + 1) * fields, :] = fold(acc[r], fields)


def cross(far_block, near_members, beyond, far_coarse, rates, order, near_out, far_out,
          w, keep, rate, fw, near, far, *, fields, height):
    reach = SPREAD_PASSES
    step = pl.program_id(0)
    parts = parts_of(w.shape[2])

    @pl.when(step == 0)
    def _():
        fill_rates(rates, keep, rate, 2 * reach, height)
        near[...] = jnp.zeros(near.shape, F32)
        far[...] = jnp.zeros(far.shape, F32)

    w[0 : reach + 1] = jnp.zeros((reach + 1,) + w.shape[1:], F32)
    block = far_block[...].reshape(fw.shape[1], w.shape[2]).astype(jnp.bfloat16)
    moved = jnp.dot(block, order[...], preferred_element_type=F32)
    for t, p in enumerate(parts):
        fw[t] = moved[:, p]
        for r in range(reach):
            line = fw[t, pl.ds(r, SUB, stride=reach), :]
            w[r + reach + 1, :, p] = line * far_coarse[r, :, p]
            far[r, :, p] = far[r, :, p] + line * beyond[0, r, :, p]
    for s in range(1, SPREAD_PASSES + 1):
        sweep(w, keep, rate, height - s, height - s + reach, reach + 1 - height, reach - height)
    for r in range(reach):
        near[r] = near[r] + near_members[0, r] * w[r + 1]

    @pl.when(step == pl.num_programs(0) - 1)
    def _():
        for r in range(reach):
            near_out[r * fields : (r + 1) * fields, :] = fold(near[r], fields)
            far_out[r * fields : (r + 1) * fields, :] = fold(far[r], fields)


def gather_parts(*refs, groups, fields):
    own_ref = refs[0]
    nears = refs[1 : 1 + groups]
    fars = refs[1 + groups : 1 + 2 * groups]
    total_out, below_out = refs[1 + 2 * groups :]
    rows = own_ref.shape[0]
    reach = SPREAD_PASSES * fields
    near = nears[0][...]
    far = fars[0][...]
    for x, y in zip(nears[1:], fars[1:]):
        near = near + x[...]
        far = far + y[...]
    near = near + own_ref[rows - reach : rows, :]
    total_out[0 : rows - reach, :] = own_ref[0 : rows - reach, :]
    total_out[rows - reach : rows, :] = near
    below_out[0:fields, :] = jnp.zeros((fields, near.shape[1]), F32)
    below_out[fields : 2 * fields, :] = near[reach - fields : reach, :]
    below_out[2 * fields :, :] = far


def pack_sums(total, below, from_above, from_below, order, *refs, count, fields):
    outs, moved_in, held = refs[:-2], refs[-2], refs[-1]
    rows = total.shape[0]
    tall = held.shape[1]
    two = 2 * fields
    tiles = held.shape[0] - 2
    held[0] = jnp.zeros(held.shape[1:], F32)
    held[tiles + 1] = jnp.zeros(held.shape[1:], F32)
    reach = from_above.shape[0]
    moved_in[0:two, :] = from_above[0:two, :]
    moved_in[two:reach, :] = from_above[two:reach, :] + total[0 : reach - two, :]
    moved_in[reach : rows + two, :] = total[reach - two : rows, :]
    moved_in[rows + two : tall, :] = below[two : 2 * two, :] + from_below[0:two, :]
    natural = reorder(moved_in[...], order[...], 1)
    for t, p in enumerate(parts_of(total.shape[1])):
        held[t + 1] = natural[:, p]
    me = lax.axis_index("mem")
    lane = lane_iota((SUB, LANES))
    width = tiles // count
    for d in range(count):
        at = lax.rem(me + d, count) * width
        packed = jnp.zeros((SUB, LANES), F32)
        for w in range(width):
            outs[d][0:tall, w * LANES : (w + 1) * LANES] = held[at + 1 + w]
        for k in range(tall // SUB):
            rows8 = slice(k * SUB, (k + 1) * SUB)
            edge = jnp.where(lane == 0, held[at + 1 + width, rows8, :], held[at, rows8, :])
            edge = pltpu.roll(edge, 2 * k + 1, 1)
            packed = jnp.where((lane == 2 * k) | (lane == 2 * k + 1), edge, packed)
        outs[d][tall : tall + SUB, 0:LANES] = packed


def finish(*refs, count, fields):
    pieces = refs[:count]
    static, table, out, held, wide = refs[count:]
    height = table.shape[1]
    rows, cols = out.shape[1:]
    breadth = table.shape[2]
    tall = held.shape[1]
    total = pieces[0][...]
    for piece in pieces[1:]:
        total = total + piece[...]
    packed = total[tall:, :]
    lane = lane_iota((SUB, LANES))
    for k in range(tall // SUB):
        x = total[k * SUB : (k + 1) * SUB, :]
        rows8 = slice(k * SUB, (k + 1) * SUB)
        held[0, rows8, :] = x
        left = pltpu.roll(packed, LANES - 2 * k, 1) if k else packed
        right = pltpu.roll(packed, LANES - 2 - 2 * k, 1)
        held[1, rows8, :] = jnp.where(lane == 0, left, pltpu.roll(x, 1, 1))
        held[2, rows8, :] = jnp.where(lane == LANES - 1, right, pltpu.roll(x, LANES - 1, 1))
    for f in range(fields):
        for p in range(2):
            even = jnp.zeros((height, breadth), F32)
            odd = jnp.zeros((height, breadth), F32)
            for a, off in ((1 + p, 0), (3 - 3 * p, 2 * p - 1)):
                at = pl.ds(f + fields * (2 + off), height, stride=fields)
                here = held[0, at, :]
                even = even + table[4 * a + 1] * here + table[4 * a + 3] * held[1, at, :]
                odd = odd + table[4 * a + 2] * here + table[4 * a] * held[2, at, :]
            at = pl.ds(f * rows + p, height, stride=2)
            wide[0, at, :] = even
            wide[1, at, :] = odd
    both = jnp.concatenate([wide[0], wide[1]], axis=1)
    fine = jnp.dot(both, spread_columns(cols), precision=EXACT, preferred_element_type=F32)
    for f in range(fields):
        out[f] = static[f] + fine[f * rows : (f + 1) * rows, :]


def groups_of(pairs):
    sizes = [max(1, pairs // 5), max(1, 2 * pairs // 5)]
    sizes += [max(1, pairs - sum(sizes) - 1), 1]
    return [(sum(sizes[:g]), size) for g, size in enumerate(sizes)]


def local(gradient, static_scale, static_rate, interp_index, interp_weight, members, spread_rate):
    fields, rows, cols = gradient.shape
    slots, height, breadth = interp_index.shape
    member_count, _, _, width = members.shape
    reach = SPREAD_PASSES
    tiles = lax.axis_size("tile")
    count = lax.axis_size("mem")
    upward = [(i + 1, i) for i in range(tiles - 1)]
    downward = [(i, i + 1) for i in range(tiles - 1)]
    rings = [[(i, (i + d) % count) for i in range(count)] for d in range(count)]
    per = SUB // fields
    pairs = member_count // per
    vmem = pl.BlockSpec(memory_space=pltpu.VMEM)
    smem = pl.BlockSpec(memory_space=pltpu.SMEM)
    smalls = (gradient, static_scale, interp_index, interp_weight, spread_rate)
    column_parts = width // cols
    order = permutation(width)

    groups = groups_of(pairs)
    far_members = [
        lax.ppermute(members[per * g : per * (g + n), :, 0:reach, :].astype(F32), "tile", upward)
        for g, n in groups
    ]

    up, down = call(
        pack_tile,
        [
            (fields * 24 + slots * 8 + column_parts * 8, cols),
            (fields * 8 + (slots + column_parts * 4 + 7) // 8 * 8, cols),
        ],
        [pltpu.VMEM(x.shape, x.dtype) for x in smalls] + [pltpu.SemaphoreType.DMA((5,))],
        in_specs=[pl.BlockSpec(memory_space=pltpu.HBM)] * 5,
        limit=VMEM_BYTES / (1 << 20),
        name="pack_tile",
    )(*smalls)
    up = lax.ppermute(up, "tile", upward)
    down = lax.ppermute(down, "tile", downward)

    tall = height + reach
    message = (fields * tall + 64, breadth)
    quarter, rates = call(
        restrict,
        [message, (height + 16, width)],
        [(64, cols), (4, 64, breadth), (64, LANES)],
        name="restrict",
    )(*smalls, up, down)
    pieces = [quarter] + [lax.ppermute(quarter, "mem", rings[d]) for d in range(1, count)]

    static, table = call(
        functools.partial(side, members_all=member_count * count),
        [(fields, rows, cols), (16, height, breadth)],
        [
            (rows + 16, cols + 2 * LANES),
            (slots, height + 16, breadth),
            (slots, height + 16, breadth),
            (height + 16, breadth),
        ],
        in_specs=[vmem, vmem, smem] + [vmem] * 6,
        name="side",
    )(
        gradient, static_scale, static_rate, interp_index, interp_weight,
        up, down, pieces[1], pieces[-1],
    )

    line = (SUB, width)
    lane_tiles = width // LANES
    whole = lambda i: (0, 0)
    per_pair = pl.BlockSpec((1, reach) + line, lambda i: (i, 0, 0, 0))
    own_sum, beyond, near_members, far_coarse, rates = call(
        functools.partial(own, count=count, fields=fields),
        [
            (height * fields, width),
            (pairs, reach) + line,
            (pairs, reach) + line,
            (reach,) + line,
            rates.shape,
        ],
        [
            (height + reach + 6,) + line,
            (height,) + line,
            (height + 12,) + line,
            (height + 12,) + line,
            (height,) + line,
            (fields * tall, width),
            (lane_tiles, fields * tall, LANES),
            (lane_tiles, SUB * height, LANES),
            (height,) + line,
            (count, 64, LANES),
        ],
        grid=(pairs,),
        in_specs=[
            pl.BlockSpec((per, fields, height, width), lambda i: (i, 0, 0, 0)),
            pl.BlockSpec(rates.shape, whole),
            pl.BlockSpec(order.shape, whole),
        ]
        + [pl.BlockSpec(quarter.shape, whole)] * count,
        out_specs=(
            pl.BlockSpec((height * fields, width), whole),
            per_pair,
            per_pair,
            pl.BlockSpec((reach,) + line, lambda i: (0, 0, 0)),
            pl.BlockSpec(rates.shape, whole),
        ),
        limit=12,
        name="own",
    )(members, rates, order, *pieces)
    edge = lax.ppermute(own_sum[0 : 2 * fields], "tile", upward)

    nears, fars = [], []
    for k, (g, n) in enumerate(groups):
        shifted = pl.BlockSpec((1, reach) + line, lambda i, g=g: (i + g, 0, 0, 0))
        near, far = call(
            functools.partial(cross, fields=fields, height=height),
            [(reach * fields, width)] * 2,
            [
                (2 * reach + 1,) + line,
                (2 * reach,) + line,
                (2 * reach,) + line,
                (lane_tiles, SUB * reach, LANES),
                (reach,) + line,
                (reach,) + line,
            ],
            grid=(n,),
            in_specs=[
                pl.BlockSpec((per, fields, reach, width), lambda i: (i, 0, 0, 0)),
                shifted,
                shifted,
                pl.BlockSpec((reach,) + line, lambda i: (0, 0, 0)),
                pl.BlockSpec(rates.shape, whole),
                pl.BlockSpec(order.shape, whole),
            ],
            out_specs=(pl.BlockSpec((reach * fields, width), whole),) * 2,
            limit=8,
            name="cross",
        )(far_members[k], near_members, beyond, far_coarse, rates, order)
        nears.append(near)
        fars.append(far)

    total, below = call(
        functools.partial(gather_parts, groups=len(groups), fields=fields),
        [(height * fields, width), ((reach + 2) * fields, width)],
        name="gather_parts",
    )(own_sum, *nears, *fars)
    from_above = lax.ppermute(below, "tile", downward)
    high = (height + 4) * fields
    sums = call(
        functools.partial(pack_sums, count=count, fields=fields),
        [(high + SUB, breadth)] * count,
        [(high, width), (lane_tiles + 2, high, LANES)],
        name="pack_sums",
    )(total, below, from_above, edge, order)
    arrived = [sums[0]] + [lax.ppermute(sums[d], "mem", rings[d]) for d in range(1, count)]
    (hybrid,) = call(
        functools.partial(finish, count=count, fields=fields),
        [(fields, rows, cols)],
        [(3, high, LANES), (2, fields * rows, breadth)],
        name="finish",
    )(*arrived, static, table)
    return hybrid


def solution(mesh):
    return jax.shard_map(
        local,
        mesh=mesh,
        in_specs=(
            P(None, "tile", "mem"),
            P(None, "tile", "mem"),
            P(),
            P(None, "tile", "mem"),
            P(None, "tile", "mem"),
            P("mem", None, "tile", None),
            P("tile", None),
        ),
        out_specs=P(None, "tile", "mem"),
        check_vma=False,
    )
```

```python
import functools

import jax
import jax.numpy as jnp
from jax import lax
from jax.experimental import pallas as pl
from jax.experimental.pallas import tpu as pltpu
from jax.sharding import PartitionSpec as P


STATIC_PASSES = 4
SPREAD_PASSES = 8
LANES = 128
SUB = 8
VMEM_BYTES = 67043328


F32 = jnp.float32
EXACT = lax.Precision.HIGHEST


def call(kernel, out_shapes, scratch=(), limit=4, **kw):
    return pl.pallas_call(
        kernel,
        out_shape=tuple(jax.ShapeDtypeStruct(s, F32) for s in out_shapes),
        scratch_shapes=[pltpu.VMEM(s, F32) if isinstance(s, tuple) else s for s in scratch],
        compiler_params=pltpu.CompilerParams(vmem_limit_bytes=int(limit * (1 << 20))),
        **kw,
    )


def pack_tile(*refs):
    sources, (up, down, kept), held, done = refs[:5], refs[5:8], refs[8:13], refs[13]
    copies = [
        pltpu.make_async_copy(source, target, done.at[k])
        for k, (source, target) in enumerate(zip(sources, held))
    ]
    for copy in copies:
        copy.start()
    for copy in copies:
        copy.wait()
    grad, scale, index, weight, rate = held
    fields, rows, cols = grad.shape
    slots, height, breadth = index.shape
    parts = rate.shape[1] // cols
    reach = SPREAD_PASSES
    up[...] = jnp.zeros(up.shape, F32)
    down[...] = jnp.zeros(down.shape, F32)
    for f in range(fields):
        top = 2 * reach + 1
        up[f * 24 : f * 24 + top, :] = grad[f, 0:top, :]
        up[f * 24 + top : f * 24 + top + STATIC_PASSES, :] = (
            scale[f, 0:STATIC_PASSES, :] * grad[f, 0:STATIC_PASSES, :]
        )
        down[f * 8 : f * 8 + 1, :] = grad[f, rows - 1 : rows, :]
        down[f * 8 + 1 : f * 8 + 1 + STATIC_PASSES, :] = (
            scale[f, rows - STATIC_PASSES : rows, :] * grad[f, rows - STATIC_PASSES : rows, :]
        )
    base = fields * 24
    low = fields * 8
    for s in range(slots):
        up[base + s * 8 : base + s * 8 + 8, 0:breadth] = index[s, 0:8, :].astype(F32)
        up[base + s * 8 : base + s * 8 + 8, breadth:] = weight[s, 0:8, :]
        down[low + s : low + s + 1, 0:breadth] = index[s, height - 1 : height, :].astype(F32)
        down[low + s : low + s + 1, breadth:] = weight[s, height - 1 : height, :]
    base += slots * 8
    low += slots
    for p in range(parts):
        part = slice(p * cols, (p + 1) * cols)
        up[base + p * 8 : base + p * 8 + 8, :] = rate[0:8, part]
        down[low + p * 4 : low + p * 4 + 4, :] = rate[height - 4 : height, part]
        kept[(slots + p) * height : (slots + p + 1) * height, :] = rate[:, part]
    for s in range(slots):
        kept[s * height : (s + 1) * height, 0:breadth] = index[s].astype(F32)
        kept[s * height : (s + 1) * height, breadth:] = weight[s]


def lane_iota(shape):
    return lax.broadcasted_iota(jnp.int32, shape, len(shape) - 1)


def pick_columns(cols):
    source = lax.broadcasted_iota(jnp.int32, (cols, cols), 0)
    target = lax.broadcasted_iota(jnp.int32, (cols, cols), 1)
    half = cols // 2
    wanted = jnp.where(target < half, 2 * target, 2 * (target - half) + 1)
    return jnp.where(source == wanted, 1.0, 0.0).astype(F32)


def spread_columns(cols):
    source = lax.broadcasted_iota(jnp.int32, (cols, cols), 0)
    target = lax.broadcasted_iota(jnp.int32, (cols, cols), 1)
    half = cols // 2
    wanted = jnp.where(source < half, 2 * source, 2 * (source - half) + 1)
    return jnp.where(target == wanted, 1.0, 0.0).astype(F32)


def table_rows(index, weight):
    rows = []
    for o in range(16):
        total = jnp.zeros(index[0].shape, F32)
        for i, w in zip(index, weight):
            total = total + jnp.where(i == float(o), w, 0.0)
        rows.append(total)
    return rows


def slots_of(kept, height, breadth, slots):
    rows = [slice(s * height, (s + 1) * height) for s in range(slots)]
    return [kept[r, 0:breadth] for r in rows], [kept[r, breadth:] for r in rows]


def restrict(grad, scale, kept, up, down, out, rate_out, ext, cols4, edge, *, slots):
    fields, rows, cols = grad.shape
    height, breadth = rows // 2, cols // 2
    parts = kept.shape[0] // height - slots
    index, weight = slots_of(kept, height, breadth, slots)
    n = STATIC_PASSES
    top = 2 * SPREAD_PASSES + 1
    tall = height + SPREAD_PASSES
    base = fields * 24
    low = fields * 8
    table = table_rows(
        [
            jnp.concatenate(
                [index[s], up[base + s * 8 : base + s * 8 + 8, 0:breadth]], axis=0
            )
            for s in range(slots)
        ],
        [
            jnp.concatenate([weight[s], up[base + s * 8 : base + s * 8 + 8, breadth:]], axis=0)
            for s in range(slots)
        ],
    )
    pick = pick_columns(cols)
    ext[...] = jnp.zeros(ext.shape, F32)
    edge[...] = jnp.zeros(edge.shape, F32)
    lane = lane_iota((ext.shape[0], breadth))
    for f in range(fields):
        ext[8 : 8 + rows, :] = grad[f]
        ext[7:8, :] = down[f * 8 : f * 8 + 1, :]
        ext[8 + rows : 8 + rows + top, :] = up[f * 24 : f * 24 + top, :]
        edge[:, 16 + f : 17 + f] = ext[:, 0:1]
        edge[:, 80 + f : 81 + f] = ext[:, cols - 1 : cols]
        both = jnp.dot(ext[...], pick, precision=EXACT, preferred_element_type=F32)
        even = both[:, :breadth]
        odd = both[:, breadth:]
        cols4[0] = jnp.where(lane == 0, 0.0, pltpu.roll(odd, 1, 1))
        cols4[1] = even
        cols4[2] = odd
        cols4[3] = jnp.where(lane == breadth - 1, 0.0, pltpu.roll(even, breadth - 1, 1))
        total = jnp.zeros((tall, breadth), F32)
        for a in range(4):
            for b in range(4):
                total = total + table[4 * a + b] * cols4[b, pl.ds(a + 7, tall, stride=2), :]
        out[f * tall : (f + 1) * tall, :] = total
    for at, wide, lone in ((0, 0, 0), (64, cols - n, breadth - 1)):
        for f in range(fields):
            lanes = slice(at + 4 * f, at + 4 * f + n)
            columns = slice(wide, wide + n)
            edge[8 : 8 + rows, lanes] = scale[f, :, columns] * grad[f, :, columns]
            edge[8 - n : 8, lanes] = down[f * 8 + 1 : f * 8 + 1 + n, columns]
            edge[8 + rows : 8 + rows + n, lanes] = up[f * 24 + top : f * 24 + top + n, columns]
        one = slice(lone, lone + 1)
        second = slice(breadth + lone, breadth + lone + 1)
        for s in range(slots):
            lanes = slice(at + 32 + s, at + 33 + s)
            edge[8 : 8 + height, lanes] = index[s][:, one]
            edge[7:8, lanes] = down[low + s : low + s + 1, one]
            edge[8 + height : 9 + height, lanes] = up[base + s * 8 : base + s * 8 + 1, one]
            lanes = slice(at + 36 + s, at + 37 + s)
            edge[8 : 8 + height, lanes] = weight[s][:, one]
            edge[7:8, lanes] = down[low + s : low + s + 1, second]
            edge[8 + height : 9 + height, lanes] = up[base + s * 8 : base + s * 8 + 1, second]
        for a in range(4):
            entry = table[4 * a] if at == 0 else table[4 * a + 3]
            edge[8 : 8 + tall, at + 40 + a : at + 41 + a] = entry[:, one]
    out[fields * tall :, :] = edge[...]
    base = fields * 24 + slots * 8
    low = fields * 8 + slots
    rate_out[0:4, :] = jnp.zeros((4, rate_out.shape[1]), F32)
    for p in range(parts):
        part = slice(p * cols, (p + 1) * cols)
        rate_out[8 : 8 + height, part] = kept[(slots + p) * height : (slots + p + 1) * height, :]
        rate_out[4:8, part] = down[low + p * 4 : low + p * 4 + 4, :]
        rate_out[8 + height : 16 + height, part] = up[base + p * 8 : base + p * 8 + 8, :]


def side(grad, scale, stat_rate, kept, up, down, west_message, east_message,
         static, table_out, box, idx, wgt, tab, *, members_all):
    fields, rows, cols = grad.shape
    slots, (height, breadth) = idx.shape[0], table_out.shape[1:]
    index, weight = slots_of(kept, height, breadth, slots)
    n = STATIC_PASSES
    top = 2 * SPREAD_PASSES + 1
    me = lax.axis_index("mem")
    skip = fields * (height + SPREAD_PASSES)
    from_west = jnp.where(me > 0, pltpu.roll(west_message[skip:, :], 64, 1), 0.0)
    from_east = jnp.where(me < lax.axis_size("mem") - 1, east_message[skip:, :], 0.0)
    wide = cols + 2 * LANES
    shape = (rows + 16, wide)
    row = lax.broadcasted_iota(jnp.int32, shape, 0)
    col = lane_iota(shape)
    first_row = jnp.where(lax.axis_index("tile") == 0, 8, 0)
    last_row = jnp.where(lax.axis_index("tile") == lax.axis_size("tile") - 1, 8 + rows, rows + 16)
    first_col = jnp.where(lax.axis_index("mem") == 0, LANES, 0)
    last_col = jnp.where(lax.axis_index("mem") == lax.axis_size("mem") - 1, LANES + cols, wide)
    inside = (row >= first_row) & (row < last_row) & (col >= first_col) & (col < last_col)
    for f in range(fields):
        box[...] = jnp.zeros(box.shape, F32)
        box[8 : 8 + rows, LANES : LANES + cols] = scale[f] * grad[f]
        box[8 - n : 8, LANES : LANES + cols] = down[f * 8 + 1 : f * 8 + 1 + n, :]
        box[8 + rows : 8 + rows + n, LANES : LANES + cols] = up[f * 24 + top : f * 24 + top + n, :]
        box[:, LANES - n : LANES] = from_west[0 : rows + 16, 4 * f : 4 * f + n]
        box[:, LANES + cols : LANES + cols + n] = from_east[0 : rows + 16, 4 * f : 4 * f + n]
        field = box[...]
        rate = jnp.where(inside, stat_rate[f], 0.0)
        for _ in range(n):
            beside = (
                pltpu.roll(field, 1, 0)
                + pltpu.roll(field, rows + 15, 0)
                + pltpu.roll(field, 1, 1)
                + pltpu.roll(field, wide - 1, 1)
            )
            field = field + rate * (beside - 4.0 * field)
        static[f] = 0.3 * scale[f] * field[8 : 8 + rows, LANES : LANES + cols]
    factor = 2.8 / (members_all - 1)
    base = fields * 24
    low = fields * 8
    tall = height + 16
    lane = lane_iota((tall, breadth))
    for s in range(slots):
        idx[s] = jnp.zeros((tall, breadth), F32)
        wgt[s] = jnp.zeros((tall, breadth), F32)
        idx[s, 8 : 8 + height, :] = index[s]
        wgt[s, 8 : 8 + height, :] = weight[s]
        idx[s, 7:8, :] = down[low + s : low + s + 1, 0:breadth]
        wgt[s, 7:8, :] = down[low + s : low + s + 1, breadth:]
        idx[s, 8 + height : 9 + height, :] = up[base + s * 8 : base + s * 8 + 1, 0:breadth]
        wgt[s, 8 + height : 9 + height, :] = up[base + s * 8 : base + s * 8 + 1, breadth:]
    west = from_west[0:tall, :]
    east = from_east[0:tall, :]

    def shifted(x, shift, at):
        if shift == 1:
            return jnp.where(lane == 0, pltpu.roll(west, LANES - at, 1), pltpu.roll(x, 1, 1))
        if shift == 2:
            return jnp.where(
                lane == breadth - 1,
                pltpu.roll(east, LANES - 1 - at, 1),
                pltpu.roll(x, breadth - 1, 1),
            )
        return x

    for shift, columns in ((0, (1, 2)), (1, (3,)), (2, (0,))):
        table = table_rows(
            [shifted(idx[s], shift, 32 + s) for s in range(slots)],
            [shifted(wgt[s], shift, 36 + s) for s in range(slots)],
        )
        for b in columns:
            for a in range(4):
                off = (1, 0, 0, -1)[a]
                tab[...] = factor * table[4 * a + b]
                table_out[4 * a + b] = tab[8 + off : 8 + off + height, :]


def parts_of(width):
    return [slice(t, t + LANES) for t in range(0, width, LANES)]


def sweep(v, keep, rate, lo, hi, v_at, rate_at):
    parts = parts_of(v.shape[2])
    lane = lane_iota((SUB, LANES))

    def right_below(here, below):
        right = jnp.where(lane == LANES - 1, 0.0, pltpu.roll(here[0], LANES - 1, 1))
        return [x + y for x, y in zip(here[1:] + [right], below)]

    above = [v[lo - 1 + v_at, :, p] for p in parts]
    here = [v[lo + v_at, :, p] for p in parts]
    after = right_below(above, here)
    for r in range(lo, hi):
        below = [v[r + 1 + v_at, :, p] for p in parts]
        first = jnp.where(lane == 0, above[0], pltpu.roll(after[-1], 1, 1))
        before = [first] + after[:-1]
        after = right_below(here, below)
        for t, p in enumerate(parts):
            total = before[t] + after[t]
            v[r + v_at, :, p] = keep[r + rate_at, :, p] * here[t] + rate[r + rate_at, :, p] * total
        above, here = here, below


def permutation(width):
    source = lax.broadcasted_iota(jnp.int32, (width, width), 0)
    target = lax.broadcasted_iota(jnp.int32, (width, width), 1)
    tiles = width // LANES
    return jnp.where(source == tiles * (target % LANES) + target // LANES, 1.0, 0.0).astype(
        jnp.bfloat16
    )


def reorder(x, order, contract=0):
    dims = (((1,), (contract,)), ((), ()))
    high = x.astype(jnp.bfloat16)
    rest = x - high.astype(F32)
    middle = rest.astype(jnp.bfloat16)
    low = (rest - middle.astype(F32)).astype(jnp.bfloat16)
    moved = [
        lax.dot_general(y, order, dims, preferred_element_type=F32) for y in (high, middle, low)
    ]
    return moved[0] + (moved[1] + moved[2])


def fill_rates(rate_ref, keep, rate, rows, at):
    for r in range(rows):
        line = jnp.broadcast_to(rate_ref[r + at : r + at + 1, :], rate.shape[1:])
        rate[r] = line
        keep[r] = 1.0 - 4.0 * line


def fold(total, fields):
    folded = total[0:fields]
    for j in range(fields, SUB, fields):
        folded = folded + total[j : j + fields]
    return folded


def own(*refs, count, fields, pairs, last):
    members, rate_ref, order = refs[0:3]
    pieces = refs[3 : 3 + count]
    own_out, beyond, near_members, far_coarse, rates_out, message = refs[3 + count : 9 + count]
    v, m, keep, rate, c, cw, cp, mw, acc, eb = refs[9 + count :]
    height = m.shape[0]
    reach = SPREAD_PASSES
    tall = height + reach
    per = members.shape[0] // pairs
    parts = parts_of(v.shape[2])

    rates_out[...] = reorder(rate_ref[...], order[...])
    fill_rates(rates_out, keep, rate, height + 12, 4)
    me = lax.axis_index("mem")
    for d, piece in enumerate(pieces):
        breadth = piece.shape[1]
        where = lax.rem(me - d + count, count)
        at = pl.ds(pl.multiple_of(where * breadth, LANES), breadth)
        cw[:, at] = piece[0 : fields * tall, :]
        eb[where] = piece[fields * tall :, :]
    lane = lane_iota((tall, LANES))
    for q in range(count - 1):
        last_column = (q + 1) * breadth - 1
        for mine, other, table_at, grad_at, goal in (
            (q, q + 1, 104, 16, last_column),
            (q + 1, q, 40, 80, last_column + 1),
        ):
            added = jnp.zeros((tall, LANES), F32)
            for a in range(4):
                entry = eb[mine, 8 : 8 + tall, table_at + a : table_at + a + 1]
                added = added + entry * eb[other, pl.ds(a + 7, tall, stride=2), :]
            begin = goal // LANES * LANES
            for f in range(fields):
                turn = (goal - begin - grad_at - f) % LANES
                here = jnp.where(lane == goal - begin, pltpu.roll(added, turn, 1), 0.0)
                rows = slice(f * tall, (f + 1) * tall)
                cw[rows, begin : begin + LANES] = cw[rows, begin : begin + LANES] + here
    moved = reorder(cw[...], order[...])
    for t, p in enumerate(parts):
        cp[t] = moved[:, p]
        for r in range(tall):
            row = cp[t, pl.ds(r, fields, stride=tall), :]
            for j in range(0, SUB, fields):
                if r < height:
                    c[r, j : j + fields, p] = row
                else:
                    far_coarse[r - height, j : j + fields, p] = row
    acc[...] = jnp.zeros(acc.shape, F32)
    off = 5

    def one(i, _):
        v[0:off] = jnp.zeros((off,) + v.shape[1:], F32)
        v[height + off :] = jnp.zeros((v.shape[0] - height - off,) + v.shape[1:], F32)
        block = members[pl.ds(i * per, per)].reshape(mw.shape[1], v.shape[2])
        moved = jnp.dot(block, order[...], preferred_element_type=F32)
        for t, p in enumerate(parts):
            mw[t] = moved[:, p]
            for r in range(height):
                line = mw[t, pl.ds(r, SUB, stride=height), :]
                m[r, :, p] = line
                v[r + off, :, p] = line * c[r, :, p]
        for s in range(1, SPREAD_PASSES + 1):
            sweep(v, keep, rate, -min(s, SPREAD_PASSES - s), height + s, off, 4)
        for r in range(height):
            acc[r] = acc[r] + m[r] * v[r + off]
        for r in range(reach):
            beyond[i, r] = v[r + height + off]
            near_members[i, r] = m[height - reach + r]
        return _

    lax.fori_loop(0, pairs, one, 0)
    for r in range(height):
        own_out[r * fields : (r + 1) * fields, :] = fold(acc[r], fields)
    two = 2 * fields
    message[0:two, :] = own_out[0:two, :]
    rows = SUB * reach
    for j in range(last):
        at = (pairs - last + j) * per
        block = members[at : at + per, :, 0:reach, :].astype(F32)
        message[two + j * rows : two + (j + 1) * rows, :] = block.reshape(rows, v.shape[2])


def cross(far_rows, near_members, beyond, far_coarse, rates, order, near_out, far_out,
          w, keep, rate, fw, near, far, *, fields, height, begin, number, skip):
    reach = SPREAD_PASSES
    parts = parts_of(w.shape[2])
    fill_rates(rates, keep, rate, 2 * reach, height)
    near[...] = jnp.zeros(near.shape, F32)
    far[...] = jnp.zeros(far.shape, F32)
    size = fw.shape[1]

    def one(i, _):
        w[0 : reach + 1] = jnp.zeros((reach + 1,) + w.shape[1:], F32)
        at = pl.multiple_of(skip + i * size, SUB)
        block = far_rows[pl.ds(at, size), :].astype(jnp.bfloat16)
        moved = jnp.dot(block, order[...], preferred_element_type=F32)
        for t, p in enumerate(parts):
            fw[t] = moved[:, p]
            for r in range(reach):
                line = fw[t, pl.ds(r, SUB, stride=reach), :]
                w[r + reach + 1, :, p] = line * far_coarse[r, :, p]
                far[r, :, p] = far[r, :, p] + line * beyond[begin + i, r, :, p]
        for s in range(1, SPREAD_PASSES + 1):
            sweep(w, keep, rate, height - s, height - s + reach, reach + 1 - height, reach - height)
        for r in range(reach):
            near[r] = near[r] + near_members[begin + i, r] * w[r + 1]
        return _

    lax.fori_loop(0, number, one, 0)
    for r in range(reach):
        near_out[r * fields : (r + 1) * fields, :] = fold(near[r], fields)
        far_out[r * fields : (r + 1) * fields, :] = fold(far[r], fields)


def gather_parts(*refs, groups, fields):
    own_ref = refs[0]
    nears = refs[1 : 1 + groups]
    fars = refs[1 + groups : 1 + 2 * groups]
    total_out, below_out = refs[1 + 2 * groups :]
    rows = own_ref.shape[0]
    reach = SPREAD_PASSES * fields
    near = nears[0][...]
    far = fars[0][...]
    for x, y in zip(nears[1:], fars[1:]):
        near = near + x[...]
        far = far + y[...]
    near = near + own_ref[rows - reach : rows, :]
    total_out[0 : rows - reach, :] = own_ref[0 : rows - reach, :]
    total_out[rows - reach : rows, :] = near
    below_out[0:fields, :] = jnp.zeros((fields, near.shape[1]), F32)
    below_out[fields : 2 * fields, :] = near[reach - fields : reach, :]
    below_out[2 * fields :, :] = far


def pack_sums(total, below, from_above, from_below, order, *refs, count, fields):
    outs, moved_in, held = refs[:-2], refs[-2], refs[-1]
    rows = total.shape[0]
    tall = held.shape[1]
    two = 2 * fields
    tiles = held.shape[0] - 2
    held[0] = jnp.zeros(held.shape[1:], F32)
    held[tiles + 1] = jnp.zeros(held.shape[1:], F32)
    reach = from_above.shape[0]
    moved_in[0:two, :] = from_above[0:two, :]
    moved_in[two:reach, :] = from_above[two:reach, :] + total[0 : reach - two, :]
    moved_in[reach : rows + two, :] = total[reach - two : rows, :]
    moved_in[rows + two : tall, :] = below[two : 2 * two, :] + from_below[0:two, :]
    natural = reorder(moved_in[...], order[...], 1)
    for t, p in enumerate(parts_of(total.shape[1])):
        held[t + 1] = natural[:, p]
    me = lax.axis_index("mem")
    lane = lane_iota((SUB, LANES))
    width = tiles // count
    for d in range(count):
        at = lax.rem(me + d, count) * width
        packed = jnp.zeros((SUB, LANES), F32)
        for w in range(width):
            outs[d][0:tall, w * LANES : (w + 1) * LANES] = held[at + 1 + w]
        for k in range(tall // SUB):
            rows8 = slice(k * SUB, (k + 1) * SUB)
            edge = jnp.where(lane == 0, held[at + 1 + width, rows8, :], held[at, rows8, :])
            edge = pltpu.roll(edge, 2 * k + 1, 1)
            packed = jnp.where((lane == 2 * k) | (lane == 2 * k + 1), edge, packed)
        outs[d][tall : tall + SUB, 0:LANES] = packed


def finish(*refs, count, fields):
    pieces = refs[:count]
    static, table, out, held, wide = refs[count:]
    height = table.shape[1]
    rows, cols = out.shape[1:]
    breadth = table.shape[2]
    tall = held.shape[1]
    total = pieces[0][...]
    for piece in pieces[1:]:
        total = total + piece[...]
    packed = total[tall:, :]
    lane = lane_iota((SUB, LANES))
    for k in range(tall // SUB):
        x = total[k * SUB : (k + 1) * SUB, :]
        rows8 = slice(k * SUB, (k + 1) * SUB)
        held[0, rows8, :] = x
        left = pltpu.roll(packed, LANES - 2 * k, 1) if k else packed
        right = pltpu.roll(packed, LANES - 2 - 2 * k, 1)
        held[1, rows8, :] = jnp.where(lane == 0, left, pltpu.roll(x, 1, 1))
        held[2, rows8, :] = jnp.where(lane == LANES - 1, right, pltpu.roll(x, LANES - 1, 1))
    for f in range(fields):
        for p in range(2):
            even = jnp.zeros((height, breadth), F32)
            odd = jnp.zeros((height, breadth), F32)
            for a, off in ((1 + p, 0), (3 - 3 * p, 2 * p - 1)):
                at = pl.ds(f + fields * (2 + off), height, stride=fields)
                here = held[0, at, :]
                even = even + table[4 * a + 1] * here + table[4 * a + 3] * held[1, at, :]
                odd = odd + table[4 * a + 2] * here + table[4 * a] * held[2, at, :]
            at = pl.ds(f * rows + p, height, stride=2)
            wide[0, at, :] = even
            wide[1, at, :] = odd
    both = jnp.concatenate([wide[0], wide[1]], axis=1)
    fine = jnp.dot(both, spread_columns(cols), precision=EXACT, preferred_element_type=F32)
    for f in range(fields):
        out[f] = static[f] + fine[f * rows : (f + 1) * rows, :]


def groups_of(pairs):
    sizes = [max(1, pairs // 5), max(1, 2 * pairs // 5)]
    sizes += [max(1, pairs - sum(sizes) - 1), 1]
    return [(sum(sizes[:g]), size) for g, size in enumerate(sizes)]


def local(gradient, static_scale, static_rate, interp_index, interp_weight, members, spread_rate):
    fields, rows, cols = gradient.shape
    slots, height, breadth = interp_index.shape
    member_count, _, _, width = members.shape
    reach = SPREAD_PASSES
    tiles = lax.axis_size("tile")
    count = lax.axis_size("mem")
    upward = [(i + 1, i) for i in range(tiles - 1)]
    downward = [(i, i + 1) for i in range(tiles - 1)]
    rings = [[(i, (i + d) % count) for i in range(count)] for d in range(count)]
    per = SUB // fields
    pairs = member_count // per
    vmem = pl.BlockSpec(memory_space=pltpu.VMEM)
    smem = pl.BlockSpec(memory_space=pltpu.SMEM)
    smalls = (gradient, static_scale, interp_index, interp_weight, spread_rate)
    column_parts = width // cols
    order = permutation(width)

    groups = groups_of(pairs)
    last = groups[-1][1]
    far_rows = [
        lax.ppermute(
            members[per * g : per * (g + n), :, 0:reach, :]
            .astype(F32)
            .reshape(n * SUB * reach, width),
            "tile",
            upward,
        )
        for g, n in groups[:-1]
    ]

    up, down, kept = call(
        pack_tile,
        [
            (fields * 24 + slots * 8 + column_parts * 8, cols),
            (fields * 8 + (slots + column_parts * 4 + 7) // 8 * 8, cols),
            ((slots + column_parts) * height, cols),
        ],
        [pltpu.VMEM(x.shape, x.dtype) for x in smalls] + [pltpu.SemaphoreType.DMA((5,))],
        in_specs=[pl.BlockSpec(memory_space=pltpu.HBM)] * 5,
        limit=VMEM_BYTES / (1 << 20),
        name="pack_tile",
    )(*smalls)
    up = lax.ppermute(up, "tile", upward)
    down = lax.ppermute(down, "tile", downward)

    tall = height + reach
    quarter, rates = call(
        functools.partial(restrict, slots=slots),
        [(fields * tall + 64, breadth), (height + 16, width)],
        [(64, cols), (4, 64, breadth), (64, LANES)],
        name="restrict",
    )(gradient, static_scale, kept, up, down)
    pieces = [quarter] + [lax.ppermute(quarter, "mem", rings[d]) for d in range(1, count)]

    static, table = call(
        functools.partial(side, members_all=member_count * count),
        [(fields, rows, cols), (16, height, breadth)],
        [
            (rows + 16, cols + 2 * LANES),
            (slots, height + 16, breadth),
            (slots, height + 16, breadth),
            (height + 16, breadth),
        ],
        in_specs=[vmem, vmem, smem] + [vmem] * 5,
        name="side",
    )(gradient, static_scale, static_rate, kept, up, down, pieces[1], pieces[-1])

    line = (SUB, width)
    lane_tiles = width // LANES
    two = 2 * fields
    own_sum, beyond, near_members, far_coarse, rates, message = call(
        functools.partial(own, count=count, fields=fields, pairs=pairs, last=last),
        [
            (height * fields, width),
            (pairs, reach) + line,
            (pairs, reach) + line,
            (reach,) + line,
            rates.shape,
            (two + last * SUB * reach, width),
        ],
        [
            (height + reach + 6,) + line,
            (height,) + line,
            (height + 12,) + line,
            (height + 12,) + line,
            (height,) + line,
            (fields * tall, width),
            (lane_tiles, fields * tall, LANES),
            (lane_tiles, SUB * height, LANES),
            (height,) + line,
            (count, 64, LANES),
        ],
        limit=8,
        name="own",
    )(members, rates, order, *pieces)
    message = lax.ppermute(message, "tile", upward)
    far_rows.append(message)

    nears, fars = [], []
    for k, (g, n) in enumerate(groups):
        near, far = call(
            functools.partial(
                cross,
                fields=fields,
                height=height,
                begin=g,
                number=n,
                skip=two if k == len(groups) - 1 else 0,
            ),
            [(reach * fields, width)] * 2,
            [
                (2 * reach + 1,) + line,
                (2 * reach,) + line,
                (2 * reach,) + line,
                (lane_tiles, SUB * reach, LANES),
                (reach,) + line,
                (reach,) + line,
            ],
            limit=4,
            name="cross",
        )(far_rows[k], near_members, beyond, far_coarse, rates, order)
        nears.append(near)
        fars.append(far)

    total, below = call(
        functools.partial(gather_parts, groups=len(groups), fields=fields),
        [(height * fields, width), ((reach + 2) * fields, width)],
        name="gather_parts",
    )(own_sum, *nears, *fars)
    from_above = lax.ppermute(below, "tile", downward)
    high = (height + 4) * fields
    sums = call(
        functools.partial(pack_sums, count=count, fields=fields),
        [(high + SUB, breadth)] * count,
        [(high, width), (lane_tiles + 2, high, LANES)],
        name="pack_sums",
    )(total, below, from_above, message, order)
    arrived = [sums[0]] + [lax.ppermute(sums[d], "mem", rings[d]) for d in range(1, count)]
    (hybrid,) = call(
        functools.partial(finish, count=count, fields=fields),
        [(fields, rows, cols)],
        [(3, high, LANES), (2, fields * rows, breadth)],
        name="finish",
    )(*arrived, static, table)
    return hybrid


def solution(mesh):
    return jax.shard_map(
        local,
        mesh=mesh,
        in_specs=(
            P(None, "tile", "mem"),
            P(None, "tile", "mem"),
            P(),
            P(None, "tile", "mem"),
            P(None, "tile", "mem"),
            P("mem", None, "tile", None),
            P("tile", None),
        ),
        out_specs=P(None, "tile", "mem"),
        check_vma=False,
    )
```

```python
import functools

import jax
import jax.numpy as jnp
from jax import lax
from jax.experimental import pallas as pl
from jax.experimental.pallas import tpu as pltpu
from jax.sharding import PartitionSpec as P


STATIC_PASSES = 4
SPREAD_PASSES = 8
LANES = 128
SUB = 8
VMEM_BYTES = 67043328


F32 = jnp.float32
EXACT = lax.Precision.HIGHEST


def call(kernel, out_shapes, scratch=(), limit=4, **kw):
    return pl.pallas_call(
        kernel,
        out_shape=tuple(jax.ShapeDtypeStruct(s, F32) for s in out_shapes),
        scratch_shapes=[pltpu.VMEM(s, F32) if isinstance(s, tuple) else s for s in scratch],
        compiler_params=pltpu.CompilerParams(vmem_limit_bytes=int(limit * (1 << 20))),
        **kw,
    )


def pack_tile(*refs):
    sources, (up, down, kept, first), held, done = refs[:6], refs[6:10], refs[10:16], refs[16]
    number = held[5].shape[0]
    sources = sources[:5] + (sources[5].at[0:number],)
    copies = [
        pltpu.make_async_copy(source, target, done.at[k])
        for k, (source, target) in enumerate(zip(sources, held))
    ]
    for copy in copies:
        copy.start()
    for copy in copies:
        copy.wait()
    grad, scale, index, weight, rate, members = held
    first[...] = members[:, :, 0:SPREAD_PASSES, :].astype(F32).reshape(first.shape)
    fields, rows, cols = grad.shape
    slots, height, breadth = index.shape
    parts = rate.shape[1] // cols
    reach = SPREAD_PASSES
    up[...] = jnp.zeros(up.shape, F32)
    down[...] = jnp.zeros(down.shape, F32)
    for f in range(fields):
        top = 2 * reach + 1
        up[f * 24 : f * 24 + top, :] = grad[f, 0:top, :]
        up[f * 24 + top : f * 24 + top + STATIC_PASSES, :] = (
            scale[f, 0:STATIC_PASSES, :] * grad[f, 0:STATIC_PASSES, :]
        )
        down[f * 8 : f * 8 + 1, :] = grad[f, rows - 1 : rows, :]
        down[f * 8 + 1 : f * 8 + 1 + STATIC_PASSES, :] = (
            scale[f, rows - STATIC_PASSES : rows, :] * grad[f, rows - STATIC_PASSES : rows, :]
        )
    base = fields * 24
    low = fields * 8
    for s in range(slots):
        up[base + s * 8 : base + s * 8 + 8, 0:breadth] = index[s, 0:8, :].astype(F32)
        up[base + s * 8 : base + s * 8 + 8, breadth:] = weight[s, 0:8, :]
        down[low + s : low + s + 1, 0:breadth] = index[s, height - 1 : height, :].astype(F32)
        down[low + s : low + s + 1, breadth:] = weight[s, height - 1 : height, :]
    base += slots * 8
    low += slots
    for p in range(parts):
        part = slice(p * cols, (p + 1) * cols)
        up[base + p * 8 : base + p * 8 + 8, :] = rate[0:8, part]
        down[low + p * 4 : low + p * 4 + 4, :] = rate[height - 4 : height, part]
        kept[(slots + p) * height : (slots + p + 1) * height, :] = rate[:, part]
    for s in range(slots):
        kept[s * height : (s + 1) * height, 0:breadth] = index[s].astype(F32)
        kept[s * height : (s + 1) * height, breadth:] = weight[s]


def lane_iota(shape):
    return lax.broadcasted_iota(jnp.int32, shape, len(shape) - 1)


def pick_columns(cols):
    source = lax.broadcasted_iota(jnp.int32, (cols, cols), 0)
    target = lax.broadcasted_iota(jnp.int32, (cols, cols), 1)
    half = cols // 2
    wanted = jnp.where(target < half, 2 * target, 2 * (target - half) + 1)
    return jnp.where(source == wanted, 1.0, 0.0).astype(F32)


def spread_columns(cols):
    source = lax.broadcasted_iota(jnp.int32, (cols, cols), 0)
    target = lax.broadcasted_iota(jnp.int32, (cols, cols), 1)
    half = cols // 2
    wanted = jnp.where(source < half, 2 * source, 2 * (source - half) + 1)
    return jnp.where(target == wanted, 1.0, 0.0).astype(F32)


def table_rows(index, weight):
    rows = []
    for o in range(16):
        total = jnp.zeros(index[0].shape, F32)
        for i, w in zip(index, weight):
            total = total + jnp.where(i == float(o), w, 0.0)
        rows.append(total)
    return rows


def slots_of(kept, height, breadth, slots):
    rows = [slice(s * height, (s + 1) * height) for s in range(slots)]
    return [kept[r, 0:breadth] for r in rows], [kept[r, breadth:] for r in rows]


def restrict(grad, scale, kept, up, down, out, rate_out, ext, cols4, edge, *, slots):
    fields, rows, cols = grad.shape
    height, breadth = rows // 2, cols // 2
    parts = kept.shape[0] // height - slots
    index, weight = slots_of(kept, height, breadth, slots)
    n = STATIC_PASSES
    top = 2 * SPREAD_PASSES + 1
    tall = height + SPREAD_PASSES
    base = fields * 24
    low = fields * 8
    table = table_rows(
        [
            jnp.concatenate(
                [index[s], up[base + s * 8 : base + s * 8 + 8, 0:breadth]], axis=0
            )
            for s in range(slots)
        ],
        [
            jnp.concatenate([weight[s], up[base + s * 8 : base + s * 8 + 8, breadth:]], axis=0)
            for s in range(slots)
        ],
    )
    pick = pick_columns(cols)
    ext[...] = jnp.zeros(ext.shape, F32)
    edge[...] = jnp.zeros(edge.shape, F32)
    lane = lane_iota((ext.shape[0], breadth))
    for f in range(fields):
        ext[8 : 8 + rows, :] = grad[f]
        ext[7:8, :] = down[f * 8 : f * 8 + 1, :]
        ext[8 + rows : 8 + rows + top, :] = up[f * 24 : f * 24 + top, :]
        edge[:, 16 + f : 17 + f] = ext[:, 0:1]
        edge[:, 80 + f : 81 + f] = ext[:, cols - 1 : cols]
        both = jnp.dot(ext[...], pick, precision=EXACT, preferred_element_type=F32)
        even = both[:, :breadth]
        odd = both[:, breadth:]
        cols4[0] = jnp.where(lane == 0, 0.0, pltpu.roll(odd, 1, 1))
        cols4[1] = even
        cols4[2] = odd
        cols4[3] = jnp.where(lane == breadth - 1, 0.0, pltpu.roll(even, breadth - 1, 1))
        total = jnp.zeros((tall, breadth), F32)
        for a in range(4):
            for b in range(4):
                total = total + table[4 * a + b] * cols4[b, pl.ds(a + 7, tall, stride=2), :]
        out[f * tall : (f + 1) * tall, :] = total
    for at, wide, lone in ((0, 0, 0), (64, cols - n, breadth - 1)):
        for f in range(fields):
            lanes = slice(at + 4 * f, at + 4 * f + n)
            columns = slice(wide, wide + n)
            edge[8 : 8 + rows, lanes] = scale[f, :, columns] * grad[f, :, columns]
            edge[8 - n : 8, lanes] = down[f * 8 + 1 : f * 8 + 1 + n, columns]
            edge[8 + rows : 8 + rows + n, lanes] = up[f * 24 + top : f * 24 + top + n, columns]
        one = slice(lone, lone + 1)
        second = slice(breadth + lone, breadth + lone + 1)
        for s in range(slots):
            lanes = slice(at + 32 + s, at + 33 + s)
            edge[8 : 8 + height, lanes] = index[s][:, one]
            edge[7:8, lanes] = down[low + s : low + s + 1, one]
            edge[8 + height : 9 + height, lanes] = up[base + s * 8 : base + s * 8 + 1, one]
            lanes = slice(at + 36 + s, at + 37 + s)
            edge[8 : 8 + height, lanes] = weight[s][:, one]
            edge[7:8, lanes] = down[low + s : low + s + 1, second]
            edge[8 + height : 9 + height, lanes] = up[base + s * 8 : base + s * 8 + 1, second]
        for a in range(4):
            entry = table[4 * a] if at == 0 else table[4 * a + 3]
            edge[8 : 8 + tall, at + 40 + a : at + 41 + a] = entry[:, one]
    out[fields * tall :, :] = edge[...]
    base = fields * 24 + slots * 8
    low = fields * 8 + slots
    rate_out[0:4, :] = jnp.zeros((4, rate_out.shape[1]), F32)
    for p in range(parts):
        part = slice(p * cols, (p + 1) * cols)
        rate_out[8 : 8 + height, part] = kept[(slots + p) * height : (slots + p + 1) * height, :]
        rate_out[4:8, part] = down[low + p * 4 : low + p * 4 + 4, :]
        rate_out[8 + height : 16 + height, part] = up[base + p * 8 : base + p * 8 + 8, :]


def side(grad, scale, stat_rate, kept, up, down, west_message, east_message,
         static, table_out, box, idx, wgt, tab, *, members_all):
    fields, rows, cols = grad.shape
    slots, (height, breadth) = idx.shape[0], table_out.shape[1:]
    index, weight = slots_of(kept, height, breadth, slots)
    n = STATIC_PASSES
    top = 2 * SPREAD_PASSES + 1
    me = lax.axis_index("mem")
    skip = fields * (height + SPREAD_PASSES)
    from_west = jnp.where(me > 0, pltpu.roll(west_message[skip:, :], 64, 1), 0.0)
    from_east = jnp.where(me < lax.axis_size("mem") - 1, east_message[skip:, :], 0.0)
    wide = cols + 2 * LANES
    shape = (rows + 16, wide)
    row = lax.broadcasted_iota(jnp.int32, shape, 0)
    col = lane_iota(shape)
    first_row = jnp.where(lax.axis_index("tile") == 0, 8, 0)
    last_row = jnp.where(lax.axis_index("tile") == lax.axis_size("tile") - 1, 8 + rows, rows + 16)
    first_col = jnp.where(lax.axis_index("mem") == 0, LANES, 0)
    last_col = jnp.where(lax.axis_index("mem") == lax.axis_size("mem") - 1, LANES + cols, wide)
    inside = (row >= first_row) & (row < last_row) & (col >= first_col) & (col < last_col)
    for f in range(fields):
        box[...] = jnp.zeros(box.shape, F32)
        box[8 : 8 + rows, LANES : LANES + cols] = scale[f] * grad[f]
        box[8 - n : 8, LANES : LANES + cols] = down[f * 8 + 1 : f * 8 + 1 + n, :]
        box[8 + rows : 8 + rows + n, LANES : LANES + cols] = up[f * 24 + top : f * 24 + top + n, :]
        box[:, LANES - n : LANES] = from_west[0 : rows + 16, 4 * f : 4 * f + n]
        box[:, LANES + cols : LANES + cols + n] = from_east[0 : rows + 16, 4 * f : 4 * f + n]
        field = box[...]
        rate = jnp.where(inside, stat_rate[f], 0.0)
        for _ in range(n):
            beside = (
                pltpu.roll(field, 1, 0)
                + pltpu.roll(field, rows + 15, 0)
                + pltpu.roll(field, 1, 1)
                + pltpu.roll(field, wide - 1, 1)
            )
            field = field + rate * (beside - 4.0 * field)
        static[f] = 0.3 * scale[f] * field[8 : 8 + rows, LANES : LANES + cols]
    factor = 2.8 / (members_all - 1)
    base = fields * 24
    low = fields * 8
    tall = height + 16
    lane = lane_iota((tall, breadth))
    for s in range(slots):
        idx[s] = jnp.zeros((tall, breadth), F32)
        wgt[s] = jnp.zeros((tall, breadth), F32)
        idx[s, 8 : 8 + height, :] = index[s]
        wgt[s, 8 : 8 + height, :] = weight[s]
        idx[s, 7:8, :] = down[low + s : low + s + 1, 0:breadth]
        wgt[s, 7:8, :] = down[low + s : low + s + 1, breadth:]
        idx[s, 8 + height : 9 + height, :] = up[base + s * 8 : base + s * 8 + 1, 0:breadth]
        wgt[s, 8 + height : 9 + height, :] = up[base + s * 8 : base + s * 8 + 1, breadth:]
    west = from_west[0:tall, :]
    east = from_east[0:tall, :]

    def shifted(x, shift, at):
        if shift == 1:
            return jnp.where(lane == 0, pltpu.roll(west, LANES - at, 1), pltpu.roll(x, 1, 1))
        if shift == 2:
            return jnp.where(
                lane == breadth - 1,
                pltpu.roll(east, LANES - 1 - at, 1),
                pltpu.roll(x, breadth - 1, 1),
            )
        return x

    for shift, columns in ((0, (1, 2)), (1, (3,)), (2, (0,))):
        table = table_rows(
            [shifted(idx[s], shift, 32 + s) for s in range(slots)],
            [shifted(wgt[s], shift, 36 + s) for s in range(slots)],
        )
        for b in columns:
            for a in range(4):
                off = (1, 0, 0, -1)[a]
                tab[...] = factor * table[4 * a + b]
                table_out[4 * a + b] = tab[8 + off : 8 + off + height, :]


def parts_of(width):
    return [slice(t, t + LANES) for t in range(0, width, LANES)]


def sweep(v, keep, rate, lo, hi, v_at, rate_at):
    parts = parts_of(v.shape[2])
    lane = lane_iota((SUB, LANES))

    def right_below(here, below):
        right = jnp.where(lane == LANES - 1, 0.0, pltpu.roll(here[0], LANES - 1, 1))
        return [x + y for x, y in zip(here[1:] + [right], below)]

    above = [v[lo - 1 + v_at, :, p] for p in parts]
    here = [v[lo + v_at, :, p] for p in parts]
    after = right_below(above, here)
    for r in range(lo, hi):
        below = [v[r + 1 + v_at, :, p] for p in parts]
        first = jnp.where(lane == 0, 0.0, pltpu.roll(here[-1], 1, 1)) + above[0]
        before = [first] + after[:-1]
        after = right_below(here, below)
        for t, p in enumerate(parts):
            total = before[t] + after[t]
            v[r + v_at, :, p] = keep[r + rate_at, :, p] * here[t] + rate[r + rate_at, :, p] * total
        above, here = here, below


def climb(rows, keep, rate, lo, rate_at):
    tiles = len(rows[0])
    lane = lane_iota((SUB, LANES))
    parts = parts_of(tiles * LANES)
    result = []
    above = here = after = None
    for k, below in enumerate(rows):
        r = lo + k + rate_at
        if here is None:
            result.append([rate[r, :, p] * x for p, x in zip(parts, below)])
            above, here, after = None, below, list(below)
            continue
        left = jnp.where(lane == 0, 0.0, pltpu.roll(here[-1], 1, 1))
        first = left if above is None else left + above[0]
        before = [first] + after[: tiles - 1] if above is not None else [first] + here[: tiles - 1]
        right = jnp.where(lane == LANES - 1, 0.0, pltpu.roll(here[0], LANES - 1, 1))
        after = [x + y for x, y in zip(here[1:] + [right], below)]
        result.append(
            [
                keep[r, :, p] * here[t] + rate[r, :, p] * (before[t] + after[t])
                for t, p in enumerate(parts)
            ]
        )
        above, here = here, below
    return result


def permutation(width):
    source = lax.broadcasted_iota(jnp.int32, (width, width), 0)
    target = lax.broadcasted_iota(jnp.int32, (width, width), 1)
    tiles = width // LANES
    return jnp.where(source == tiles * (target % LANES) + target // LANES, 1.0, 0.0).astype(
        jnp.bfloat16
    )


def reorder(x, order, contract=0):
    dims = (((1,), (contract,)), ((), ()))
    high = x.astype(jnp.bfloat16)
    rest = x - high.astype(F32)
    middle = rest.astype(jnp.bfloat16)
    low = (rest - middle.astype(F32)).astype(jnp.bfloat16)
    moved = [
        lax.dot_general(y, order, dims, preferred_element_type=F32) for y in (high, middle, low)
    ]
    return moved[0] + (moved[1] + moved[2])


def arrange(members, order, *refs, pairs, groups):
    held, firsts, moved_rows = refs[0], refs[1:-1], refs[-1]
    per = members.shape[0] // pairs
    height, width = members.shape[2:]
    rows = SUB * height
    for b in range(0, pairs, 2):
        n = min(2, pairs - b)
        block = members[b * per : (b + n) * per].reshape(n * rows, width)
        moved = jnp.dot(block, order[...], preferred_element_type=F32)
        for t, p in enumerate(parts_of(width)):
            moved_rows[t, b * rows : (b + n) * rows, :] = moved[:, p]
            for i in range(b, b + n):
                outs = [(out, g) for out, (g, m) in zip(firsts, groups) if g <= i < g + m]
                for r in range(height):
                    line = moved_rows[t, pl.ds(i * rows + r, SUB, stride=height), :]
                    held[i, r, :, p] = line
                    if r < SPREAD_PASSES:
                        for out, g in outs:
                            at = ((i - g) * SPREAD_PASSES + r) * SUB
                            out[at : at + SUB, p] = line


def fill_rates(rate_ref, keep, rate, rows, at):
    for r in range(rows):
        line = jnp.broadcast_to(rate_ref[r + at : r + at + 1, :], rate.shape[1:])
        rate[r] = line
        keep[r] = 1.0 - 4.0 * line


def fold(total, fields):
    folded = total[0:fields]
    for j in range(fields, SUB, fields):
        folded = folded + total[j : j + fields]
    return folded


def own(*refs, count, fields, pairs, last):
    members, rate_ref, order = refs[0:3]
    pieces = refs[3 : 3 + count]
    own_out, beyond, far_coarse, rates_out, message = refs[3 + count : 8 + count]
    v, keep, rate, c, cw, cp, acc, eb = refs[8 + count :]
    height = c.shape[0]
    reach = SPREAD_PASSES
    tall = height + reach
    parts = parts_of(v.shape[2])

    rates_out[...] = reorder(rate_ref[...], order[...])
    fill_rates(rates_out, keep, rate, height + 12, 4)
    me = lax.axis_index("mem")
    for d, piece in enumerate(pieces):
        breadth = piece.shape[1]
        where = lax.rem(me - d + count, count)
        at = pl.ds(pl.multiple_of(where * breadth, LANES), breadth)
        cw[:, at] = piece[0 : fields * tall, :]
        eb[where] = piece[fields * tall :, :]
    lane = lane_iota((tall, LANES))
    for q in range(count - 1):
        last_column = (q + 1) * breadth - 1
        for mine, other, table_at, grad_at, goal in (
            (q, q + 1, 104, 16, last_column),
            (q + 1, q, 40, 80, last_column + 1),
        ):
            added = jnp.zeros((tall, LANES), F32)
            for a in range(4):
                entry = eb[mine, 8 : 8 + tall, table_at + a : table_at + a + 1]
                added = added + entry * eb[other, pl.ds(a + 7, tall, stride=2), :]
            begin = goal // LANES * LANES
            for f in range(fields):
                turn = (goal - begin - grad_at - f) % LANES
                here = jnp.where(lane == goal - begin, pltpu.roll(added, turn, 1), 0.0)
                rows = slice(f * tall, (f + 1) * tall)
                cw[rows, begin : begin + LANES] = cw[rows, begin : begin + LANES] + here
    moved = reorder(cw[...], order[...])
    for t, p in enumerate(parts):
        cp[t] = moved[:, p]
        for r in range(tall):
            row = cp[t, pl.ds(r, fields, stride=tall), :]
            for j in range(0, SUB, fields):
                if r < height:
                    c[r, j : j + fields, p] = row
                else:
                    far_coarse[r - height, j : j + fields, p] = row
    acc[...] = jnp.zeros(acc.shape, F32)
    off = 5

    def one(i, _):
        v[0:off] = jnp.zeros((off,) + v.shape[1:], F32)
        v[height + off :] = jnp.zeros((v.shape[0] - height - off,) + v.shape[1:], F32)
        for r in range(height):
            v[r + off] = members[i, r] * c[r]
        for s in range(1, SPREAD_PASSES + 1):
            sweep(v, keep, rate, -min(s, SPREAD_PASSES - s), height + s, off, 4)
        for r in range(height):
            acc[r] = acc[r] + members[i, r] * v[r + off]
        for r in range(reach):
            beyond[i, r] = v[r + height + off]
        return _

    lax.fori_loop(0, pairs, one, 0)
    for r in range(height):
        own_out[r * fields : (r + 1) * fields, :] = fold(acc[r], fields)
    two = 2 * fields
    message[0:two, :] = own_out[0:two, :]
    for j in range(last):
        for r in range(reach):
            at = two + (j * reach + r) * SUB
            message[at : at + SUB, :] = members[pairs - last + j, r]


def cross(far_rows, members, beyond, far_coarse, rates, order, near_out, far_out,
          keep, rate, near, far, fw, *, fields, begin, number, skip, arranged):
    reach = SPREAD_PASSES
    height = members.shape[1]
    parts = parts_of(rates.shape[1])
    fill_rates(rates, keep, rate, 2 * reach, height)
    near[...] = jnp.zeros(near.shape, F32)
    far[...] = jnp.zeros(far.shape, F32)
    size = SUB * reach
    if not arranged:
        moved = jnp.dot(
            far_rows[...].astype(jnp.bfloat16), order[...], preferred_element_type=F32
        )
        for t, p in enumerate(parts):
            fw[t] = moved[:, p]

    def one(i, x):
        window = [[None] * len(parts) for _ in range(reach)]
        for t, p in enumerate(parts):
            for r in range(reach):
                if arranged:
                    at = pl.multiple_of(skip + i * size + r * SUB, SUB)
                    line = far_rows[pl.ds(at, SUB), p]
                else:
                    line = fw[t, pl.ds(i * size + r, SUB, stride=reach), :]
                window[r][t] = line * far_coarse[r, :, p]
                far[r, :, p] = far[r, :, p] + line * beyond[begin + i, r, :, p]
        for s in range(1, SPREAD_PASSES + 1):
            window = climb(window, keep, rate, height - s, reach - height)
        for r in range(reach):
            for t, p in enumerate(parts):
                line = members[begin + i, height - reach + r, :, p]
                near[r, :, p] = near[r, :, p] + line * window[r][t]
        return x

    if arranged:
        lax.fori_loop(0, number, one, 0)
    else:
        for i in range(number):
            one(i, 0)
    for r in range(reach):
        near_out[r * fields : (r + 1) * fields, :] = fold(near[r], fields)
        far_out[r * fields : (r + 1) * fields, :] = fold(far[r], fields)


def gather_parts(*refs, groups, fields):
    own_ref = refs[0]
    nears = refs[1 : 1 + groups]
    fars = refs[1 + groups : 1 + 2 * groups]
    total_out, below_out = refs[1 + 2 * groups :]
    rows = own_ref.shape[0]
    reach = SPREAD_PASSES * fields
    near = nears[0][...]
    far = fars[0][...]
    for x, y in zip(nears[1:], fars[1:]):
        near = near + x[...]
        far = far + y[...]
    near = near + own_ref[rows - reach : rows, :]
    total_out[0 : rows - reach, :] = own_ref[0 : rows - reach, :]
    total_out[rows - reach : rows, :] = near
    below_out[0:fields, :] = jnp.zeros((fields, near.shape[1]), F32)
    below_out[fields : 2 * fields, :] = near[reach - fields : reach, :]
    below_out[2 * fields :, :] = far


def pack_sums(total, below, from_above, from_below, order, *refs, count, fields):
    outs, moved_in, held = refs[:-2], refs[-2], refs[-1]
    rows = total.shape[0]
    tall = held.shape[1]
    two = 2 * fields
    tiles = held.shape[0] - 2
    held[0] = jnp.zeros(held.shape[1:], F32)
    held[tiles + 1] = jnp.zeros(held.shape[1:], F32)
    reach = from_above.shape[0]
    moved_in[0:two, :] = from_above[0:two, :]
    moved_in[two:reach, :] = from_above[two:reach, :] + total[0 : reach - two, :]
    moved_in[reach : rows + two, :] = total[reach - two : rows, :]
    moved_in[rows + two : tall, :] = below[two : 2 * two, :] + from_below[0:two, :]
    natural = reorder(moved_in[...], order[...], 1)
    for t, p in enumerate(parts_of(total.shape[1])):
        held[t + 1] = natural[:, p]
    me = lax.axis_index("mem")
    lane = lane_iota((SUB, LANES))
    width = tiles // count
    for d in range(count):
        at = lax.rem(me + d, count) * width
        packed = jnp.zeros((SUB, LANES), F32)
        for w in range(width):
            outs[d][0:tall, w * LANES : (w + 1) * LANES] = held[at + 1 + w]
        for k in range(tall // SUB):
            rows8 = slice(k * SUB, (k + 1) * SUB)
            edge = jnp.where(lane == 0, held[at + 1 + width, rows8, :], held[at, rows8, :])
            edge = pltpu.roll(edge, 2 * k + 1, 1)
            packed = jnp.where((lane == 2 * k) | (lane == 2 * k + 1), edge, packed)
        outs[d][tall : tall + SUB, 0:LANES] = packed


def finish(*refs, count, fields):
    pieces = refs[:count]
    static, table, out, held, wide = refs[count:]
    height = table.shape[1]
    rows, cols = out.shape[1:]
    breadth = table.shape[2]
    tall = held.shape[1]
    total = pieces[0][...]
    for piece in pieces[1:]:
        total = total + piece[...]
    packed = total[tall:, :]
    lane = lane_iota((SUB, LANES))
    for k in range(tall // SUB):
        x = total[k * SUB : (k + 1) * SUB, :]
        rows8 = slice(k * SUB, (k + 1) * SUB)
        held[0, rows8, :] = x
        left = pltpu.roll(packed, LANES - 2 * k, 1) if k else packed
        right = pltpu.roll(packed, LANES - 2 - 2 * k, 1)
        held[1, rows8, :] = jnp.where(lane == 0, left, pltpu.roll(x, 1, 1))
        held[2, rows8, :] = jnp.where(lane == LANES - 1, right, pltpu.roll(x, LANES - 1, 1))
    for f in range(fields):
        for p in range(2):
            even = jnp.zeros((height, breadth), F32)
            odd = jnp.zeros((height, breadth), F32)
            for a, off in ((1 + p, 0), (3 - 3 * p, 2 * p - 1)):
                at = pl.ds(f + fields * (2 + off), height, stride=fields)
                here = held[0, at, :]
                even = even + table[4 * a + 1] * here + table[4 * a + 3] * held[1, at, :]
                odd = odd + table[4 * a + 2] * here + table[4 * a] * held[2, at, :]
            at = pl.ds(f * rows + p, height, stride=2)
            wide[0, at, :] = even
            wide[1, at, :] = odd
    both = jnp.concatenate([wide[0], wide[1]], axis=1)
    fine = jnp.dot(both, spread_columns(cols), precision=EXACT, preferred_element_type=F32)
    for f in range(fields):
        out[f] = static[f] + fine[f * rows : (f + 1) * rows, :]


def groups_of(pairs):
    sizes = [max(1, pairs // 5), max(1, 2 * pairs // 5)]
    sizes += [max(1, pairs - sum(sizes) - 1), 1]
    return [(sum(sizes[:g]), size) for g, size in enumerate(sizes)]


def local(gradient, static_scale, static_rate, interp_index, interp_weight, members, spread_rate):
    fields, rows, cols = gradient.shape
    slots, height, breadth = interp_index.shape
    member_count, _, _, width = members.shape
    reach = SPREAD_PASSES
    tiles = lax.axis_size("tile")
    count = lax.axis_size("mem")
    upward = [(i + 1, i) for i in range(tiles - 1)]
    downward = [(i, i + 1) for i in range(tiles - 1)]
    rings = [[(i, (i + d) % count) for i in range(count)] for d in range(count)]
    per = SUB // fields
    pairs = member_count // per
    vmem = pl.BlockSpec(memory_space=pltpu.VMEM)
    smem = pl.BlockSpec(memory_space=pltpu.SMEM)
    smalls = (gradient, static_scale, interp_index, interp_weight, spread_rate)
    column_parts = width // cols
    order = permutation(width)

    groups = groups_of(pairs)
    last = groups[-1][1]
    line = (SUB, width)
    lane_tiles = width // LANES
    size = SUB * reach
    number = groups[0][1]

    up, down, kept, first = call(
        pack_tile,
        [
            (fields * 24 + slots * 8 + column_parts * 8, cols),
            (fields * 8 + (slots + column_parts * 4 + 7) // 8 * 8, cols),
            ((slots + column_parts) * height, cols),
            (number * size, width),
        ],
        [pltpu.VMEM(x.shape, x.dtype) for x in smalls]
        + [
            pltpu.VMEM((per * number,) + members.shape[1:], members.dtype),
            pltpu.SemaphoreType.DMA((6,)),
        ],
        in_specs=[pl.BlockSpec(memory_space=pltpu.HBM)] * 6,
        limit=VMEM_BYTES / (1 << 20),
        name="pack_tile",
    )(*smalls, members)
    first = lax.ppermute(first, "tile", upward)
    up = lax.ppermute(up, "tile", upward)
    down = lax.ppermute(down, "tile", downward)
    members, *firsts = call(
        functools.partial(arrange, pairs=pairs, groups=groups[1:-1]),
        [(pairs, height) + line] + [(n * size, width) for _, n in groups[1:-1]],
        [(lane_tiles, pairs * SUB * height, LANES)],
        limit=8,
        name="arrange",
    )(members, order)
    far_rows = [first] + [lax.ppermute(rows_k, "tile", upward) for rows_k in firsts]

    tall = height + reach
    quarter, rates = call(
        functools.partial(restrict, slots=slots),
        [(fields * tall + 64, breadth), (height + 16, width)],
        [(64, cols), (4, 64, breadth), (64, LANES)],
        name="restrict",
    )(gradient, static_scale, kept, up, down)
    pieces = [quarter] + [lax.ppermute(quarter, "mem", rings[d]) for d in range(1, count)]

    static, table = call(
        functools.partial(side, members_all=member_count * count),
        [(fields, rows, cols), (16, height, breadth)],
        [
            (rows + 16, cols + 2 * LANES),
            (slots, height + 16, breadth),
            (slots, height + 16, breadth),
            (height + 16, breadth),
        ],
        in_specs=[vmem, vmem, smem] + [vmem] * 5,
        name="side",
    )(gradient, static_scale, static_rate, kept, up, down, pieces[1], pieces[-1])

    two = 2 * fields
    own_sum, beyond, far_coarse, rates, message = call(
        functools.partial(own, count=count, fields=fields, pairs=pairs, last=last),
        [
            (height * fields, width),
            (pairs, reach) + line,
            (reach,) + line,
            rates.shape,
            (two + last * size, width),
        ],
        [
            (height + reach + 6,) + line,
            (height + 12,) + line,
            (height + 12,) + line,
            (height,) + line,
            (fields * tall, width),
            (lane_tiles, fields * tall, LANES),
            (height,) + line,
            (count, 64, LANES),
        ],
        limit=8,
        name="own",
    )(members, rates, order, *pieces)
    message = lax.ppermute(message, "tile", upward)
    far_rows.append(message)

    nears, fars = [], []
    for k, (g, n) in enumerate(groups):
        near, far = call(
            functools.partial(
                cross,
                fields=fields,
                begin=g,
                number=n,
                skip=two if k == len(groups) - 1 else 0,
                arranged=k > 0,
            ),
            [(reach * fields, width)] * 2,
            [
                (2 * reach,) + line,
                (2 * reach,) + line,
                (reach,) + line,
                (reach,) + line,
                (lane_tiles, size if k else n * size, LANES),
            ],
            limit=4,
            name="cross",
        )(far_rows[k], members, beyond, far_coarse, rates, order)
        nears.append(near)
        fars.append(far)

    total, below = call(
        functools.partial(gather_parts, groups=len(groups), fields=fields),
        [(height * fields, width), ((reach + 2) * fields, width)],
        name="gather_parts",
    )(own_sum, *nears, *fars)
    from_above = lax.ppermute(below, "tile", downward)
    high = (height + 4) * fields
    sums = call(
        functools.partial(pack_sums, count=count, fields=fields),
        [(high + SUB, breadth)] * count,
        [(high, width), (lane_tiles + 2, high, LANES)],
        name="pack_sums",
    )(total, below, from_above, message, order)
    arrived = [sums[0]] + [lax.ppermute(sums[d], "mem", rings[d]) for d in range(1, count)]
    (hybrid,) = call(
        functools.partial(finish, count=count, fields=fields),
        [(fields, rows, cols)],
        [(3, high, LANES), (2, fields * rows, breadth)],
        name="finish",
    )(*arrived, static, table)
    return hybrid


def solution(mesh):
    return jax.shard_map(
        local,
        mesh=mesh,
        in_specs=(
            P(None, "tile", "mem"),
            P(None, "tile", "mem"),
            P(),
            P(None, "tile", "mem"),
            P(None, "tile", "mem"),
            P("mem", None, "tile", None),
            P("tile", None),
        ),
        out_specs=P(None, "tile", "mem"),
        check_vma=False,
    )
```

```python
import functools

import jax
import jax.numpy as jnp
from jax import lax
from jax.experimental import pallas as pl
from jax.experimental.pallas import tpu as pltpu
from jax.sharding import PartitionSpec as P


STATIC_PASSES = 4
SPREAD_PASSES = 8
LANES = 128
SUB = 8
VMEM_BYTES = 67043328


F32 = jnp.float32
EXACT = lax.Precision.HIGHEST


def call(kernel, out_shapes, scratch=(), limit=4, **kw):
    return pl.pallas_call(
        kernel,
        out_shape=tuple(jax.ShapeDtypeStruct(s, F32) for s in out_shapes),
        scratch_shapes=[pltpu.VMEM(s, F32) if isinstance(s, tuple) else s for s in scratch],
        compiler_params=pltpu.CompilerParams(vmem_limit_bytes=int(limit * (1 << 20))),
        **kw,
    )


def pack_tile(*refs):
    sources, (up, down, kept, first), held, done = refs[:6], refs[6:10], refs[10:16], refs[16]
    number = held[5].shape[0]
    sources = sources[:5] + (sources[5].at[0:number],)
    copies = [
        pltpu.make_async_copy(source, target, done.at[k])
        for k, (source, target) in enumerate(zip(sources, held))
    ]
    for copy in copies:
        copy.start()
    for copy in copies:
        copy.wait()
    grad, scale, index, weight, rate, members = held
    first[...] = members[:, :, 0:SPREAD_PASSES, :].astype(F32).reshape(first.shape)
    fields, rows, cols = grad.shape
    slots, height, breadth = index.shape
    parts = rate.shape[1] // cols
    reach = SPREAD_PASSES
    up[...] = jnp.zeros(up.shape, F32)
    down[...] = jnp.zeros(down.shape, F32)
    for f in range(fields):
        top = 2 * reach + 1
        up[f * 24 : f * 24 + top, :] = grad[f, 0:top, :]
        up[f * 24 + top : f * 24 + top + STATIC_PASSES, :] = (
            scale[f, 0:STATIC_PASSES, :] * grad[f, 0:STATIC_PASSES, :]
        )
        down[f * 8 : f * 8 + 1, :] = grad[f, rows - 1 : rows, :]
        down[f * 8 + 1 : f * 8 + 1 + STATIC_PASSES, :] = (
            scale[f, rows - STATIC_PASSES : rows, :] * grad[f, rows - STATIC_PASSES : rows, :]
        )
    base = fields * 24
    low = fields * 8
    for s in range(slots):
        up[base + s * 8 : base + s * 8 + 8, 0:breadth] = index[s, 0:8, :].astype(F32)
        up[base + s * 8 : base + s * 8 + 8, breadth:] = weight[s, 0:8, :]
        down[low + s : low + s + 1, 0:breadth] = index[s, height - 1 : height, :].astype(F32)
        down[low + s : low + s + 1, breadth:] = weight[s, height - 1 : height, :]
    base += slots * 8
    low += slots
    for p in range(parts):
        part = slice(p * cols, (p + 1) * cols)
        up[base + p * 8 : base + p * 8 + 8, :] = rate[0:8, part]
        down[low + p * 4 : low + p * 4 + 4, :] = rate[height - 4 : height, part]
        kept[(slots + p) * height : (slots + p + 1) * height, :] = rate[:, part]
    for s in range(slots):
        kept[s * height : (s + 1) * height, 0:breadth] = index[s].astype(F32)
        kept[s * height : (s + 1) * height, breadth:] = weight[s]


def lane_iota(shape):
    return lax.broadcasted_iota(jnp.int32, shape, len(shape) - 1)


def pick_columns(cols):
    source = lax.broadcasted_iota(jnp.int32, (cols, cols), 0)
    target = lax.broadcasted_iota(jnp.int32, (cols, cols), 1)
    half = cols // 2
    wanted = jnp.where(target < half, 2 * target, 2 * (target - half) + 1)
    return jnp.where(source == wanted, 1.0, 0.0).astype(F32)


def quarter_column(lane, count):
    seg = LANES // count
    return count * (lane % seg) + lane // seg


def spread_columns(cols, count):
    source = lax.broadcasted_iota(jnp.int32, (cols, cols), 0)
    target = lax.broadcasted_iota(jnp.int32, (cols, cols), 1)
    half = cols // 2
    wanted = 2 * quarter_column(source % half, count) + source // half
    return jnp.where(target == wanted, 1.0, 0.0).astype(jnp.bfloat16)


def table_rows(index, weight):
    rows = []
    for o in range(16):
        total = jnp.zeros(index[0].shape, F32)
        for i, w in zip(index, weight):
            total = total + jnp.where(i == float(o), w, 0.0)
        rows.append(total)
    return rows


def slots_of(kept, height, breadth, slots):
    rows = [slice(s * height, (s + 1) * height) for s in range(slots)]
    return [kept[r, 0:breadth] for r in rows], [kept[r, breadth:] for r in rows]


def restrict(grad, scale, kept, up, down, out, rate_out, ext, cols4, edge, *, slots):
    fields, rows, cols = grad.shape
    height, breadth = rows // 2, cols // 2
    parts = kept.shape[0] // height - slots
    index, weight = slots_of(kept, height, breadth, slots)
    n = STATIC_PASSES
    top = 2 * SPREAD_PASSES + 1
    tall = height + SPREAD_PASSES
    base = fields * 24
    low = fields * 8
    table = table_rows(
        [
            jnp.concatenate(
                [index[s], up[base + s * 8 : base + s * 8 + 8, 0:breadth]], axis=0
            )
            for s in range(slots)
        ],
        [
            jnp.concatenate([weight[s], up[base + s * 8 : base + s * 8 + 8, breadth:]], axis=0)
            for s in range(slots)
        ],
    )
    pick = pick_columns(cols)
    ext[...] = jnp.zeros(ext.shape, F32)
    edge[...] = jnp.zeros(edge.shape, F32)
    lane = lane_iota((ext.shape[0], breadth))
    for f in range(fields):
        ext[8 : 8 + rows, :] = grad[f]
        ext[7:8, :] = down[f * 8 : f * 8 + 1, :]
        ext[8 + rows : 8 + rows + top, :] = up[f * 24 : f * 24 + top, :]
        edge[:, 16 + f : 17 + f] = ext[:, 0:1]
        edge[:, 80 + f : 81 + f] = ext[:, cols - 1 : cols]
        both = jnp.dot(ext[...], pick, precision=EXACT, preferred_element_type=F32)
        even = both[:, :breadth]
        odd = both[:, breadth:]
        cols4[0] = jnp.where(lane == 0, 0.0, pltpu.roll(odd, 1, 1))
        cols4[1] = even
        cols4[2] = odd
        cols4[3] = jnp.where(lane == breadth - 1, 0.0, pltpu.roll(even, breadth - 1, 1))
        total = jnp.zeros((tall, breadth), F32)
        for a in range(4):
            for b in range(4):
                total = total + table[4 * a + b] * cols4[b, pl.ds(a + 7, tall, stride=2), :]
        out[f * tall : (f + 1) * tall, :] = total
    for at, wide, lone in ((0, 0, 0), (64, cols - n, breadth - 1)):
        for f in range(fields):
            lanes = slice(at + 4 * f, at + 4 * f + n)
            columns = slice(wide, wide + n)
            edge[8 : 8 + rows, lanes] = scale[f, :, columns] * grad[f, :, columns]
            edge[8 - n : 8, lanes] = down[f * 8 + 1 : f * 8 + 1 + n, columns]
            edge[8 + rows : 8 + rows + n, lanes] = up[f * 24 + top : f * 24 + top + n, columns]
        one = slice(lone, lone + 1)
        second = slice(breadth + lone, breadth + lone + 1)
        for s in range(slots):
            lanes = slice(at + 32 + s, at + 33 + s)
            edge[8 : 8 + height, lanes] = index[s][:, one]
            edge[7:8, lanes] = down[low + s : low + s + 1, one]
            edge[8 + height : 9 + height, lanes] = up[base + s * 8 : base + s * 8 + 1, one]
            lanes = slice(at + 36 + s, at + 37 + s)
            edge[8 : 8 + height, lanes] = weight[s][:, one]
            edge[7:8, lanes] = down[low + s : low + s + 1, second]
            edge[8 + height : 9 + height, lanes] = up[base + s * 8 : base + s * 8 + 1, second]
        for a in range(4):
            entry = table[4 * a] if at == 0 else table[4 * a + 3]
            edge[8 : 8 + tall, at + 40 + a : at + 41 + a] = entry[:, one]
    out[fields * tall :, :] = edge[...]
    base = fields * 24 + slots * 8
    low = fields * 8 + slots
    rate_out[0:4, :] = jnp.zeros((4, rate_out.shape[1]), F32)
    for p in range(parts):
        part = slice(p * cols, (p + 1) * cols)
        rate_out[8 : 8 + height, part] = kept[(slots + p) * height : (slots + p + 1) * height, :]
        rate_out[4:8, part] = down[low + p * 4 : low + p * 4 + 4, :]
        rate_out[8 + height : 16 + height, part] = up[base + p * 8 : base + p * 8 + 8, :]


def side(grad, scale, stat_rate, kept, up, down, west_message, east_message,
         static, table_out, box, idx, wgt, tab, *, members_all):
    fields, rows, cols = grad.shape
    slots, (height, breadth) = idx.shape[0], table_out.shape[1:]
    index, weight = slots_of(kept, height, breadth, slots)
    n = STATIC_PASSES
    top = 2 * SPREAD_PASSES + 1
    me = lax.axis_index("mem")
    skip = fields * (height + SPREAD_PASSES)
    from_west = jnp.where(me > 0, pltpu.roll(west_message[skip:, :], 64, 1), 0.0)
    from_east = jnp.where(me < lax.axis_size("mem") - 1, east_message[skip:, :], 0.0)
    wide = cols + 2 * LANES
    shape = (rows + 16, wide)
    row = lax.broadcasted_iota(jnp.int32, shape, 0)
    col = lane_iota(shape)
    first_row = jnp.where(lax.axis_index("tile") == 0, 8, 0)
    last_row = jnp.where(lax.axis_index("tile") == lax.axis_size("tile") - 1, 8 + rows, rows + 16)
    first_col = jnp.where(lax.axis_index("mem") == 0, LANES, 0)
    last_col = jnp.where(lax.axis_index("mem") == lax.axis_size("mem") - 1, LANES + cols, wide)
    inside = (row >= first_row) & (row < last_row) & (col >= first_col) & (col < last_col)
    for f in range(fields):
        box[...] = jnp.zeros(box.shape, F32)
        box[8 : 8 + rows, LANES : LANES + cols] = scale[f] * grad[f]
        box[8 - n : 8, LANES : LANES + cols] = down[f * 8 + 1 : f * 8 + 1 + n, :]
        box[8 + rows : 8 + rows + n, LANES : LANES + cols] = up[f * 24 + top : f * 24 + top + n, :]
        box[:, LANES - n : LANES] = from_west[0 : rows + 16, 4 * f : 4 * f + n]
        box[:, LANES + cols : LANES + cols + n] = from_east[0 : rows + 16, 4 * f : 4 * f + n]
        field = box[...]
        rate = jnp.where(inside, stat_rate[f], 0.0)
        for _ in range(n):
            beside = (
                pltpu.roll(field, 1, 0)
                + pltpu.roll(field, rows + 15, 0)
                + pltpu.roll(field, 1, 1)
                + pltpu.roll(field, wide - 1, 1)
            )
            field = field + rate * (beside - 4.0 * field)
        static[f] = 0.3 * scale[f] * field[8 : 8 + rows, LANES : LANES + cols]
    factor = 2.8 / (members_all - 1)
    base = fields * 24
    low = fields * 8
    tall = height + 16
    lane = lane_iota((tall, breadth))
    for s in range(slots):
        idx[s] = jnp.zeros((tall, breadth), F32)
        wgt[s] = jnp.zeros((tall, breadth), F32)
        idx[s, 8 : 8 + height, :] = index[s]
        wgt[s, 8 : 8 + height, :] = weight[s]
        idx[s, 7:8, :] = down[low + s : low + s + 1, 0:breadth]
        wgt[s, 7:8, :] = down[low + s : low + s + 1, breadth:]
        idx[s, 8 + height : 9 + height, :] = up[base + s * 8 : base + s * 8 + 1, 0:breadth]
        wgt[s, 8 + height : 9 + height, :] = up[base + s * 8 : base + s * 8 + 1, breadth:]
    west = from_west[0:tall, :]
    east = from_east[0:tall, :]

    def shifted(x, shift, at):
        if shift == 1:
            return jnp.where(lane == 0, pltpu.roll(west, LANES - at, 1), pltpu.roll(x, 1, 1))
        if shift == 2:
            return jnp.where(
                lane == breadth - 1,
                pltpu.roll(east, LANES - 1 - at, 1),
                pltpu.roll(x, breadth - 1, 1),
            )
        return x

    for shift, columns in ((0, (1, 2)), (1, (3,)), (2, (0,))):
        table = table_rows(
            [shifted(idx[s], shift, 32 + s) for s in range(slots)],
            [shifted(wgt[s], shift, 36 + s) for s in range(slots)],
        )
        for b in columns:
            for a in range(4):
                off = (1, 0, 0, -1)[a]
                tab[...] = factor * table[4 * a + b]
                table_out[4 * a + b] = tab[8 + off : 8 + off + height, :]
    source = lax.broadcasted_iota(jnp.int32, (breadth, breadth), 0)
    target = lax.broadcasted_iota(jnp.int32, (breadth, breadth), 1)
    order = jnp.where(source == quarter_column(target, lax.axis_size("mem")), 1.0, 0.0)
    flat = reorder(table_out[...].reshape(16 * height, breadth), order.astype(jnp.bfloat16))
    table_out[...] = flat.reshape(16, height, breadth)


def parts_of(width):
    return [slice(t, t + LANES) for t in range(0, width, LANES)]


def sweep(v, keep, rate, lo, hi, v_at, rate_at):
    parts = parts_of(v.shape[2])
    lane = lane_iota((SUB, LANES))

    def right_below(here, below):
        right = jnp.where(lane == LANES - 1, 0.0, pltpu.roll(here[0], LANES - 1, 1))
        return [x + y for x, y in zip(here[1:] + [right], below)]

    above = [v[lo - 1 + v_at, :, p] for p in parts]
    here = [v[lo + v_at, :, p] for p in parts]
    after = right_below(above, here)
    for r in range(lo, hi):
        below = [v[r + 1 + v_at, :, p] for p in parts]
        first = jnp.where(lane == 0, 0.0, pltpu.roll(here[-1], 1, 1)) + above[0]
        before = [first] + after[:-1]
        after = right_below(here, below)
        for t, p in enumerate(parts):
            total = before[t] + after[t]
            v[r + v_at, :, p] = keep[r + rate_at, :, p] * here[t] + rate[r + rate_at, :, p] * total
        above, here = here, below


def climb(rows, keep, rate, lo, rate_at):
    tiles = len(rows[0])
    lane = lane_iota((SUB, LANES))
    parts = parts_of(tiles * LANES)
    result = []
    above = here = after = None
    for k, below in enumerate(rows):
        r = lo + k + rate_at
        if here is None:
            result.append([rate[r, :, p] * x for p, x in zip(parts, below)])
            above, here, after = None, below, list(below)
            continue
        left = jnp.where(lane == 0, 0.0, pltpu.roll(here[-1], 1, 1))
        first = left if above is None else left + above[0]
        before = [first] + after[: tiles - 1] if above is not None else [first] + here[: tiles - 1]
        right = jnp.where(lane == LANES - 1, 0.0, pltpu.roll(here[0], LANES - 1, 1))
        after = [x + y for x, y in zip(here[1:] + [right], below)]
        result.append(
            [
                keep[r, :, p] * here[t] + rate[r, :, p] * (before[t] + after[t])
                for t, p in enumerate(parts)
            ]
        )
        above, here = here, below
    return result


def permutation(width):
    source = lax.broadcasted_iota(jnp.int32, (width, width), 0)
    target = lax.broadcasted_iota(jnp.int32, (width, width), 1)
    tiles = width // LANES
    return jnp.where(source == tiles * (target % LANES) + target // LANES, 1.0, 0.0).astype(
        jnp.bfloat16
    )


def reorder(x, order, contract=0):
    dims = (((1,), (contract,)), ((), ()))
    high = x.astype(jnp.bfloat16)
    rest = x - high.astype(F32)
    middle = rest.astype(jnp.bfloat16)
    low = (rest - middle.astype(F32)).astype(jnp.bfloat16)
    moved = [
        lax.dot_general(y, order, dims, preferred_element_type=F32) for y in (high, middle, low)
    ]
    return moved[0] + (moved[1] + moved[2])


def arrange(members, order, *refs, pairs, groups):
    held, firsts, moved_rows = refs[0], refs[1:-1], refs[-1]
    per = members.shape[0] // pairs
    height, width = members.shape[2:]
    rows = SUB * height
    for b in range(0, pairs, 2):
        n = min(2, pairs - b)
        block = members[b * per : (b + n) * per].reshape(n * rows, width)
        moved = jnp.dot(block, order[...], preferred_element_type=F32)
        for t, p in enumerate(parts_of(width)):
            moved_rows[t, b * rows : (b + n) * rows, :] = moved[:, p]
            for i in range(b, b + n):
                outs = [(out, g) for out, (g, m) in zip(firsts, groups) if g <= i < g + m]
                for r in range(height):
                    line = moved_rows[t, pl.ds(i * rows + r, SUB, stride=height), :]
                    held[i, r, :, p] = line
                    if r < SPREAD_PASSES:
                        for out, g in outs:
                            at = ((i - g) * SPREAD_PASSES + r) * SUB
                            out[at : at + SUB, p] = line


def fill_rates(rate_ref, keep, rate, rows, at):
    for r in range(rows):
        line = jnp.broadcast_to(rate_ref[r + at : r + at + 1, :], rate.shape[1:])
        rate[r] = line
        keep[r] = 1.0 - 4.0 * line


def fold(total, fields):
    folded = total[0:fields]
    for j in range(fields, SUB, fields):
        folded = folded + total[j : j + fields]
    return folded


def own(*refs, count, fields, pairs, last):
    members, rate_ref, order = refs[0:3]
    pieces = refs[3 : 3 + count]
    own_out, beyond, far_coarse, rates_out, message = refs[3 + count : 8 + count]
    v, keep, rate, c, cw, cp, acc, eb = refs[8 + count :]
    height = c.shape[0]
    reach = SPREAD_PASSES
    tall = height + reach
    parts = parts_of(v.shape[2])

    rates_out[...] = reorder(rate_ref[...], order[...])
    fill_rates(rates_out, keep, rate, height + 12, 4)
    me = lax.axis_index("mem")
    for d, piece in enumerate(pieces):
        breadth = piece.shape[1]
        where = lax.rem(me - d + count, count)
        at = pl.ds(pl.multiple_of(where * breadth, LANES), breadth)
        cw[:, at] = piece[0 : fields * tall, :]
        eb[where] = piece[fields * tall :, :]
    lane = lane_iota((tall, LANES))
    for q in range(count - 1):
        last_column = (q + 1) * breadth - 1
        for mine, other, table_at, grad_at, goal in (
            (q, q + 1, 104, 16, last_column),
            (q + 1, q, 40, 80, last_column + 1),
        ):
            added = jnp.zeros((tall, LANES), F32)
            for a in range(4):
                entry = eb[mine, 8 : 8 + tall, table_at + a : table_at + a + 1]
                added = added + entry * eb[other, pl.ds(a + 7, tall, stride=2), :]
            begin = goal // LANES * LANES
            for f in range(fields):
                turn = (goal - begin - grad_at - f) % LANES
                here = jnp.where(lane == goal - begin, pltpu.roll(added, turn, 1), 0.0)
                rows = slice(f * tall, (f + 1) * tall)
                cw[rows, begin : begin + LANES] = cw[rows, begin : begin + LANES] + here
    moved = reorder(cw[...], order[...])
    for t, p in enumerate(parts):
        cp[t] = moved[:, p]
        for r in range(tall):
            row = cp[t, pl.ds(r, fields, stride=tall), :]
            for j in range(0, SUB, fields):
                if r < height:
                    c[r, j : j + fields, p] = row
                else:
                    far_coarse[r - height, j : j + fields, p] = row
    acc[...] = jnp.zeros(acc.shape, F32)
    off = 5

    def one(i, _):
        v[0:off] = jnp.zeros((off,) + v.shape[1:], F32)
        v[height + off :] = jnp.zeros((v.shape[0] - height - off,) + v.shape[1:], F32)
        for r in range(height):
            v[r + off] = members[i, r] * c[r]
        for s in range(1, SPREAD_PASSES + 1):
            sweep(v, keep, rate, -min(s, SPREAD_PASSES - s), height + s, off, 4)
        for r in range(height):
            acc[r] = acc[r] + members[i, r] * v[r + off]
        for r in range(reach):
            beyond[i, r] = v[r + height + off]
        return _

    lax.fori_loop(0, pairs, one, 0)
    for r in range(height):
        own_out[r * fields : (r + 1) * fields, :] = fold(acc[r], fields)
    two = 2 * fields
    message[0:two, :] = own_out[0:two, :]
    for j in range(last):
        for r in range(reach):
            at = two + (j * reach + r) * SUB
            message[at : at + SUB, :] = members[pairs - last + j, r]


def cross(far_rows, members, beyond, far_coarse, rates, order, near_out, far_out,
          keep, rate, near, far, fw, *, fields, begin, number, skip, arranged):
    reach = SPREAD_PASSES
    height = members.shape[1]
    parts = parts_of(rates.shape[1])
    fill_rates(rates, keep, rate, 2 * reach, height)
    near[...] = jnp.zeros(near.shape, F32)
    far[...] = jnp.zeros(far.shape, F32)
    size = SUB * reach
    if not arranged:
        moved = jnp.dot(
            far_rows[...].astype(jnp.bfloat16), order[...], preferred_element_type=F32
        )
        for t, p in enumerate(parts):
            fw[t] = moved[:, p]

    def one(i, x):
        window = [[None] * len(parts) for _ in range(reach)]
        for t, p in enumerate(parts):
            for r in range(reach):
                if arranged:
                    at = pl.multiple_of(skip + i * size + r * SUB, SUB)
                    line = far_rows[pl.ds(at, SUB), p]
                else:
                    line = fw[t, pl.ds(i * size + r, SUB, stride=reach), :]
                window[r][t] = line * far_coarse[r, :, p]
                far[r, :, p] = far[r, :, p] + line * beyond[begin + i, r, :, p]
        for s in range(1, SPREAD_PASSES + 1):
            window = climb(window, keep, rate, height - s, reach - height)
        for r in range(reach):
            for t, p in enumerate(parts):
                line = members[begin + i, height - reach + r, :, p]
                near[r, :, p] = near[r, :, p] + line * window[r][t]
        return x

    if arranged:
        lax.fori_loop(0, number, one, 0)
    else:
        for i in range(number):
            one(i, 0)
    for r in range(reach):
        near_out[r * fields : (r + 1) * fields, :] = fold(near[r], fields)
        far_out[r * fields : (r + 1) * fields, :] = fold(far[r], fields)


def pack_sums(*refs, groups, count, fields):
    own_ref, edge = refs[:2]
    nears = refs[2 : 2 + groups]
    fars = refs[2 + groups : 2 + 2 * groups]
    outs, held = refs[2 + 2 * groups : -1], refs[-1]
    rows = own_ref.shape[0]
    tiles, tall = held.shape[:2]
    two = 2 * fields
    reach = SPREAD_PASSES * fields
    near = nears[0][...]
    far = fars[0][...]
    for x, y in zip(nears[1:], fars[1:]):
        near = near + x[...]
        far = far + y[...]
    near = near + own_ref[rows - reach : rows, :]
    for t, p in enumerate(parts_of(own_ref.shape[1])):
        held[t, 0 : rows - reach, :] = own_ref[0 : rows - reach, p]
        held[t, rows - reach : rows, :] = near[:, p]
        held[t, rows : rows + reach, :] = far[:, p]
        held[t, rows + reach : tall, :] = edge[0:two, p]
    me = lax.axis_index("mem")
    seg = LANES // count
    lane = lane_iota((SUB, LANES))
    lanes = lane_iota((tall, LANES))
    for d in range(count):
        q = me ^ d
        quarter = jnp.zeros((tall, LANES), F32)
        for t in range(tiles):
            turned = pltpu.roll(held[t], lax.rem(t - q + count, count) * seg, 1)
            quarter = jnp.where(lanes // seg == t, turned, quarter)
        out, at = (outs[d // 2], 0) if d % 2 == 0 else (outs[-1], d // 2 * (tall + SUB))
        out[at : at + tall, :] = quarter
        packed = jnp.zeros((SUB, LANES), F32)
        for k in range(tall // SUB):
            rows8 = slice(k * SUB, (k + 1) * SUB)
            turn = 2 * k + 1 + LANES - q * seg
            left = pltpu.roll(held[tiles - 1, rows8, :], lax.rem(turn, LANES), 1)
            right = pltpu.roll(held[0, rows8, :], lax.rem(turn + LANES - seg, LANES), 1)
            packed = jnp.where(lane == 2 * k, left, packed)
            packed = jnp.where(lane == 2 * k + 1, right, packed)
        west = jnp.where(q > 0, 1.0, 0.0).astype(F32)
        east = jnp.where(q < count - 1, 1.0, 0.0).astype(F32)
        out[at + tall : at + tall + SUB, :] = packed * jnp.where(lane % 2 == 0, west, east)


def add_quarters(*refs):
    *pieces, out, below = refs
    total = pieces[0][...]
    for piece in pieces[1:]:
        total = total + piece[0 : out.shape[0], :]
    out[...] = total
    below[...] = total[out.shape[0] - below.shape[0] :, :]


def ref_end(ref):
    return ref[ref.shape[0] - SUB :, :]


def finish(total_ref, above, static, table, out, held, wide, *, count, fields):
    height = table.shape[1]
    rows, cols = out.shape[1:]
    breadth = table.shape[2]
    lane = lane_iota((SUB, LANES))
    seg = LANES // count
    mine = height * fields // SUB
    reach = SPREAD_PASSES * fields // SUB

    def block(ref, number):
        return ref[number * SUB : (number + 1) * SUB, :]

    borders = ref_end(total_ref), ref_end(above)
    terms = [[(1, 0, mine - 1)]]
    for k in range(mine):
        terms.append([(0, k, k)] + ([(1, k + 1, mine + k)] if k < reach else []))
    terms.append([(0, mine, mine), (0, mine + reach, mine + reach)])
    for number, parts in enumerate(terms):
        x = left = right = 0.0
        for source, at, k in parts:
            x = x + block((total_ref, above)[source], at)
            packed = borders[source]
            left = left + (pltpu.roll(packed, LANES - 2 * k, 1) if k else packed)
            right = right + pltpu.roll(packed, LANES - 2 - 2 * k, 1)
        rows8 = slice(number * SUB, (number + 1) * SUB)
        held[0, rows8, :] = x
        before = jnp.where(lane == 0, left, pltpu.roll(x, seg + 1, 1))
        held[1, rows8, :] = jnp.where(lane < seg, before, pltpu.roll(x, seg, 1))
        after = jnp.where(lane == LANES - 1, right, pltpu.roll(x, LANES - seg - 1, 1))
        held[2, rows8, :] = jnp.where(lane >= LANES - seg, after, pltpu.roll(x, LANES - seg, 1))
    for f in range(fields):
        for p in range(2):
            even = jnp.zeros((height, breadth), F32)
            odd = jnp.zeros((height, breadth), F32)
            for a, off in ((1 + p, 0), (3 - 3 * p, 2 * p - 1)):
                at = pl.ds(f + fields * (2 + off), height, stride=fields)
                here = held[0, at, :]
                even = even + table[4 * a + 1] * here + table[4 * a + 3] * held[1, at, :]
                odd = odd + table[4 * a + 2] * here + table[4 * a] * held[2, at, :]
            at = pl.ds(f * rows + p, height, stride=2)
            wide[0, at, :] = even
            wide[1, at, :] = odd
    both = jnp.concatenate([wide[0], wide[1]], axis=1)
    fine = reorder(both, spread_columns(cols, count))
    for f in range(fields):
        out[f] = static[f] + fine[f * rows : (f + 1) * rows, :]


def groups_of(pairs):
    first = max(1, pairs // 5)
    sizes = (first, pairs - first - 1, 1)
    return [(sum(sizes[:g]), size) for g, size in enumerate(sizes)]


def local(gradient, static_scale, static_rate, interp_index, interp_weight, members, spread_rate):
    fields, rows, cols = gradient.shape
    slots, height, breadth = interp_index.shape
    member_count, _, _, width = members.shape
    reach = SPREAD_PASSES
    tiles = lax.axis_size("tile")
    count = lax.axis_size("mem")
    upward = [(i + 1, i) for i in range(tiles - 1)]
    downward = [(i, i + 1) for i in range(tiles - 1)]
    rings = [[(i, (i + d) % count) for i in range(count)] for d in range(count)]
    per = SUB // fields
    pairs = member_count // per
    vmem = pl.BlockSpec(memory_space=pltpu.VMEM)
    smem = pl.BlockSpec(memory_space=pltpu.SMEM)
    smalls = (gradient, static_scale, interp_index, interp_weight, spread_rate)
    column_parts = width // cols
    order = permutation(width)

    groups = groups_of(pairs)
    last = groups[-1][1]
    line = (SUB, width)
    lane_tiles = width // LANES
    size = SUB * reach
    number = groups[0][1]

    up, down, kept, first = call(
        pack_tile,
        [
            (fields * 24 + slots * 8 + column_parts * 8, cols),
            (fields * 8 + (slots + column_parts * 4 + 7) // 8 * 8, cols),
            ((slots + column_parts) * height, cols),
            (number * size, width),
        ],
        [pltpu.VMEM(x.shape, x.dtype) for x in smalls]
        + [
            pltpu.VMEM((per * number,) + members.shape[1:], members.dtype),
            pltpu.SemaphoreType.DMA((6,)),
        ],
        in_specs=[pl.BlockSpec(memory_space=pltpu.HBM)] * 6,
        limit=(VMEM_BYTES - members.size * members.dtype.itemsize * 17 // 16) / (1 << 20),
        name="pack_tile",
    )(*smalls, members)
    first = lax.ppermute(first, "tile", upward)
    down = lax.ppermute(down, "tile", downward)
    up = lax.ppermute(up, "tile", upward)
    members, *firsts = call(
        functools.partial(arrange, pairs=pairs, groups=groups[1:-1]),
        [(pairs, height) + line] + [(n * size, width) for _, n in groups[1:-1]],
        [(lane_tiles, pairs * SUB * height, LANES)],
        limit=8,
        name="arrange",
    )(members, order)
    far_rows = [first] + [lax.ppermute(rows_k, "tile", upward) for rows_k in firsts]

    tall = height + reach
    quarter, rates = call(
        functools.partial(restrict, slots=slots),
        [(fields * tall + 64, breadth), (height + 16, width)],
        [(64, cols), (4, 64, breadth), (64, LANES)],
        name="restrict",
    )(gradient, static_scale, kept, up, down)
    pieces = [quarter] + [lax.ppermute(quarter, "mem", rings[d]) for d in range(1, count)]

    static, table = call(
        functools.partial(side, members_all=member_count * count),
        [(fields, rows, cols), (16, height, breadth)],
        [
            (rows + 16, cols + 2 * LANES),
            (slots, height + 16, breadth),
            (slots, height + 16, breadth),
            (height + 16, breadth),
        ],
        in_specs=[vmem, vmem, smem] + [vmem] * 5,
        name="side",
    )(gradient, static_scale, static_rate, kept, up, down, pieces[1], pieces[-1])

    two = 2 * fields
    own_sum, beyond, far_coarse, rates, message = call(
        functools.partial(own, count=count, fields=fields, pairs=pairs, last=last),
        [
            (height * fields, width),
            (pairs, reach) + line,
            (reach,) + line,
            rates.shape,
            (two + last * size, width),
        ],
        [
            (height + reach + 6,) + line,
            (height + 12,) + line,
            (height + 12,) + line,
            (height,) + line,
            (fields * tall, width),
            (lane_tiles, fields * tall, LANES),
            (height,) + line,
            (count, 64, LANES),
        ],
        limit=8,
        name="own",
    )(members, rates, order, *pieces)
    message = lax.ppermute(message, "tile", upward)
    far_rows.append(message)

    nears, fars = [], []
    for k, (g, n) in enumerate(groups):
        near, far = call(
            functools.partial(
                cross,
                fields=fields,
                begin=g,
                number=n,
                skip=two if k == len(groups) - 1 else 0,
                arranged=k > 0,
            ),
            [(reach * fields, width)] * 2,
            [
                (2 * reach,) + line,
                (2 * reach,) + line,
                (reach,) + line,
                (reach,) + line,
                (lane_tiles, size if k else n * size, LANES),
            ],
            limit=4,
            name="cross",
        )(far_rows[k], members, beyond, far_coarse, rates, order)
        nears.append(near)
        fars.append(far)

    high = (height + reach) * fields + two + SUB
    *kept_sums, leaving = call(
        functools.partial(pack_sums, groups=len(groups), count=count, fields=fields),
        [(high, breadth)] * (count // 2) + [(count // 2 * high, breadth)],
        [(lane_tiles, high - SUB, LANES)],
        name="pack_sums",
    )(own_sum, message, *nears, *fars)
    assert count == 4
    came = lax.ppermute(leaving, "mem", [(i, i ^ 1) for i in range(count)])
    going = kept_sums[1] + came[high:]
    last_came = lax.ppermute(going, "mem", [(i, i ^ 2) for i in range(count)])
    total, below = call(
        add_quarters,
        [(high, breadth), (high - (height * fields - SUB), breadth)],
        name="add_quarters",
    )(kept_sums[0], came, last_came)
    from_above = lax.ppermute(below, "tile", downward)
    (hybrid,) = call(
        functools.partial(finish, count=count, fields=fields),
        [(fields, rows, cols)],
        [(3, (height + 4) * fields, LANES), (2, fields * rows, breadth)],
        name="finish",
    )(total, from_above, static, table)
    return hybrid


def solution(mesh):
    return jax.shard_map(
        local,
        mesh=mesh,
        in_specs=(
            P(None, "tile", "mem"),
            P(None, "tile", "mem"),
            P(),
            P(None, "tile", "mem"),
            P(None, "tile", "mem"),
            P("mem", None, "tile", None),
            P("tile", None),
        ),
        out_specs=P(None, "tile", "mem"),
        check_vma=False,
    )
```

```python
import functools

import jax
import jax.numpy as jnp
from jax import lax
from jax.experimental import pallas as pl
from jax.experimental.pallas import tpu as pltpu
from jax.sharding import PartitionSpec as P


STATIC_PASSES = 4
SPREAD_PASSES = 8
LANES = 128
SUB = 8
VMEM_BYTES = 67043328


F32 = jnp.float32
EXACT = lax.Precision.HIGHEST


def call(kernel, out_shapes, scratch=(), limit=4, **kw):
    return pl.pallas_call(
        kernel,
        out_shape=tuple(jax.ShapeDtypeStruct(s, F32) for s in out_shapes),
        scratch_shapes=[pltpu.VMEM(s, F32) if isinstance(s, tuple) else s for s in scratch],
        compiler_params=pltpu.CompilerParams(vmem_limit_bytes=int(limit * (1 << 20))),
        **kw,
    )


def pack_tile(*refs):
    sources, (up, down, kept, first), held, done = refs[:6], refs[6:10], refs[10:16], refs[16]
    number = held[5].shape[0]
    sources = sources[:5] + (sources[5].at[0:number],)
    copies = [
        pltpu.make_async_copy(source, target, done.at[k])
        for k, (source, target) in enumerate(zip(sources, held))
    ]
    for copy in copies:
        copy.start()
    for copy in copies:
        copy.wait()
    grad, scale, index, weight, rate, members = held
    first[...] = members[:, :, 0:SPREAD_PASSES, :].astype(F32).reshape(first.shape)
    fields, rows, cols = grad.shape
    slots, height, breadth = index.shape
    parts = rate.shape[1] // cols
    reach = SPREAD_PASSES
    up[...] = jnp.zeros(up.shape, F32)
    down[...] = jnp.zeros(down.shape, F32)
    for f in range(fields):
        top = 2 * reach + 1
        up[f * 24 : f * 24 + top, :] = grad[f, 0:top, :]
        up[f * 24 + top : f * 24 + top + STATIC_PASSES, :] = (
            scale[f, 0:STATIC_PASSES, :] * grad[f, 0:STATIC_PASSES, :]
        )
        down[f * 8 : f * 8 + 1, :] = grad[f, rows - 1 : rows, :]
        down[f * 8 + 1 : f * 8 + 1 + STATIC_PASSES, :] = (
            scale[f, rows - STATIC_PASSES : rows, :] * grad[f, rows - STATIC_PASSES : rows, :]
        )
    base = fields * 24
    low = fields * 8
    for s in range(slots):
        up[base + s * 8 : base + s * 8 + 8, 0:breadth] = index[s, 0:8, :].astype(F32)
        up[base + s * 8 : base + s * 8 + 8, breadth:] = weight[s, 0:8, :]
        down[low + s : low + s + 1, 0:breadth] = index[s, height - 1 : height, :].astype(F32)
        down[low + s : low + s + 1, breadth:] = weight[s, height - 1 : height, :]
    base += slots * 8
    low += slots
    for p in range(parts):
        part = slice(p * cols, (p + 1) * cols)
        up[base + p * 8 : base + p * 8 + 8, :] = rate[0:8, part]
        down[low + p * 4 : low + p * 4 + 4, :] = rate[height - 4 : height, part]
        kept[(slots + p) * height : (slots + p + 1) * height, :] = rate[:, part]
    for s in range(slots):
        kept[s * height : (s + 1) * height, 0:breadth] = index[s].astype(F32)
        kept[s * height : (s + 1) * height, breadth:] = weight[s]


def lane_iota(shape):
    return lax.broadcasted_iota(jnp.int32, shape, len(shape) - 1)


def pick_columns(cols):
    source = lax.broadcasted_iota(jnp.int32, (cols, cols), 0)
    target = lax.broadcasted_iota(jnp.int32, (cols, cols), 1)
    half = cols // 2
    wanted = jnp.where(target < half, 2 * target, 2 * (target - half) + 1)
    return jnp.where(source == wanted, 1.0, 0.0).astype(F32)


def quarter_column(lane, count):
    seg = LANES // count
    return count * (lane % seg) + lane // seg


def spread_columns(cols, count):
    source = lax.broadcasted_iota(jnp.int32, (cols, cols), 0)
    target = lax.broadcasted_iota(jnp.int32, (cols, cols), 1)
    half = cols // 2
    wanted = 2 * quarter_column(source % half, count) + source // half
    return jnp.where(target == wanted, 1.0, 0.0).astype(jnp.bfloat16)


def table_rows(index, weight):
    rows = []
    for o in range(16):
        total = jnp.zeros(index[0].shape, F32)
        for i, w in zip(index, weight):
            total = total + jnp.where(i == float(o), w, 0.0)
        rows.append(total)
    return rows


def slots_of(kept, height, breadth, slots):
    rows = [slice(s * height, (s + 1) * height) for s in range(slots)]
    return [kept[r, 0:breadth] for r in rows], [kept[r, breadth:] for r in rows]


def restrict(grad, scale, kept, up, down, out, rate_out, ext, cols4, edge, *, slots):
    fields, rows, cols = grad.shape
    height, breadth = rows // 2, cols // 2
    parts = kept.shape[0] // height - slots
    index, weight = slots_of(kept, height, breadth, slots)
    n = STATIC_PASSES
    top = 2 * SPREAD_PASSES + 1
    tall = height + SPREAD_PASSES
    base = fields * 24
    low = fields * 8
    table = table_rows(
        [
            jnp.concatenate(
                [index[s], up[base + s * 8 : base + s * 8 + 8, 0:breadth]], axis=0
            )
            for s in range(slots)
        ],
        [
            jnp.concatenate([weight[s], up[base + s * 8 : base + s * 8 + 8, breadth:]], axis=0)
            for s in range(slots)
        ],
    )
    pick = pick_columns(cols)
    ext[...] = jnp.zeros(ext.shape, F32)
    edge[...] = jnp.zeros(edge.shape, F32)
    lane = lane_iota((ext.shape[0], breadth))
    for f in range(fields):
        ext[8 : 8 + rows, :] = grad[f]
        ext[7:8, :] = down[f * 8 : f * 8 + 1, :]
        ext[8 + rows : 8 + rows + top, :] = up[f * 24 : f * 24 + top, :]
        edge[:, 16 + f : 17 + f] = ext[:, 0:1]
        edge[:, 80 + f : 81 + f] = ext[:, cols - 1 : cols]
        both = jnp.dot(ext[...], pick, precision=EXACT, preferred_element_type=F32)
        even = both[:, :breadth]
        odd = both[:, breadth:]
        cols4[0] = jnp.where(lane == 0, 0.0, pltpu.roll(odd, 1, 1))
        cols4[1] = even
        cols4[2] = odd
        cols4[3] = jnp.where(lane == breadth - 1, 0.0, pltpu.roll(even, breadth - 1, 1))
        total = jnp.zeros((tall, breadth), F32)
        for a in range(4):
            for b in range(4):
                total = total + table[4 * a + b] * cols4[b, pl.ds(a + 7, tall, stride=2), :]
        out[f * tall : (f + 1) * tall, :] = total
    for at, wide, lone in ((0, 0, 0), (64, cols - n, breadth - 1)):
        for f in range(fields):
            lanes = slice(at + 4 * f, at + 4 * f + n)
            columns = slice(wide, wide + n)
            edge[8 : 8 + rows, lanes] = scale[f, :, columns] * grad[f, :, columns]
            edge[8 - n : 8, lanes] = down[f * 8 + 1 : f * 8 + 1 + n, columns]
            edge[8 + rows : 8 + rows + n, lanes] = up[f * 24 + top : f * 24 + top + n, columns]
        one = slice(lone, lone + 1)
        second = slice(breadth + lone, breadth + lone + 1)
        for s in range(slots):
            lanes = slice(at + 32 + s, at + 33 + s)
            edge[8 : 8 + height, lanes] = index[s][:, one]
            edge[7:8, lanes] = down[low + s : low + s + 1, one]
            edge[8 + height : 9 + height, lanes] = up[base + s * 8 : base + s * 8 + 1, one]
            lanes = slice(at + 36 + s, at + 37 + s)
            edge[8 : 8 + height, lanes] = weight[s][:, one]
            edge[7:8, lanes] = down[low + s : low + s + 1, second]
            edge[8 + height : 9 + height, lanes] = up[base + s * 8 : base + s * 8 + 1, second]
        for a in range(4):
            entry = table[4 * a] if at == 0 else table[4 * a + 3]
            edge[8 : 8 + tall, at + 40 + a : at + 41 + a] = entry[:, one]
    out[fields * tall :, :] = edge[...]
    base = fields * 24 + slots * 8
    low = fields * 8 + slots
    rate_out[0:4, :] = jnp.zeros((4, rate_out.shape[1]), F32)
    for p in range(parts):
        part = slice(p * cols, (p + 1) * cols)
        rate_out[8 : 8 + height, part] = kept[(slots + p) * height : (slots + p + 1) * height, :]
        rate_out[4:8, part] = down[low + p * 4 : low + p * 4 + 4, :]
        rate_out[8 + height : 16 + height, part] = up[base + p * 8 : base + p * 8 + 8, :]


def side(grad, scale, stat_rate, kept, up, down, west_message, east_message,
         static, table_out, box, idx, wgt, tab, *, members_all):
    fields, rows, cols = grad.shape
    slots, (height, breadth) = idx.shape[0], table_out.shape[1:]
    index, weight = slots_of(kept, height, breadth, slots)
    n = STATIC_PASSES
    top = 2 * SPREAD_PASSES + 1
    me = lax.axis_index("mem")
    skip = fields * (height + SPREAD_PASSES)
    from_west = jnp.where(me > 0, pltpu.roll(west_message[skip:, :], 64, 1), 0.0)
    from_east = jnp.where(me < lax.axis_size("mem") - 1, east_message[skip:, :], 0.0)
    wide = cols + LANES
    deep = rows + 2 * n
    shape = (deep, wide)
    row = lax.broadcasted_iota(jnp.int32, shape, 0)
    col = lane_iota(shape)
    tile = lax.axis_index("tile")
    after_row = jnp.where(tile == lax.axis_size("tile") - 1, rows, rows + n)
    before_row = jnp.where(tile == 0, deep, rows + n)
    after_col = jnp.where(me == lax.axis_size("mem") - 1, cols, cols + n)
    before_col = jnp.where(me == 0, wide, wide - n)
    inside_row = jnp.where(row < after_row, 1.0, 0.0) + jnp.where(row >= before_row, 1.0, 0.0)
    inside_col = jnp.where(col < after_col, 1.0, 0.0) + jnp.where(col >= before_col, 1.0, 0.0)
    inside = inside_row * inside_col
    for f in range(fields):
        box[...] = jnp.zeros(box.shape, F32)
        box[0:rows, 0:cols] = scale[f] * grad[f]
        box[rows : rows + n, 0:cols] = up[f * 24 + top : f * 24 + top + n, :]
        box[rows + n : deep, 0:cols] = down[f * 8 + 1 : f * 8 + 1 + n, :]
        for message, at in ((from_east, cols), (from_west, wide - n)):
            lanes = slice(4 * f, 4 * f + n)
            box[0 : rows + n, at : at + n] = message[8 : 8 + rows + n, lanes]
            box[rows + n : deep, at : at + n] = message[8 - n : 8, lanes]
        field = box[...]
        rate = stat_rate[f] * inside
        for _ in range(n):
            beside = (
                pltpu.roll(field, 1, 0)
                + pltpu.roll(field, deep - 1, 0)
                + pltpu.roll(field, 1, 1)
                + pltpu.roll(field, wide - 1, 1)
            )
            field = field + rate * (beside - 4.0 * field)
        static[f] = 0.3 * scale[f] * field[0:rows, 0:cols]
    factor = 2.8 / (members_all - 1)
    base = fields * 24
    low = fields * 8
    tall = height + 16
    lane = lane_iota((tall, breadth))
    for s in range(slots):
        idx[s] = jnp.zeros((tall, breadth), F32)
        wgt[s] = jnp.zeros((tall, breadth), F32)
        idx[s, 8 : 8 + height, :] = index[s]
        wgt[s, 8 : 8 + height, :] = weight[s]
        idx[s, 7:8, :] = down[low + s : low + s + 1, 0:breadth]
        wgt[s, 7:8, :] = down[low + s : low + s + 1, breadth:]
        idx[s, 8 + height : 9 + height, :] = up[base + s * 8 : base + s * 8 + 1, 0:breadth]
        wgt[s, 8 + height : 9 + height, :] = up[base + s * 8 : base + s * 8 + 1, breadth:]
    west = from_west[0:tall, :]
    east = from_east[0:tall, :]

    def shifted(x, shift, at):
        if shift == 1:
            return jnp.where(lane == 0, pltpu.roll(west, LANES - at, 1), pltpu.roll(x, 1, 1))
        if shift == 2:
            return jnp.where(
                lane == breadth - 1,
                pltpu.roll(east, LANES - 1 - at, 1),
                pltpu.roll(x, breadth - 1, 1),
            )
        return x

    for shift, columns in ((0, (1, 2)), (1, (3,)), (2, (0,))):
        table = table_rows(
            [shifted(idx[s], shift, 32 + s) for s in range(slots)],
            [shifted(wgt[s], shift, 36 + s) for s in range(slots)],
        )
        for b in columns:
            for a in range(4):
                off = (1, 0, 0, -1)[a]
                tab[...] = factor * table[4 * a + b]
                table_out[4 * a + b] = tab[8 + off : 8 + off + height, :]
    source = lax.broadcasted_iota(jnp.int32, (breadth, breadth), 0)
    target = lax.broadcasted_iota(jnp.int32, (breadth, breadth), 1)
    order = jnp.where(source == quarter_column(target, lax.axis_size("mem")), 1.0, 0.0)
    flat = reorder(table_out[...].reshape(16 * height, breadth), order.astype(jnp.bfloat16))
    table_out[...] = flat.reshape(16, height, breadth)


def parts_of(width):
    return [slice(t, t + LANES) for t in range(0, width, LANES)]


def sweep(v, keep, rate, lo, hi, v_at, rate_at):
    parts = parts_of(v.shape[2])
    lane = lane_iota((SUB, LANES))

    def right_below(here, below):
        right = jnp.where(lane == LANES - 1, 0.0, pltpu.roll(here[0], LANES - 1, 1))
        return [x + y for x, y in zip(here[1:] + [right], below)]

    above = [v[lo - 1 + v_at, :, p] for p in parts]
    here = [v[lo + v_at, :, p] for p in parts]
    after = right_below(above, here)
    for r in range(lo, hi):
        below = [v[r + 1 + v_at, :, p] for p in parts]
        first = jnp.where(lane == 0, 0.0, pltpu.roll(here[-1], 1, 1)) + above[0]
        before = [first] + after[:-1]
        after = right_below(here, below)
        for t, p in enumerate(parts):
            total = before[t] + after[t]
            v[r + v_at, :, p] = keep[r + rate_at, :, p] * here[t] + rate[r + rate_at, :, p] * total
        above, here = here, below


def climb(rows, keep, rate, lo, rate_at):
    tiles = len(rows[0])
    lane = lane_iota((SUB, LANES))
    parts = parts_of(tiles * LANES)
    result = []
    above = here = after = None
    for k, below in enumerate(rows):
        r = lo + k + rate_at
        if here is None:
            result.append([rate[r, :, p] * x for p, x in zip(parts, below)])
            above, here, after = None, below, list(below)
            continue
        left = jnp.where(lane == 0, 0.0, pltpu.roll(here[-1], 1, 1))
        first = left if above is None else left + above[0]
        before = [first] + after[: tiles - 1] if above is not None else [first] + here[: tiles - 1]
        right = jnp.where(lane == LANES - 1, 0.0, pltpu.roll(here[0], LANES - 1, 1))
        after = [x + y for x, y in zip(here[1:] + [right], below)]
        result.append(
            [
                keep[r, :, p] * here[t] + rate[r, :, p] * (before[t] + after[t])
                for t, p in enumerate(parts)
            ]
        )
        above, here = here, below
    return result


def permutation(width):
    source = lax.broadcasted_iota(jnp.int32, (width, width), 0)
    target = lax.broadcasted_iota(jnp.int32, (width, width), 1)
    tiles = width // LANES
    return jnp.where(source == tiles * (target % LANES) + target // LANES, 1.0, 0.0).astype(
        jnp.bfloat16
    )


def reorder(x, order, contract=0):
    dims = (((1,), (contract,)), ((), ()))
    high = x.astype(jnp.bfloat16)
    rest = x - high.astype(F32)
    middle = rest.astype(jnp.bfloat16)
    low = (rest - middle.astype(F32)).astype(jnp.bfloat16)
    moved = [
        lax.dot_general(y, order, dims, preferred_element_type=F32) for y in (high, middle, low)
    ]
    return moved[0] + (moved[1] + moved[2])


def arrange(members, order, *refs, pairs, groups):
    held, firsts, moved_rows = refs[0], refs[1:-1], refs[-1]
    per = members.shape[0] // pairs
    height, width = members.shape[2:]
    rows = SUB * height
    for b in range(0, pairs, 2):
        n = min(2, pairs - b)
        block = members[b * per : (b + n) * per].reshape(n * rows, width)
        moved = jnp.dot(block, order[...], preferred_element_type=F32)
        for t, p in enumerate(parts_of(width)):
            moved_rows[t, b * rows : (b + n) * rows, :] = moved[:, p]
            for i in range(b, b + n):
                outs = [(out, g) for out, (g, m) in zip(firsts, groups) if g <= i < g + m]
                for r in range(height):
                    line = moved_rows[t, pl.ds(i * rows + r, SUB, stride=height), :]
                    held[i, r, :, p] = line
                    if r < SPREAD_PASSES:
                        for out, g in outs:
                            at = ((i - g) * SPREAD_PASSES + r) * SUB
                            out[at : at + SUB, p] = line


def fill_rates(rate_ref, keep, rate, rows, at):
    for r in range(rows):
        line = jnp.broadcast_to(rate_ref[r + at : r + at + 1, :], rate.shape[1:])
        rate[r] = line
        keep[r] = 1.0 - 4.0 * line


def spread_rates(rate_ref, order, keep, rate, moved):
    moved[...] = reorder(rate_ref[...], order[...])
    fill_rates(moved, keep, rate, rate.shape[0], 4)


def fold(total, fields):
    folded = total[0:fields]
    for j in range(fields, SUB, fields):
        folded = folded + total[j : j + fields]
    return folded


def own(*refs, count, fields, pairs, last):
    members, keep, rate, order = refs[0:4]
    pieces = refs[4 : 4 + count]
    own_out, beyond, far_coarse, message = refs[4 + count : 8 + count]
    v, c, cw, cp, acc, eb = refs[8 + count :]
    height = c.shape[0]
    reach = SPREAD_PASSES
    tall = height + reach
    parts = parts_of(v.shape[2])

    me = lax.axis_index("mem")
    for d, piece in enumerate(pieces):
        breadth = piece.shape[1]
        where = lax.rem(me - d + count, count)
        at = pl.ds(pl.multiple_of(where * breadth, LANES), breadth)
        cw[:, at] = piece[0 : fields * tall, :]
        eb[where] = piece[fields * tall :, :]
    lane = lane_iota((tall, LANES))
    for q in range(count - 1):
        last_column = (q + 1) * breadth - 1
        for mine, other, table_at, grad_at, goal in (
            (q, q + 1, 104, 16, last_column),
            (q + 1, q, 40, 80, last_column + 1),
        ):
            added = jnp.zeros((tall, LANES), F32)
            for a in range(4):
                entry = eb[mine, 8 : 8 + tall, table_at + a : table_at + a + 1]
                added = added + entry * eb[other, pl.ds(a + 7, tall, stride=2), :]
            begin = goal // LANES * LANES
            for f in range(fields):
                turn = (goal - begin - grad_at - f) % LANES
                here = jnp.where(lane == goal - begin, pltpu.roll(added, turn, 1), 0.0)
                rows = slice(f * tall, (f + 1) * tall)
                cw[rows, begin : begin + LANES] = cw[rows, begin : begin + LANES] + here
    moved = reorder(cw[...], order[...])
    for t, p in enumerate(parts):
        cp[t] = moved[:, p]
        for r in range(tall):
            row = cp[t, pl.ds(r, fields, stride=tall), :]
            for j in range(0, SUB, fields):
                if r < height:
                    c[r, j : j + fields, p] = row
                else:
                    far_coarse[r - height, j : j + fields, p] = row
    acc[...] = jnp.zeros(acc.shape, F32)
    off = 5

    def one(i, _):
        v[0:off] = jnp.zeros((off,) + v.shape[1:], F32)
        v[height + off :] = jnp.zeros((v.shape[0] - height - off,) + v.shape[1:], F32)
        for r in range(height):
            v[r + off] = members[i, r] * c[r]
        for s in range(1, SPREAD_PASSES + 1):
            sweep(v, keep, rate, -min(s, SPREAD_PASSES - s), height + s, off, 4)
        for r in range(height):
            acc[r] = acc[r] + members[i, r] * v[r + off]
        for r in range(reach):
            beyond[i, r] = v[r + height + off]
        return _

    lax.fori_loop(0, pairs, one, 0)
    for r in range(height):
        own_out[r * fields : (r + 1) * fields, :] = fold(acc[r], fields)
    two = 2 * fields
    message[0:two, :] = own_out[0:two, :]
    for j in range(last):
        for r in range(reach):
            at = two + (j * reach + r) * SUB
            message[at : at + SUB, :] = members[pairs - last + j, r]


def cross(far_rows, members, beyond, far_coarse, keep, rate, order, near_out, far_out,
          near, far, fw, *, fields, begin, number, skip, arranged):
    reach = SPREAD_PASSES
    height = members.shape[1]
    parts = parts_of(order.shape[1])
    near[...] = jnp.zeros(near.shape, F32)
    far[...] = jnp.zeros(far.shape, F32)
    size = SUB * reach
    if not arranged:
        moved = jnp.dot(
            far_rows[...].astype(jnp.bfloat16), order[...], preferred_element_type=F32
        )
        for t, p in enumerate(parts):
            fw[t] = moved[:, p]

    def one(i, x):
        window = [[None] * len(parts) for _ in range(reach)]
        for t, p in enumerate(parts):
            for r in range(reach):
                if arranged:
                    at = pl.multiple_of(skip + i * size + r * SUB, SUB)
                    line = far_rows[pl.ds(at, SUB), p]
                else:
                    line = fw[t, pl.ds(i * size + r, SUB, stride=reach), :]
                window[r][t] = line * far_coarse[r, :, p]
                far[r, :, p] = far[r, :, p] + line * beyond[begin + i, r, :, p]
        for s in range(1, SPREAD_PASSES + 1):
            window = climb(window, keep, rate, height - s, 4)
        for r in range(reach):
            for t, p in enumerate(parts):
                line = members[begin + i, height - reach + r, :, p]
                near[r, :, p] = near[r, :, p] + line * window[r][t]
        return x

    if arranged:
        lax.fori_loop(0, number, one, 0)
    else:
        for i in range(number):
            one(i, 0)
    for r in range(reach):
        near_out[r * fields : (r + 1) * fields, :] = fold(near[r], fields)
        far_out[r * fields : (r + 1) * fields, :] = fold(far[r], fields)


def pack_sums(*refs, groups, count, fields):
    own_ref, edge = refs[:2]
    nears = refs[2 : 2 + groups]
    fars = refs[2 + groups : 2 + 2 * groups]
    outs, held = refs[2 + 2 * groups : -1], refs[-1]
    rows = own_ref.shape[0]
    tiles, tall = held.shape[:2]
    two = 2 * fields
    reach = SPREAD_PASSES * fields
    near = nears[0][...]
    far = fars[0][...]
    for x, y in zip(nears[1:], fars[1:]):
        near = near + x[...]
        far = far + y[...]
    near = near + own_ref[rows - reach : rows, :]
    for t, p in enumerate(parts_of(own_ref.shape[1])):
        held[t, 0 : rows - reach, :] = own_ref[0 : rows - reach, p]
        held[t, rows - reach : rows, :] = near[:, p]
        held[t, rows : rows + reach, :] = far[:, p]
        held[t, rows + reach : tall, :] = edge[0:two, p]
    me = lax.axis_index("mem")
    seg = LANES // count
    lane = lane_iota((SUB, LANES))
    lanes = lane_iota((tall, LANES))
    for d in range(count):
        q = me ^ d
        quarter = jnp.zeros((tall, LANES), F32)
        for t in range(tiles):
            turned = pltpu.roll(held[t], lax.rem(t - q + count, count) * seg, 1)
            quarter = jnp.where(lanes // seg == t, turned, quarter)
        out, at = (outs[d // 2], 0) if d % 2 == 0 else (outs[-1], d // 2 * (tall + SUB))
        out[at : at + tall, :] = quarter
        packed = jnp.zeros((SUB, LANES), F32)
        for k in range(tall // SUB):
            rows8 = slice(k * SUB, (k + 1) * SUB)
            turn = 2 * k + 1 + LANES - q * seg
            left = pltpu.roll(held[tiles - 1, rows8, :], lax.rem(turn, LANES), 1)
            right = pltpu.roll(held[0, rows8, :], lax.rem(turn + LANES - seg, LANES), 1)
            packed = jnp.where(lane == 2 * k, left, packed)
            packed = jnp.where(lane == 2 * k + 1, right, packed)
        west = jnp.where(q > 0, 1.0, 0.0).astype(F32)
        east = jnp.where(q < count - 1, 1.0, 0.0).astype(F32)
        out[at + tall : at + tall + SUB, :] = packed * jnp.where(lane % 2 == 0, west, east)


def add_quarters(*refs):
    *pieces, out, below = refs
    total = pieces[0][...]
    for piece in pieces[1:]:
        total = total + piece[0 : out.shape[0], :]
    out[...] = total
    below[...] = total[out.shape[0] - below.shape[0] :, :]


def ref_end(ref):
    return ref[ref.shape[0] - SUB :, :]


def finish(total_ref, above, static, table, out, held, wide, *, count, fields):
    height = table.shape[1]
    rows, cols = out.shape[1:]
    breadth = table.shape[2]
    lane = lane_iota((SUB, LANES))
    seg = LANES // count
    mine = height * fields // SUB
    reach = SPREAD_PASSES * fields // SUB

    def block(ref, number):
        return ref[number * SUB : (number + 1) * SUB, :]

    borders = ref_end(total_ref), ref_end(above)
    terms = [[(1, 0, mine - 1)]]
    for k in range(mine):
        terms.append([(0, k, k)] + ([(1, k + 1, mine + k)] if k < reach else []))
    terms.append([(0, mine, mine), (0, mine + reach, mine + reach)])
    for number, parts in enumerate(terms):
        x = left = right = 0.0
        for source, at, k in parts:
            x = x + block((total_ref, above)[source], at)
            packed = borders[source]
            left = left + (pltpu.roll(packed, LANES - 2 * k, 1) if k else packed)
            right = right + pltpu.roll(packed, LANES - 2 - 2 * k, 1)
        rows8 = slice(number * SUB, (number + 1) * SUB)
        held[0, rows8, :] = x
        before = jnp.where(lane == 0, left, pltpu.roll(x, seg + 1, 1))
        held[1, rows8, :] = jnp.where(lane < seg, before, pltpu.roll(x, seg, 1))
        after = jnp.where(lane == LANES - 1, right, pltpu.roll(x, LANES - seg - 1, 1))
        held[2, rows8, :] = jnp.where(lane >= LANES - seg, after, pltpu.roll(x, LANES - seg, 1))
    for f in range(fields):
        for p in range(2):
            even = jnp.zeros((height, breadth), F32)
            odd = jnp.zeros((height, breadth), F32)
            for a, off in ((1 + p, 0), (3 - 3 * p, 2 * p - 1)):
                at = pl.ds(f + fields * (2 + off), height, stride=fields)
                here = held[0, at, :]
                even = even + table[4 * a + 1] * here + table[4 * a + 3] * held[1, at, :]
                odd = odd + table[4 * a + 2] * here + table[4 * a] * held[2, at, :]
            at = pl.ds(f * rows + p, height, stride=2)
            wide[0, at, :] = even
            wide[1, at, :] = odd
    both = jnp.concatenate([wide[0], wide[1]], axis=1)
    fine = reorder(both, spread_columns(cols, count))
    for f in range(fields):
        out[f] = static[f] + fine[f * rows : (f + 1) * rows, :]


def groups_of(pairs):
    first = max(1, pairs // 5)
    sizes = (first, pairs - first - 1, 1)
    return [(sum(sizes[:g]), size) for g, size in enumerate(sizes)]


def local(gradient, static_scale, static_rate, interp_index, interp_weight, members, spread_rate):
    fields, rows, cols = gradient.shape
    slots, height, breadth = interp_index.shape
    member_count, _, _, width = members.shape
    reach = SPREAD_PASSES
    tiles = lax.axis_size("tile")
    count = lax.axis_size("mem")
    upward = [(i + 1, i) for i in range(tiles - 1)]
    downward = [(i, i + 1) for i in range(tiles - 1)]
    rings = [[(i, (i + d) % count) for i in range(count)] for d in range(count)]
    per = SUB // fields
    pairs = member_count // per
    vmem = pl.BlockSpec(memory_space=pltpu.VMEM)
    smem = pl.BlockSpec(memory_space=pltpu.SMEM)
    smalls = (gradient, static_scale, interp_index, interp_weight, spread_rate)
    column_parts = width // cols
    order = permutation(width)

    groups = groups_of(pairs)
    last = groups[-1][1]
    line = (SUB, width)
    lane_tiles = width // LANES
    size = SUB * reach
    number = groups[0][1]

    up, down, kept, first = call(
        pack_tile,
        [
            (fields * 24 + slots * 8 + column_parts * 8, cols),
            (fields * 8 + (slots + column_parts * 4 + 7) // 8 * 8, cols),
            ((slots + column_parts) * height, cols),
            (number * size, width),
        ],
        [pltpu.VMEM(x.shape, x.dtype) for x in smalls]
        + [
            pltpu.VMEM((per * number,) + members.shape[1:], members.dtype),
            pltpu.SemaphoreType.DMA((6,)),
        ],
        in_specs=[pl.BlockSpec(memory_space=pltpu.HBM)] * 6,
        limit=(VMEM_BYTES - members.size * members.dtype.itemsize * 17 // 16) / (1 << 20),
        name="pack_tile",
    )(*smalls, members)
    first = lax.ppermute(first, "tile", upward)
    down = lax.ppermute(down, "tile", downward)
    up = lax.ppermute(up, "tile", upward)
    members, *firsts = call(
        functools.partial(arrange, pairs=pairs, groups=groups[1:-1]),
        [(pairs, height) + line] + [(n * size, width) for _, n in groups[1:-1]],
        [(lane_tiles, pairs * SUB * height, LANES)],
        limit=8,
        name="arrange",
    )(members, order)
    far_rows = [first] + [lax.ppermute(rows_k, "tile", upward) for rows_k in firsts]

    tall = height + reach
    quarter, rates = call(
        functools.partial(restrict, slots=slots),
        [(fields * tall + 64, breadth), (height + 16, width)],
        [(64, cols), (4, 64, breadth), (64, LANES)],
        name="restrict",
    )(gradient, static_scale, kept, up, down)
    pieces = [quarter] + [lax.ppermute(quarter, "mem", rings[d]) for d in range(1, count)]

    static, table = call(
        functools.partial(side, members_all=member_count * count),
        [(fields, rows, cols), (16, height, breadth)],
        [
            (rows + 2 * STATIC_PASSES, cols + LANES),
            (slots, height + 16, breadth),
            (slots, height + 16, breadth),
            (height + 16, breadth),
        ],
        in_specs=[vmem, vmem, smem] + [vmem] * 5,
        name="side",
    )(gradient, static_scale, static_rate, kept, up, down, pieces[1], pieces[-1])

    two = 2 * fields
    keep, rate = call(
        spread_rates,
        [(height + 12,) + line] * 2,
        [rates.shape],
        name="spread_rates",
    )(rates, order)
    own_sum, beyond, far_coarse, message = call(
        functools.partial(own, count=count, fields=fields, pairs=pairs, last=last),
        [
            (height * fields, width),
            (pairs, reach) + line,
            (reach,) + line,
            (two + last * size, width),
        ],
        [
            (height + reach + 6,) + line,
            (height,) + line,
            (fields * tall, width),
            (lane_tiles, fields * tall, LANES),
            (height,) + line,
            (count, 64, LANES),
        ],
        limit=8,
        name="own",
    )(members, keep, rate, order, *pieces)
    message = lax.ppermute(message, "tile", upward)
    far_rows.append(message)

    nears, fars = [], []
    for k, (g, n) in enumerate(groups):
        near, far = call(
            functools.partial(
                cross,
                fields=fields,
                begin=g,
                number=n,
                skip=two if k == len(groups) - 1 else 0,
                arranged=k > 0,
            ),
            [(reach * fields, width)] * 2,
            [
                (reach,) + line,
                (reach,) + line,
                (lane_tiles, size if k else n * size, LANES),
            ],
            limit=4,
            name="cross",
        )(far_rows[k], members, beyond, far_coarse, keep, rate, order)
        nears.append(near)
        fars.append(far)

    high = (height + reach) * fields + two + SUB
    *kept_sums, leaving = call(
        functools.partial(pack_sums, groups=len(groups), count=count, fields=fields),
        [(high, breadth)] * (count // 2) + [(count // 2 * high, breadth)],
        [(lane_tiles, high - SUB, LANES)],
        name="pack_sums",
    )(own_sum, message, *nears, *fars)
    assert count == 4
    came = lax.ppermute(leaving, "mem", [(i, i ^ 1) for i in range(count)])
    going = kept_sums[1] + came[high:]
    last_came = lax.ppermute(going, "mem", [(i, i ^ 2) for i in range(count)])
    total, below = call(
        add_quarters,
        [(high, breadth), (high - (height * fields - SUB), breadth)],
        name="add_quarters",
    )(kept_sums[0], came, last_came)
    from_above = lax.ppermute(below, "tile", downward)
    (hybrid,) = call(
        functools.partial(finish, count=count, fields=fields),
        [(fields, rows, cols)],
        [(3, (height + 4) * fields, LANES), (2, fields * rows, breadth)],
        name="finish",
    )(total, from_above, static, table)
    return hybrid


def solution(mesh):
    return jax.shard_map(
        local,
        mesh=mesh,
        in_specs=(
            P(None, "tile", "mem"),
            P(None, "tile", "mem"),
            P(),
            P(None, "tile", "mem"),
            P(None, "tile", "mem"),
            P("mem", None, "tile", None),
            P("tile", None),
        ),
        out_specs=P(None, "tile", "mem"),
        check_vma=False,
    )
```

```python
import functools

import jax
import jax.numpy as jnp
from jax import lax
from jax.experimental import pallas as pl
from jax.experimental.pallas import tpu as pltpu
from jax.sharding import PartitionSpec as P


STATIC_PASSES = 4
SPREAD_PASSES = 8
LANES = 128
SUB = 8
VMEM_BYTES = 67043328


F32 = jnp.float32


def call(kernel, out_shapes, scratch=(), limit=4, **kw):
    return pl.pallas_call(
        kernel,
        out_shape=tuple(jax.ShapeDtypeStruct(s, F32) for s in out_shapes),
        scratch_shapes=[pltpu.VMEM(s, F32) if isinstance(s, tuple) else s for s in scratch],
        compiler_params=pltpu.CompilerParams(vmem_limit_bytes=int(limit * (1 << 20))),
        **kw,
    )


def pack_tile(*refs):
    sources, (up, down, kept, first), held, done = refs[:6], refs[6:10], refs[10:16], refs[16]
    number = held[5].shape[0]
    sources = sources[:5] + (sources[5].at[0:number],)
    copies = [
        pltpu.make_async_copy(source, target, done.at[k])
        for k, (source, target) in enumerate(zip(sources, held))
    ]
    for copy in copies:
        copy.start()
    for copy in copies:
        copy.wait()
    grad, scale, index, weight, rate, members = held
    first[...] = members[:, :, 0:SPREAD_PASSES, :].astype(F32).reshape(first.shape)
    fields, rows, cols = grad.shape
    slots, height, breadth = index.shape
    parts = rate.shape[1] // cols
    reach = SPREAD_PASSES
    up[...] = jnp.zeros(up.shape, F32)
    down[...] = jnp.zeros(down.shape, F32)
    for f in range(fields):
        top = 2 * reach + 1
        up[f * 24 : f * 24 + top, :] = grad[f, 0:top, :]
        up[f * 24 + top : f * 24 + top + STATIC_PASSES, :] = (
            scale[f, 0:STATIC_PASSES, :] * grad[f, 0:STATIC_PASSES, :]
        )
        down[f * 8 : f * 8 + 1, :] = grad[f, rows - 1 : rows, :]
        down[f * 8 + 1 : f * 8 + 1 + STATIC_PASSES, :] = (
            scale[f, rows - STATIC_PASSES : rows, :] * grad[f, rows - STATIC_PASSES : rows, :]
        )
    base = fields * 24
    low = fields * 8
    for s in range(slots):
        up[base + s * 8 : base + s * 8 + 8, 0:breadth] = index[s, 0:8, :].astype(F32)
        up[base + s * 8 : base + s * 8 + 8, breadth:] = weight[s, 0:8, :]
        down[low + s : low + s + 1, 0:breadth] = index[s, height - 1 : height, :].astype(F32)
        down[low + s : low + s + 1, breadth:] = weight[s, height - 1 : height, :]
    base += slots * 8
    low += slots
    for p in range(parts):
        part = slice(p * cols, (p + 1) * cols)
        up[base + p * 8 : base + p * 8 + 8, :] = rate[0:8, part]
        down[low + p * 4 : low + p * 4 + 4, :] = rate[height - 4 : height, part]
        kept[(slots + p) * height : (slots + p + 1) * height, :] = rate[:, part]
    for s in range(slots):
        kept[s * height : (s + 1) * height, 0:breadth] = index[s].astype(F32)
        kept[s * height : (s + 1) * height, breadth:] = weight[s]


def lane_iota(shape):
    return lax.broadcasted_iota(jnp.int32, shape, len(shape) - 1)


def pick_columns(cols):
    source = lax.broadcasted_iota(jnp.int32, (cols, cols), 0)
    target = lax.broadcasted_iota(jnp.int32, (cols, cols), 1)
    half = cols // 2
    wanted = jnp.where(target < half, 2 * target, 2 * (target - half) + 1)
    return jnp.where(source == wanted, 1.0, 0.0).astype(jnp.bfloat16)


def quarter_column(lane, count):
    seg = LANES // count
    return count * (lane % seg) + lane // seg


def spread_columns(cols, count):
    source = lax.broadcasted_iota(jnp.int32, (cols, cols), 0)
    target = lax.broadcasted_iota(jnp.int32, (cols, cols), 1)
    half = cols // 2
    wanted = 2 * quarter_column(source % half, count) + source // half
    return jnp.where(target == wanted, 1.0, 0.0).astype(jnp.bfloat16)


def table_rows(index, weight):
    rows = []
    for o in range(16):
        total = jnp.zeros(index[0].shape, F32)
        for i, w in zip(index, weight):
            total = total + jnp.where(i == float(o), w, 0.0)
        rows.append(total)
    return rows


def slots_of(kept, height, breadth, slots):
    rows = [slice(s * height, (s + 1) * height) for s in range(slots)]
    return [kept[r, 0:breadth] for r in rows], [kept[r, breadth:] for r in rows]


def restrict(grad, scale, kept, up, down, out, rate_out, ext, cols4, edge, *, slots):
    fields, rows, cols = grad.shape
    height, breadth = rows // 2, cols // 2
    parts = kept.shape[0] // height - slots
    index, weight = slots_of(kept, height, breadth, slots)
    n = STATIC_PASSES
    top = 2 * SPREAD_PASSES + 1
    tall = height + SPREAD_PASSES
    base = fields * 24
    low = fields * 8
    table = table_rows(
        [
            jnp.concatenate(
                [index[s], up[base + s * 8 : base + s * 8 + 8, 0:breadth]], axis=0
            )
            for s in range(slots)
        ],
        [
            jnp.concatenate([weight[s], up[base + s * 8 : base + s * 8 + 8, breadth:]], axis=0)
            for s in range(slots)
        ],
    )
    pick = pick_columns(cols)
    ext[...] = jnp.zeros(ext.shape, F32)
    edge[...] = jnp.zeros(edge.shape, F32)
    lane = lane_iota((ext.shape[0], breadth))
    for f in range(fields):
        ext[8 : 8 + rows, :] = grad[f]
        ext[7:8, :] = down[f * 8 : f * 8 + 1, :]
        ext[8 + rows : 8 + rows + top, :] = up[f * 24 : f * 24 + top, :]
        edge[:, 16 + f : 17 + f] = ext[:, 0:1]
        edge[:, 80 + f : 81 + f] = ext[:, cols - 1 : cols]
        both = reorder(ext[...], pick)
        even = both[:, :breadth]
        odd = both[:, breadth:]
        cols4[0] = jnp.where(lane == 0, 0.0, pltpu.roll(odd, 1, 1))
        cols4[1] = even
        cols4[2] = odd
        cols4[3] = jnp.where(lane == breadth - 1, 0.0, pltpu.roll(even, breadth - 1, 1))
        total = jnp.zeros((tall, breadth), F32)
        for a in range(4):
            for b in range(4):
                total = total + table[4 * a + b] * cols4[b, pl.ds(a + 7, tall, stride=2), :]
        out[f * tall : (f + 1) * tall, :] = total
    for at, wide, lone in ((0, 0, 0), (64, cols - n, breadth - 1)):
        for f in range(fields):
            lanes = slice(at + 4 * f, at + 4 * f + n)
            columns = slice(wide, wide + n)
            edge[8 : 8 + rows, lanes] = scale[f, :, columns] * grad[f, :, columns]
            edge[8 - n : 8, lanes] = down[f * 8 + 1 : f * 8 + 1 + n, columns]
            edge[8 + rows : 8 + rows + n, lanes] = up[f * 24 + top : f * 24 + top + n, columns]
        one = slice(lone, lone + 1)
        second = slice(breadth + lone, breadth + lone + 1)
        for s in range(slots):
            lanes = slice(at + 32 + s, at + 33 + s)
            edge[8 : 8 + height, lanes] = index[s][:, one]
            edge[7:8, lanes] = down[low + s : low + s + 1, one]
            edge[8 + height : 9 + height, lanes] = up[base + s * 8 : base + s * 8 + 1, one]
            lanes = slice(at + 36 + s, at + 37 + s)
            edge[8 : 8 + height, lanes] = weight[s][:, one]
            edge[7:8, lanes] = down[low + s : low + s + 1, second]
            edge[8 + height : 9 + height, lanes] = up[base + s * 8 : base + s * 8 + 1, second]
        for a in range(4):
            entry = table[4 * a] if at == 0 else table[4 * a + 3]
            edge[8 : 8 + tall, at + 40 + a : at + 41 + a] = entry[:, one]
    out[fields * tall :, :] = edge[...]
    base = fields * 24 + slots * 8
    low = fields * 8 + slots
    rate_out[0:4, :] = jnp.zeros((4, rate_out.shape[1]), F32)
    for p in range(parts):
        part = slice(p * cols, (p + 1) * cols)
        rate_out[8 : 8 + height, part] = kept[(slots + p) * height : (slots + p + 1) * height, :]
        rate_out[4:8, part] = down[low + p * 4 : low + p * 4 + 4, :]
        rate_out[8 + height : 16 + height, part] = up[base + p * 8 : base + p * 8 + 8, :]


def side(grad, scale, stat_rate, kept, up, down, west_message, east_message,
         static, table_out, box, idx, wgt, tab, *, members_all):
    fields, rows, cols = grad.shape
    slots, (height, breadth) = idx.shape[0], table_out.shape[1:]
    index, weight = slots_of(kept, height, breadth, slots)
    n = STATIC_PASSES
    top = 2 * SPREAD_PASSES + 1
    me = lax.axis_index("mem")
    skip = fields * (height + SPREAD_PASSES)
    from_west = jnp.where(me > 0, pltpu.roll(west_message[skip:, :], 64, 1), 0.0)
    from_east = jnp.where(me < lax.axis_size("mem") - 1, east_message[skip:, :], 0.0)
    wide = cols + LANES
    deep = rows + 2 * n
    shape = (deep, wide)
    row = lax.broadcasted_iota(jnp.int32, shape, 0)
    col = lane_iota(shape)
    tile = lax.axis_index("tile")
    after_row = jnp.where(tile == lax.axis_size("tile") - 1, rows, rows + n)
    before_row = jnp.where(tile == 0, deep, rows + n)
    after_col = jnp.where(me == lax.axis_size("mem") - 1, cols, cols + n)
    before_col = jnp.where(me == 0, wide, wide - n)
    inside_row = jnp.where(row < after_row, 1.0, 0.0) + jnp.where(row >= before_row, 1.0, 0.0)
    inside_col = jnp.where(col < after_col, 1.0, 0.0) + jnp.where(col >= before_col, 1.0, 0.0)
    inside = inside_row * inside_col
    box[...] = jnp.zeros(box.shape, F32)
    for f in range(fields):
        box[0:rows, 0:cols] = scale[f] * grad[f]
        box[rows : rows + n, 0:cols] = up[f * 24 + top : f * 24 + top + n, :]
        box[rows + n : deep, 0:cols] = down[f * 8 + 1 : f * 8 + 1 + n, :]
        for message, at in ((from_east, cols), (from_west, wide - n)):
            lanes = slice(4 * f, 4 * f + n)
            box[0 : rows + n, at : at + n] = message[8 : 8 + rows + n, lanes]
            box[rows + n : deep, at : at + n] = message[8 - n : 8, lanes]
        field = box[...]
        rate = stat_rate[f] * inside
        for _ in range(n):
            beside = (
                pltpu.roll(field, 1, 0)
                + pltpu.roll(field, deep - 1, 0)
                + pltpu.roll(field, 1, 1)
                + pltpu.roll(field, wide - 1, 1)
            )
            field = field + rate * (beside - 4.0 * field)
        static[f] = 0.3 * scale[f] * field[0:rows, 0:cols]
    factor = 2.8 / (members_all - 1)
    base = fields * 24
    low = fields * 8
    tall = height + 16
    lane = lane_iota((tall, breadth))
    for s in range(slots):
        idx[s] = jnp.zeros((tall, breadth), F32)
        wgt[s] = jnp.zeros((tall, breadth), F32)
        idx[s, 8 : 8 + height, :] = index[s]
        wgt[s, 8 : 8 + height, :] = weight[s]
        idx[s, 7:8, :] = down[low + s : low + s + 1, 0:breadth]
        wgt[s, 7:8, :] = down[low + s : low + s + 1, breadth:]
        idx[s, 8 + height : 9 + height, :] = up[base + s * 8 : base + s * 8 + 1, 0:breadth]
        wgt[s, 8 + height : 9 + height, :] = up[base + s * 8 : base + s * 8 + 1, breadth:]
    west = from_west[0:tall, :]
    east = from_east[0:tall, :]

    def shifted(x, shift, at):
        if shift == 1:
            return jnp.where(lane == 0, pltpu.roll(west, LANES - at, 1), pltpu.roll(x, 1, 1))
        if shift == 2:
            return jnp.where(
                lane == breadth - 1,
                pltpu.roll(east, LANES - 1 - at, 1),
                pltpu.roll(x, breadth - 1, 1),
            )
        return x

    for shift, columns in ((0, (1, 2)), (1, (3,)), (2, (0,))):
        table = table_rows(
            [shifted(idx[s], shift, 32 + s) for s in range(slots)],
            [shifted(wgt[s], shift, 36 + s) for s in range(slots)],
        )
        for b in columns:
            for a in range(4):
                off = (1, 0, 0, -1)[a]
                tab[...] = factor * table[4 * a + b]
                table_out[4 * a + b] = tab[8 + off : 8 + off + height, :]
    source = lax.broadcasted_iota(jnp.int32, (breadth, breadth), 0)
    target = lax.broadcasted_iota(jnp.int32, (breadth, breadth), 1)
    order = jnp.where(source == quarter_column(target, lax.axis_size("mem")), 1.0, 0.0)
    flat = reorder(table_out[...].reshape(16 * height, breadth), order.astype(jnp.bfloat16))
    table_out[...] = flat.reshape(16, height, breadth)


def parts_of(width):
    return [slice(t, t + LANES) for t in range(0, width, LANES)]


def sweep(v, keep, rate, lo, hi, v_at, rate_at):
    parts = parts_of(v.shape[2])
    lane = lane_iota((SUB, LANES))

    def right_below(here, below):
        right = jnp.where(lane == LANES - 1, 0.0, pltpu.roll(here[0], LANES - 1, 1))
        return [x + y for x, y in zip(here[1:] + [right], below)]

    above = [v[lo - 1 + v_at, :, p] for p in parts]
    here = [v[lo + v_at, :, p] for p in parts]
    after = right_below(above, here)
    for r in range(lo, hi):
        below = [v[r + 1 + v_at, :, p] for p in parts]
        first = jnp.where(lane == 0, 0.0, pltpu.roll(here[-1], 1, 1)) + above[0]
        before = [first] + after[:-1]
        after = right_below(here, below)
        for t, p in enumerate(parts):
            total = before[t] + after[t]
            v[r + v_at, :, p] = keep[r + rate_at, :, p] * here[t] + rate[r + rate_at, :, p] * total
        above, here = here, below


def climb(rows, keep, rate, lo, rate_at):
    tiles = len(rows[0])
    lane = lane_iota((SUB, LANES))
    parts = parts_of(tiles * LANES)
    result = []
    above = here = after = None
    for k, below in enumerate(rows):
        r = lo + k + rate_at
        if here is None:
            result.append([rate[r, :, p] * x for p, x in zip(parts, below)])
            above, here, after = None, below, list(below)
            continue
        left = jnp.where(lane == 0, 0.0, pltpu.roll(here[-1], 1, 1))
        first = left if above is None else left + above[0]
        before = [first] + after[: tiles - 1] if above is not None else [first] + here[: tiles - 1]
        right = jnp.where(lane == LANES - 1, 0.0, pltpu.roll(here[0], LANES - 1, 1))
        after = [x + y for x, y in zip(here[1:] + [right], below)]
        result.append(
            [
                keep[r, :, p] * here[t] + rate[r, :, p] * (before[t] + after[t])
                for t, p in enumerate(parts)
            ]
        )
        above, here = here, below
    return result


def permutation(width):
    source = lax.broadcasted_iota(jnp.int32, (width, width), 0)
    target = lax.broadcasted_iota(jnp.int32, (width, width), 1)
    tiles = width // LANES
    return jnp.where(source == tiles * (target % LANES) + target // LANES, 1.0, 0.0).astype(
        jnp.bfloat16
    )


def reorder(x, order, contract=0):
    dims = (((1,), (contract,)), ((), ()))
    high = x.astype(jnp.bfloat16)
    rest = x - high.astype(F32)
    middle = rest.astype(jnp.bfloat16)
    low = (rest - middle.astype(F32)).astype(jnp.bfloat16)
    moved = [
        lax.dot_general(y, order, dims, preferred_element_type=F32) for y in (high, middle, low)
    ]
    return moved[0] + (moved[1] + moved[2])


def arrange(members, order, *refs, pairs, groups):
    held, firsts, moved_rows = refs[0], refs[1:-1], refs[-1]
    per = members.shape[0] // pairs
    height, width = members.shape[2:]
    rows = SUB * height
    for b in range(0, pairs, 2):
        n = min(2, pairs - b)
        block = members[b * per : (b + n) * per].reshape(n * rows, width)
        moved = jnp.dot(block, order[...], preferred_element_type=F32)
        for t, p in enumerate(parts_of(width)):
            moved_rows[t, b * rows : (b + n) * rows, :] = moved[:, p]
            for i in range(b, b + n):
                outs = [(out, g) for out, (g, m) in zip(firsts, groups) if g <= i < g + m]
                for r in range(height):
                    line = moved_rows[t, pl.ds(i * rows + r, SUB, stride=height), :]
                    held[i, r, :, p] = line
                    if r < SPREAD_PASSES:
                        for out, g in outs:
                            at = ((i - g) * SPREAD_PASSES + r) * SUB
                            out[at : at + SUB, p] = line


def fill_rates(rate_ref, keep, rate, rows, at):
    for r in range(rows):
        line = jnp.broadcast_to(rate_ref[r + at : r + at + 1, :], rate.shape[1:])
        rate[r] = line
        keep[r] = 1.0 - 4.0 * line


def spread_rates(rate_ref, order, keep, rate, moved):
    moved[...] = reorder(rate_ref[...], order[...])
    fill_rates(moved, keep, rate, rate.shape[0], 4)


def fold(total, fields):
    folded = total[0:fields]
    for j in range(fields, SUB, fields):
        folded = folded + total[j : j + fields]
    return folded


def own(*refs, count, fields, pairs, last):
    members, keep, rate, order = refs[0:4]
    pieces = refs[4 : 4 + count]
    own_out, beyond, far_coarse, message = refs[4 + count : 8 + count]
    v, c, cw, cp, acc, eb = refs[8 + count :]
    height = c.shape[0]
    reach = SPREAD_PASSES
    tall = height + reach
    parts = parts_of(v.shape[2])

    me = lax.axis_index("mem")
    for d, piece in enumerate(pieces):
        breadth = piece.shape[1]
        where = lax.rem(me - d + count, count)
        at = pl.ds(pl.multiple_of(where * breadth, LANES), breadth)
        cw[:, at] = piece[0 : fields * tall, :]
        eb[where] = piece[fields * tall :, :]
    lane = lane_iota((tall, LANES))
    for q in range(count - 1):
        last_column = (q + 1) * breadth - 1
        for mine, other, table_at, grad_at, goal in (
            (q, q + 1, 104, 16, last_column),
            (q + 1, q, 40, 80, last_column + 1),
        ):
            added = jnp.zeros((tall, LANES), F32)
            for a in range(4):
                entry = eb[mine, 8 : 8 + tall, table_at + a : table_at + a + 1]
                added = added + entry * eb[other, pl.ds(a + 7, tall, stride=2), :]
            begin = goal // LANES * LANES
            for f in range(fields):
                turn = (goal - begin - grad_at - f) % LANES
                here = jnp.where(lane == goal - begin, pltpu.roll(added, turn, 1), 0.0)
                rows = slice(f * tall, (f + 1) * tall)
                cw[rows, begin : begin + LANES] = cw[rows, begin : begin + LANES] + here
    moved = reorder(cw[...], order[...])
    for t, p in enumerate(parts):
        cp[t] = moved[:, p]
        for r in range(tall):
            row = cp[t, pl.ds(r, fields, stride=tall), :]
            for j in range(0, SUB, fields):
                if r < height:
                    c[r, j : j + fields, p] = row
                else:
                    far_coarse[r - height, j : j + fields, p] = row
    acc[...] = jnp.zeros(acc.shape, F32)
    off = 5

    def one(i, _):
        v[0:off] = jnp.zeros((off,) + v.shape[1:], F32)
        v[height + off :] = jnp.zeros((v.shape[0] - height - off,) + v.shape[1:], F32)
        for r in range(height):
            v[r + off] = members[i, r] * c[r]
        for s in range(1, SPREAD_PASSES + 1):
            sweep(v, keep, rate, -min(s, SPREAD_PASSES - s), height + s, off, 4)
        for r in range(height):
            acc[r] = acc[r] + members[i, r] * v[r + off]
        for r in range(reach):
            beyond[i, r] = v[r + height + off]
        return _

    lax.fori_loop(0, pairs, one, 0)
    for r in range(height):
        own_out[r * fields : (r + 1) * fields, :] = fold(acc[r], fields)
    two = 2 * fields
    message[0:two, :] = own_out[0:two, :]
    for j in range(last):
        for r in range(reach):
            at = two + (j * reach + r) * SUB
            message[at : at + SUB, :] = members[pairs - last + j, r]


def cross(far_rows, members, beyond, far_coarse, keep, rate, order, near_out, far_out,
          near, far, fw, *, fields, begin, number, skip, arranged):
    reach = SPREAD_PASSES
    height = members.shape[1]
    parts = parts_of(order.shape[1])
    near[...] = jnp.zeros(near.shape, F32)
    far[...] = jnp.zeros(far.shape, F32)
    size = SUB * reach
    if not arranged:
        moved = jnp.dot(
            far_rows[...].astype(jnp.bfloat16), order[...], preferred_element_type=F32
        )
        for t, p in enumerate(parts):
            fw[t] = moved[:, p]

    def one(i, x):
        window = [[None] * len(parts) for _ in range(reach)]
        for t, p in enumerate(parts):
            for r in range(reach):
                if arranged:
                    at = pl.multiple_of(skip + i * size + r * SUB, SUB)
                    line = far_rows[pl.ds(at, SUB), p]
                else:
                    line = fw[t, pl.ds(i * size + r, SUB, stride=reach), :]
                window[r][t] = line * far_coarse[r, :, p]
                far[r, :, p] = far[r, :, p] + line * beyond[begin + i, r, :, p]
        for s in range(1, SPREAD_PASSES + 1):
            window = climb(window, keep, rate, height - s, 4)
        for r in range(reach):
            for t, p in enumerate(parts):
                line = members[begin + i, height - reach + r, :, p]
                near[r, :, p] = near[r, :, p] + line * window[r][t]
        return x

    if arranged:
        lax.fori_loop(0, number, one, 0)
    else:
        for i in range(number):
            one(i, 0)
    for r in range(reach):
        near_out[r * fields : (r + 1) * fields, :] = fold(near[r], fields)
        far_out[r * fields : (r + 1) * fields, :] = fold(far[r], fields)


def pack_sums(*refs, groups, count, fields):
    own_ref, edge = refs[:2]
    nears = refs[2 : 2 + groups]
    fars = refs[2 + groups : 2 + 2 * groups]
    outs, held = refs[2 + 2 * groups : -1], refs[-1]
    rows = own_ref.shape[0]
    tiles, tall = held.shape[:2]
    two = 2 * fields
    reach = SPREAD_PASSES * fields
    near = nears[0][...]
    far = fars[0][...]
    for x, y in zip(nears[1:], fars[1:]):
        near = near + x[...]
        far = far + y[...]
    near = near + own_ref[rows - reach : rows, :]
    for t, p in enumerate(parts_of(own_ref.shape[1])):
        held[t, 0 : rows - reach, :] = own_ref[0 : rows - reach, p]
        held[t, rows - reach : rows, :] = near[:, p]
        held[t, rows : rows + reach, :] = far[:, p]
        held[t, rows + reach : tall, :] = edge[0:two, p]
    me = lax.axis_index("mem")
    seg = LANES // count
    lane = lane_iota((SUB, LANES))
    lanes = lane_iota((tall, LANES))
    for d in range(count):
        q = me ^ d
        quarter = jnp.zeros((tall, LANES), F32)
        for t in range(tiles):
            turned = pltpu.roll(held[t], lax.rem(t - q + count, count) * seg, 1)
            quarter = jnp.where(lanes // seg == t, turned, quarter)
        out, at = (outs[d // 2], 0) if d % 2 == 0 else (outs[-1], d // 2 * (tall + SUB))
        out[at : at + tall, :] = quarter
        packed = jnp.zeros((SUB, LANES), F32)
        for k in range(tall // SUB):
            rows8 = slice(k * SUB, (k + 1) * SUB)
            turn = 2 * k + 1 + LANES - q * seg
            left = pltpu.roll(held[tiles - 1, rows8, :], lax.rem(turn, LANES), 1)
            right = pltpu.roll(held[0, rows8, :], lax.rem(turn + LANES - seg, LANES), 1)
            packed = jnp.where(lane == 2 * k, left, packed)
            packed = jnp.where(lane == 2 * k + 1, right, packed)
        west = jnp.where(q > 0, 1.0, 0.0).astype(F32)
        east = jnp.where(q < count - 1, 1.0, 0.0).astype(F32)
        out[at + tall : at + tall + SUB, :] = packed * jnp.where(lane % 2 == 0, west, east)


def add_quarters(*refs):
    *pieces, out, below = refs
    total = pieces[0][...]
    for piece in pieces[1:]:
        total = total + piece[0 : out.shape[0], :]
    out[...] = total
    below[...] = total[out.shape[0] - below.shape[0] :, :]


def ref_end(ref):
    return ref[ref.shape[0] - SUB :, :]


def finish(total_ref, above, static, table, out, held, wide, *, count, fields):
    height = table.shape[1]
    rows, cols = out.shape[1:]
    breadth = table.shape[2]
    lane = lane_iota((SUB, LANES))
    seg = LANES // count
    mine = height * fields // SUB
    reach = SPREAD_PASSES * fields // SUB

    def block(ref, number):
        return ref[number * SUB : (number + 1) * SUB, :]

    borders = ref_end(total_ref), ref_end(above)
    terms = [[(1, 0, mine - 1)]]
    for k in range(mine):
        terms.append([(0, k, k)] + ([(1, k + 1, mine + k)] if k < reach else []))
    terms.append([(0, mine, mine), (0, mine + reach, mine + reach)])
    for number, parts in enumerate(terms):
        x = left = right = 0.0
        for source, at, k in parts:
            x = x + block((total_ref, above)[source], at)
            packed = borders[source]
            left = left + (pltpu.roll(packed, LANES - 2 * k, 1) if k else packed)
            right = right + pltpu.roll(packed, LANES - 2 - 2 * k, 1)
        rows8 = slice(number * SUB, (number + 1) * SUB)
        held[0, rows8, :] = x
        before = jnp.where(lane == 0, left, pltpu.roll(x, seg + 1, 1))
        held[1, rows8, :] = jnp.where(lane < seg, before, pltpu.roll(x, seg, 1))
        after = jnp.where(lane == LANES - 1, right, pltpu.roll(x, LANES - seg - 1, 1))
        held[2, rows8, :] = jnp.where(lane >= LANES - seg, after, pltpu.roll(x, LANES - seg, 1))
    for f in range(fields):
        for p in range(2):
            even = jnp.zeros((height, breadth), F32)
            odd = jnp.zeros((height, breadth), F32)
            for a, off in ((1 + p, 0), (3 - 3 * p, 2 * p - 1)):
                at = pl.ds(f + fields * (2 + off), height, stride=fields)
                here = held[0, at, :]
                even = even + table[4 * a + 1] * here + table[4 * a + 3] * held[1, at, :]
                odd = odd + table[4 * a + 2] * here + table[4 * a] * held[2, at, :]
            at = pl.ds(f * rows + p, height, stride=2)
            wide[0, at, :] = even
            wide[1, at, :] = odd
    both = jnp.concatenate([wide[0], wide[1]], axis=1)
    fine = reorder(both, spread_columns(cols, count))
    for f in range(fields):
        out[f] = static[f] + fine[f * rows : (f + 1) * rows, :]


def groups_of(pairs):
    first = max(1, pairs // 5)
    sizes = (first, pairs - first - 1, 1)
    return [(sum(sizes[:g]), size) for g, size in enumerate(sizes)]


def local(gradient, static_scale, static_rate, interp_index, interp_weight, members, spread_rate):
    fields, rows, cols = gradient.shape
    slots, height, breadth = interp_index.shape
    member_count, _, _, width = members.shape
    reach = SPREAD_PASSES
    tiles = lax.axis_size("tile")
    count = lax.axis_size("mem")
    upward = [(i + 1, i) for i in range(tiles - 1)]
    downward = [(i, i + 1) for i in range(tiles - 1)]
    rings = [[(i, (i + d) % count) for i in range(count)] for d in range(count)]
    per = SUB // fields
    pairs = member_count // per
    vmem = pl.BlockSpec(memory_space=pltpu.VMEM)
    smem = pl.BlockSpec(memory_space=pltpu.SMEM)
    smalls = (gradient, static_scale, interp_index, interp_weight, spread_rate)
    column_parts = width // cols
    order = permutation(width)

    groups = groups_of(pairs)
    last = groups[-1][1]
    line = (SUB, width)
    lane_tiles = width // LANES
    size = SUB * reach
    number = groups[0][1]

    up, down, kept, first = call(
        pack_tile,
        [
            (fields * 24 + slots * 8 + column_parts * 8, cols),
            (fields * 8 + (slots + column_parts * 4 + 7) // 8 * 8, cols),
            ((slots + column_parts) * height, cols),
            (number * size, width),
        ],
        [pltpu.VMEM(x.shape, x.dtype) for x in smalls]
        + [
            pltpu.VMEM((per * number,) + members.shape[1:], members.dtype),
            pltpu.SemaphoreType.DMA((6,)),
        ],
        in_specs=[pl.BlockSpec(memory_space=pltpu.HBM)] * 6,
        limit=(VMEM_BYTES - members.size * members.dtype.itemsize * 17 // 16) / (1 << 20),
        name="pack_tile",
    )(*smalls, members)
    first = lax.ppermute(first, "tile", upward)
    down = lax.ppermute(down, "tile", downward)
    up = lax.ppermute(up, "tile", upward)
    members, *firsts = call(
        functools.partial(arrange, pairs=pairs, groups=groups[1:-1]),
        [(pairs, height) + line] + [(n * size, width) for _, n in groups[1:-1]],
        [(lane_tiles, pairs * SUB * height, LANES)],
        limit=8,
        name="arrange",
    )(members, order)
    far_rows = [first] + [lax.ppermute(rows_k, "tile", upward) for rows_k in firsts]

    tall = height + reach
    quarter, rates = call(
        functools.partial(restrict, slots=slots),
        [(fields * tall + 64, breadth), (height + 16, width)],
        [(64, cols), (4, 64, breadth), (64, LANES)],
        name="restrict",
    )(gradient, static_scale, kept, up, down)
    pieces = [quarter] + [lax.ppermute(quarter, "mem", rings[d]) for d in range(1, count)]

    static, table = call(
        functools.partial(side, members_all=member_count * count),
        [(fields, rows, cols), (16, height, breadth)],
        [
            (rows + 2 * STATIC_PASSES, cols + LANES),
            (slots, height + 16, breadth),
            (slots, height + 16, breadth),
            (height + 16, breadth),
        ],
        in_specs=[vmem, vmem, smem] + [vmem] * 5,
        name="side",
    )(gradient, static_scale, static_rate, kept, up, down, pieces[1], pieces[-1])

    two = 2 * fields
    keep, rate = call(
        spread_rates,
        [(height + 12,) + line] * 2,
        [rates.shape],
        name="spread_rates",
    )(rates, order)
    own_sum, beyond, far_coarse, message = call(
        functools.partial(own, count=count, fields=fields, pairs=pairs, last=last),
        [
            (height * fields, width),
            (pairs, reach) + line,
            (reach,) + line,
            (two + last * size, width),
        ],
        [
            (height + reach + 6,) + line,
            (height,) + line,
            (fields * tall, width),
            (lane_tiles, fields * tall, LANES),
            (height,) + line,
            (count, 64, LANES),
        ],
        limit=8,
        name="own",
    )(members, keep, rate, order, *pieces)
    message = lax.ppermute(message, "tile", upward)
    far_rows.append(message)

    nears, fars = [], []
    for k, (g, n) in enumerate(groups):
        near, far = call(
            functools.partial(
                cross,
                fields=fields,
                begin=g,
                number=n,
                skip=two if k == len(groups) - 1 else 0,
                arranged=k > 0,
            ),
            [(reach * fields, width)] * 2,
            [
                (reach,) + line,
                (reach,) + line,
                (lane_tiles, size if k else n * size, LANES),
            ],
            limit=4,
            name="cross",
        )(far_rows[k], members, beyond, far_coarse, keep, rate, order)
        nears.append(near)
        fars.append(far)

    high = (height + reach) * fields + two + SUB
    *kept_sums, leaving = call(
        functools.partial(pack_sums, groups=len(groups), count=count, fields=fields),
        [(high, breadth)] * (count // 2) + [(count // 2 * high, breadth)],
        [(lane_tiles, high - SUB, LANES)],
        name="pack_sums",
    )(own_sum, message, *nears, *fars)
    assert count == 4
    came = lax.ppermute(leaving, "mem", [(i, i ^ 1) for i in range(count)])
    going = kept_sums[1] + came[high:]
    last_came = lax.ppermute(going, "mem", [(i, i ^ 2) for i in range(count)])
    total, below = call(
        add_quarters,
        [(high, breadth), (high - (height * fields - SUB), breadth)],
        name="add_quarters",
    )(kept_sums[0], came, last_came)
    from_above = lax.ppermute(below, "tile", downward)
    (hybrid,) = call(
        functools.partial(finish, count=count, fields=fields),
        [(fields, rows, cols)],
        [(3, (height + 4) * fields, LANES), (2, fields * rows, breadth)],
        name="finish",
    )(total, from_above, static, table)
    return hybrid


def solution(mesh):
    return jax.shard_map(
        local,
        mesh=mesh,
        in_specs=(
            P(None, "tile", "mem"),
            P(None, "tile", "mem"),
            P(),
            P(None, "tile", "mem"),
            P(None, "tile", "mem"),
            P("mem", None, "tile", None),
            P("tile", None),
        ),
        out_specs=P(None, "tile", "mem"),
        check_vma=False,
    )
```
